32 devices in a mesh: group: 2 (over x), region: 8 (over z, y), window: 2 (over core).
Axes of the slice: x: 2, y: 2, z: 4, core: 2. Of those that a mesh axis runs over, the one named last changes fastest.
Arguments:
- flux: bfloat16 [32, 4096, 128], P(('group', 'window'), 'region'), parts along dimension 0, may hold values from -6 to 6
- blend: float32 [16, 16], replicated
- footprints: bfloat16 [4, 8192, 4096], P(('group', 'window'), 'region'), parts along dimension 0, may hold values from -0.03125 to 0.03125
- receptor_block: int32 [4, 8192], P(('group', 'window'), 'region'), parts along dimension 0, may hold values from 0 to 15, as said below
- cell_block: int32 [4, 8192], P(('group', 'window'), 'region'), parts along dimension 0, may hold values from 0 to 7
- slice_index: int32 [4, 8192], P(('group', 'window'), 'region'), parts along dimension 0, may hold values from 0 to 15
- live_counts: int32 [4, 8], P(('group', 'window'), 'region'), parts along dimension 0, may hold values from 16 to 1024, as said below
- observed: bfloat16 [4, 1024, 128], P(('group', 'window'), 'region'), parts along dimension 0, may hold values from -3 to 3
- inv_var: float32 [4, 1024], P(('group', 'window'), 'region'), parts along dimension 0, may hold values from 0.5 to 2
- prior_mix: bfloat16 [128, 128], replicated, may hold values from -2 to 2
Outputs:
- misfit: bfloat16 [4, 1024, 128], P(('group', 'window'), 'region'), parts along dimension 0
- gradient: bfloat16 [32, 4096, 128], P(('group', 'window'), 'region'), parts along dimension 0
The draws below stay inside these ranges and needn't reach their ends.
There are 2 independent parts, one for each index of `group`. The reference program is written for one: setup_inputs(seed, part) draws one part's arguments, and reference() takes and returns one part's arrays. A program takes and returns all parts, laid end to end along the dimension named above; an argument that names none is the same for every part. Nothing has to cross between parts.
Inputs may be any that keep to these rules, and one draw needn't show every extreme that they name: `receptor_block`: receptor blocks j * 2 to (j + 1) * 2 - 1 of a window belong to region j. Of the 1024 slots of one window and region, the first live_counts entries are footprint blocks and the rest are unused. The live blocks of one window and region name at most 2 distinct receptor blocks of any one region, and in every draw, for each window, some region has 2 of its receptor blocks named by the live blocks of every region. `live_counts`: some window and region has all 1024 slots live.
All inputs are finite; a program needn't handle non-finite values.
Results may differ from the reference program's by a relative error of at most 0.018.
Values may be sent and summed in bfloat16 or wider, within the bound.
A program may use at most 192 MiB of HBM per device.

```python
import math
import jax
import jax.numpy as jnp
from jax import lax

ENS = 128
BLOCK = 64
CAP = 2
RB_DEV = 2
CB_DEV = 8
NB = 1024
SLICES = 16
NWIN = 2
REGIONS = 8
RB_WIN = 16
REC_WIN = 1024
CELLS = 4096
NBLK = 8192


def draw_blend(key, part):
    slot_ids = jnp.arange(SLICES)
    distance = jnp.abs(slot_ids[:, None] - slot_ids[None, :]).astype(jnp.float32)
    diagonal_part = jax.random.uniform(jax.random.fold_in(key, 5101), (SLICES, SLICES), jnp.float32, 0.6, 1.0)
    side_part = jax.random.uniform(jax.random.fold_in(key, 5102), (SLICES, SLICES), jnp.float32, -1.0, 1.0)
    decay_span = max(SLICES // 4, 1)
    return jnp.where(distance == 0.0, diagonal_part, 0.4 * side_part * jnp.exp(-distance / decay_span))


def block_plan(key):
    sub_keys = [jax.random.fold_in(key, 9100 + number) for number in range(8)]
    live_least = REGIONS * CAP
    draw_one = jax.random.randint(sub_keys[0], (NWIN, REGIONS), 0, 16)
    draw_two = jax.random.randint(sub_keys[1], (NWIN, REGIONS), 0, 16)
    counts = live_least + (NB - live_least) * draw_one * draw_two // 225
    busiest = jax.random.randint(sub_keys[2], (), 0, NWIN * REGIONS)
    counts = jnp.where(jnp.arange(NWIN * REGIONS).reshape(NWIN, REGIONS) == busiest, NB, counts)
    picked = jax.random.randint(sub_keys[3], (NWIN, REGIONS, REGIONS), 1, CAP + 1)
    fullest = jax.random.randint(sub_keys[4], (NWIN, 1, 1), 0, REGIONS)
    picked = jnp.where(jnp.arange(REGIONS)[None, None, :] == fullest, CAP, picked)
    scores = jax.random.randint(sub_keys[5], (NWIN, REGIONS, REGIONS, RB_DEV), 0, 1 << 20) * RB_DEV + jnp.arange(RB_DEV)
    ranking = jnp.argsort(scores, axis=-1)[..., :CAP]
    owners = jnp.arange(REGIONS)[None, None, :, None] * RB_DEV + ranking
    usable = jnp.arange(CAP)[None, None, None, :] < picked[..., None]
    owners = owners.reshape(NWIN, REGIONS, REGIONS * CAP)
    usable = usable.reshape(NWIN, REGIONS, REGIONS * CAP).astype(jnp.int32)
    position = jnp.cumsum(usable, axis=-1) - usable
    spot_ids = jnp.arange(REGIONS * CAP)
    matches = (position[..., None, :] == spot_ids[:, None]) & (usable[..., None, :] > 0)
    listed = jnp.sum(jnp.where(matches, owners[..., None, :], 0), axis=-1)
    touched = jnp.sum(usable, axis=-1)
    item_ids = jnp.arange(NB)
    spare_pick = jax.random.randint(sub_keys[6], (NWIN, REGIONS, NB), 0, touched[..., None])
    chosen = jnp.where(item_ids < touched[..., None], item_ids, spare_pick)
    targets = jnp.take_along_axis(listed, chosen, axis=-1)
    shuffle = jnp.where(item_ids < counts[..., None], jax.random.randint(sub_keys[7], (NWIN, REGIONS, NB), 0, 1 << 20) * NB + item_ids, (1 << 30) + item_ids)
    slot_order = jnp.argsort(shuffle, axis=-1)
    receptor_ids = jnp.take_along_axis(targets, slot_order, axis=-1)
    return (counts.astype(jnp.int32), receptor_ids.reshape(NWIN, REGIONS * NB).astype(jnp.int32))


def draw_receptor_block(key, part):
    counts, receptor_ids = block_plan(key)
    return receptor_ids


def draw_live_counts(key, part):
    counts, receptor_ids = block_plan(key)
    return counts


def touch_ends(array, stream_key, smallest, high):
    place = [jax.random.randint(jax.random.fold_in(stream_key, axis), (), 0, length) for axis, length in enumerate(array.shape)]
    main_axis = array.shape.index(max(array.shape))
    neighbour = place[:main_axis] + [(place[main_axis] + 1) % array.shape[main_axis]] + place[main_axis + 1:]
    return array.at[tuple(place)].set(smallest).at[tuple(neighbour)].set(high)


def block_levels(stream_key, dims, shards, smallest, top_value):
    def one(axis_at, shards_of):
        heights = jax.random.uniform(jax.random.fold_in(jax.random.fold_in(stream_key, 6), axis_at), (shards_of,), jnp.float32, smallest / len(shards), top_value / len(shards))
        return jnp.repeat(jnp.exp(heights), dims[axis_at] // shards_of).reshape((-1,) + (1,) * (len(dims) - axis_at - 1))

    level = one(*shards[0])
    for cut in shards[1:]:
        level = level * one(*cut)
    return level


def scatter_about(own_key, shape, deviation, most, shards=(), held_as=jnp.bfloat16):
    array = deviation * jax.random.normal(own_key, shape, jnp.float32)
    if shards:
        array = array * block_levels(own_key, shape, shards, -0.22, 0.18)
    return jnp.clip(array, -most, most).astype(held_as)


def setup_inputs(seed: int = 0, part: int = 0) -> dict:
    splits = jax.random.split(jax.random.key(seed), 11)
    part_keys = jax.random.split(jax.random.fold_in(splits[10], part), 11)
    return {
        "flux": scatter_about(part_keys[0], (SLICES, CELLS, ENS), 1.0, 6.0, ((0, 2), (1, 8))),
        "blend": draw_blend(jax.random.fold_in(splits[10], 71), part),
        "footprints": scatter_about(part_keys[2], (NWIN, NBLK, BLOCK * BLOCK), (BLOCK * NB // RB_DEV) ** -0.5, 0.03125, ((0, 2), (1, 8))),
        "receptor_block": draw_receptor_block(jax.random.fold_in(jax.random.fold_in(splits[10], part), 71), part),
        "cell_block": touch_ends(jax.random.randint(part_keys[4], (NWIN, NBLK), 0, CB_DEV), jax.random.fold_in(part_keys[4], 1), 0, CB_DEV - 1).astype(jnp.int32),
        "slice_index": touch_ends(jax.random.randint(part_keys[5], (NWIN, NBLK), 0, SLICES), jax.random.fold_in(part_keys[5], 1), 0, SLICES - 1).astype(jnp.int32),
        "live_counts": draw_live_counts(jax.random.fold_in(jax.random.fold_in(splits[10], part), 71), part),
        "observed": scatter_about(part_keys[7], (NWIN, REC_WIN, ENS), 0.5, 3.0, ((0, 2), (1, 8))),
        "inv_var": jnp.clip(jnp.exp(math.log(2.0) - 1.3862944 * jax.random.uniform(part_keys[8], (NWIN, REC_WIN), jnp.float32) ** block_levels(part_keys[8], (NWIN, REC_WIN), ((0, 2), (1, 8)), -0.2, 0.2)), 0.5, 2.0),
        "prior_mix": scatter_about(splits[9], (ENS, ENS), (ENS // 16) ** -0.5, 2.0),
    }


def reference(flux, blend, footprints, receptor_block, cell_block, slice_index, live_counts, observed, inv_var, prior_mix):
    highest = lax.Precision.HIGHEST
    blended = jnp.einsum("ts,sce->tce", blend, flux.astype(jnp.float32), precision=highest).astype(jnp.bfloat16)
    global_blocks = CELLS // BLOCK
    panels = blended.reshape(SLICES * global_blocks, BLOCK, ENS)
    device_count = NWIN * REGIONS
    footprint_sets = footprints.reshape(device_count, NB, BLOCK, BLOCK)
    receptor_sets = receptor_block.reshape(device_count, NB)
    cell_sets = cell_block.reshape(device_count, NB)
    slice_sets = slice_index.reshape(device_count, NB)
    live_sets = jnp.arange(NB, dtype=jnp.int32)[None, :] < live_counts.reshape(device_count)[:, None]
    region_ids = (jnp.arange(device_count, dtype=jnp.int32) % REGIONS).astype(jnp.int32)
    window_ids = (jnp.arange(device_count, dtype=jnp.int32) // REGIONS).astype(jnp.int32)
    panel_sets = (slice_sets * global_blocks + region_ids[:, None] * CB_DEV + cell_sets).astype(jnp.int32)
    receptor_rows = (window_ids[:, None] * RB_WIN + receptor_sets).astype(jnp.int32)
    items = (footprint_sets, receptor_rows, panel_sets, live_sets)

    def forward(totals, item):
        footprint_set, receptor_row, panel_set, live_set = item
        gathered = panels[panel_set]
        products = jnp.einsum("kab,kbe->kae", footprint_set.astype(jnp.float32), gathered.astype(jnp.float32))
        products = jnp.where(live_set[:, None, None], products, jnp.zeros_like(products))
        return totals.at[receptor_row].add(products), None

    evolved, unused = lax.scan(forward, jnp.zeros((NWIN * RB_WIN, BLOCK, ENS), jnp.float32), items)
    weights_here = inv_var.reshape(NWIN * RB_WIN, BLOCK)[:, :, None]
    observed_here = observed.reshape(NWIN * RB_WIN, BLOCK, ENS).astype(jnp.float32)
    misfit = (weights_here * (evolved - observed_here)).astype(jnp.bfloat16)

    def adjoint(totals, item):
        footprint_set, receptor_row, panel_set, live_set = item
        rows_here = misfit[receptor_row]
        pulled_back = jnp.einsum("kab,kae->kbe", footprint_set.astype(jnp.float32), rows_here.astype(jnp.float32))
        pulled_back = jnp.where(live_set[:, None, None], pulled_back, jnp.zeros_like(pulled_back))
        return totals.at[panel_set].add(pulled_back), None

    collected, unused_two = lax.scan(adjoint, jnp.zeros((SLICES * global_blocks, BLOCK, ENS), jnp.float32), items)
    collected = collected.reshape(SLICES, CELLS, ENS)
    pulled = jnp.einsum("ts,tce->sce", blend, collected, precision=highest).astype(jnp.bfloat16)
    gradient = jnp.dot(pulled.reshape(SLICES * CELLS, ENS), prior_mix, preferred_element_type=jnp.float32)
    gradient = gradient.astype(jnp.bfloat16).reshape(SLICES, CELLS, ENS)
    return misfit.reshape(NWIN, REC_WIN, ENS), gradient
```

```python
import functools

import jax
import jax.numpy as jnp
from jax import lax
from jax.experimental import pallas as pl
from jax.experimental.pallas import tpu as pltpu
from jax.sharding import PartitionSpec as P

BLOCK = 64
MESH = pl.DeviceIdType.MESH
F32 = jnp.float32
BF16 = jnp.bfloat16
SUB = 16
SUBS = 4
CELLS_AT_ONCE = 16
PIECES = 4
LOADS = 8
PAIRS = 32
TURNS = 32
LAG = 2
HALF = BLOCK // 2
CLEAR = 32
MOST = 16
AT_ONCE = 32
DENSE_LAG = 1
DENSE_BLOCKS = 16


def spread(matrix, width):
    size = matrix.shape[0]
    full = size * width
    row = lax.broadcasted_iota(jnp.int32, (full, size), 0)
    col = lax.broadcasted_iota(jnp.int32, (full, size), 1)
    pick = (row // width == col).astype(BF16)
    row_f = lax.broadcasted_iota(jnp.int32, (full, full), 0)
    col_f = lax.broadcasted_iota(jnp.int32, (full, full), 1)
    same = row_f % width == col_f % width
    high = matrix.astype(BF16)
    low = (matrix - high.astype(F32)).astype(BF16)
    parts = []
    for part in (high, low):
        tall = jnp.dot(pick, part, preferred_element_type=F32).astype(BF16)
        wide = lax.dot_general(tall, pick, (((1,), (1,)), ((), ())), preferred_element_type=F32)
        parts.append(jnp.where(same, wide, 0.0).astype(BF16))
    return parts


def halves_swapped(x):
    return pltpu.roll(x, BLOCK, 1)


def blend_kernel(
    window_blocks,
    recv_hbm,
    cell_hbm,
    slice_hbm,
    live_ref,
    blend_hbm,
    flux_hbm,
    fp_hbm,
    panels_ref,
    pairs_ref,
    index_ref,
    full,
    raw,
    blend_ref,
    recv_ref,
    cell_ref,
    slice_ref,
    small_sem,
    fp_sem,
    local_sem,
    send_sem,
    recv_sem,
):
    me = lax.axis_index("window")
    other = 1 - me
    slabs, cells, ens = flux_hbm.shape
    slices = panels_ref.shape[0]
    slots = raw.shape[0]
    barrier = pltpu.get_barrier_semaphore()
    pl.semaphore_signal(barrier, inc=1, device_id={"window": other}, device_id_type=MESH)
    smalls = [
        pltpu.make_async_copy(source, target, small_sem.at[k])
        for k, (source, target) in enumerate(
            ((blend_hbm, blend_ref), (recv_hbm, recv_ref), (cell_hbm, cell_ref), (slice_hbm, slice_ref))
        )
    ]
    for copy in smalls:
        copy.start()
    piece = cells // PIECES
    locals_, sends, loads = [], [], []
    for k in range(PIECES):
        span = pl.ds(k * piece, piece)
        locals_.append(
            pltpu.make_async_copy(
                flux_hbm.at[:, span, :], full.at[pl.ds(me * slabs, slabs), span, :], local_sem.at[k]
            )
        )
        locals_[-1].start()
    part = slots // LOADS
    for k in range(LOADS):
        span = pl.ds(k * part, part)
        loads.append(pltpu.make_async_copy(fp_hbm.at[0, span, :], raw.at[span, :], fp_sem.at[k]))
    loads[0].start()
    pl.semaphore_wait(barrier, 1)
    for k in range(PIECES):
        span = pl.ds(k * piece, piece)
        sends.append(
            pltpu.make_async_remote_copy(
                src_ref=flux_hbm.at[:, span, :],
                dst_ref=full.at[pl.ds(me * slabs, slabs), span, :],
                send_sem=send_sem.at[k],
                recv_sem=recv_sem.at[k],
                device_id={"window": other},
                device_id_type=MESH,
            )
        )
        sends[-1].start()
    for k in range(1, LOADS):
        loads[k].start()

    for copy in smalls:
        copy.wait()
    cell_blocks = cells // BLOCK
    live = lax.broadcasted_iota(jnp.int32, recv_ref.shape, 1) < live_ref[...]
    panel = slice_ref[...] * cell_blocks + cell_ref[...]
    index_ref[pl.ds(0, 1), :] = jnp.where(live, recv_ref[...], window_blocks)
    index_ref[pl.ds(1, 1), :] = jnp.where(live, panel, 0)
    index_ref[pl.ds(2, 1), :] = jnp.where(live, panel, slices * cell_blocks)
    index_ref[pl.ds(3, 1), :] = jnp.where(live, recv_ref[...], 0)
    high, low = spread(blend_ref[...], CELLS_AT_ONCE)

    def arrange(k):
        loads[k].wait()

        def body(g, carry):
            lower = lax.broadcasted_iota(jnp.int32, (BLOCK // 2, 2 * BLOCK), 1) < BLOCK
            for sub in range(SUBS):
                base = pl.multiple_of(k * part + g * SUBS * SUB + sub * SUB, SUB)
                x = raw[pl.ds(base, SUB), :].reshape(SUB, BLOCK // 2, 2 * BLOCK)
                for j in range(0, SUB, 2):
                    one, two = x[j], x[j + 1]
                    even = jnp.where(lower, one, halves_swapped(two))
                    odd = jnp.where(lower, halves_swapped(one), two)
                    place = k * (part // 2) + (g * SUBS + sub) * (SUB // 2) + j // 2
                    pairs_ref[place] = jnp.concatenate([even, odd], axis=0)
            return carry

        lax.fori_loop(0, part // SUB // SUBS, body, 0)

    for k in range(LOADS // 2):
        arrange(k)
    for k in range(PIECES):
        locals_[k].wait()
        sends[k].wait_recv()

        def group(g, carry, k=k):
            sides = []
            for half in range(2):
                start = pl.multiple_of(k * piece + g * 2 * CELLS_AT_ONCE + half * CELLS_AT_ONCE, CELLS_AT_ONCE)
                sides.append(full[:, pl.ds(start, CELLS_AT_ONCE), :].reshape(slices * CELLS_AT_ONCE, ens))
            rhs = jnp.concatenate(sides, axis=1)
            out = jnp.dot(high, rhs, preferred_element_type=F32) + jnp.dot(low, rhs, preferred_element_type=F32)
            out = out.astype(BF16)
            for half in range(2):
                start = pl.multiple_of(k * piece + g * 2 * CELLS_AT_ONCE + half * CELLS_AT_ONCE, CELLS_AT_ONCE)
                panels_ref[:, pl.ds(start, CELLS_AT_ONCE), :] = out[:, half * ens : (half + 1) * ens].reshape(
                    slices, CELLS_AT_ONCE, ens
                )
            return carry

        lax.fori_loop(0, piece // (2 * CELLS_AT_ONCE), group, 0, unroll=2)
    for k in range(LOADS // 2, LOADS):
        arrange(k)
    for k in range(PIECES):
        sends[k].wait_send()


def both(one, two):
    zero = jnp.zeros_like(one)
    return jnp.concatenate(
        [jnp.concatenate([one, zero], axis=1), jnp.concatenate([zero, two], axis=1)], axis=0
    )


def products(index_ref, left_ref, right_ref, acc, to, source):
    acc[...] = jnp.zeros_like(acc)
    ens = acc.shape[2]

    def body(g, carry):
        for j in range(PAIRS):
            pair = g * PAIRS + j
            one = right_ref[index_ref[source, 2 * pair]]
            two = right_ref[index_ref[source, 2 * pair + 1]]
            out = jnp.dot(left_ref[pair], both(one, two), preferred_element_type=F32)
            acc[index_ref[to, 2 * pair]] += out[:, :ens]
            acc[index_ref[to, 2 * pair + 1]] += out[:, ens:]
        return carry

    lax.fori_loop(0, left_ref.shape[0] // PAIRS, body, 0)


def forward_kernel(index_ref, pairs_ref, panels_ref, part_ref, acc):
    products(index_ref, pairs_ref, panels_ref, acc, 0, 1)
    part_ref[...] = acc[pl.ds(0, part_ref.shape[0])].astype(BF16)


def turned_pair(x):
    t = x.T
    return jnp.concatenate([t[:BLOCK], t[BLOCK:]], axis=1)


def exchange_kernel(
    regions, part_ref, obs_ref, inv_ref, pairs_ref, all_ref, own_ref, turned_ref, got, send_a, recv_a, send_b, recv_b, send_c, recv_c
):
    me = lax.axis_index("region")
    rows, ens = obs_ref.shape
    barrier = pltpu.get_barrier_semaphore()
    for k in range(1, regions):
        peer = lax.rem(me + k, regions)
        pl.semaphore_signal(barrier, inc=1, device_id={"region": peer}, device_id_type=MESH)
    row = lax.broadcasted_iota(jnp.int32, (rows, rows), 0)
    col = lax.broadcasted_iota(jnp.int32, (rows, rows), 1)
    inner = row % BLOCK
    half = BLOCK // 2
    picked = (row // BLOCK) * BLOCK + (inner % half) * 2 + inner // half == col
    table = picked.astype(BF16)
    obs = jnp.dot(table, obs_ref[...], preferred_element_type=F32)
    inv = jnp.sum(jnp.where(picked, inv_ref[...], 0.0), axis=1, keepdims=True)
    pl.semaphore_wait(barrier, regions - 1)

    def first(k):
        peer = lax.rem(me + k, regions)
        return pltpu.make_async_remote_copy(
            src_ref=part_ref.at[peer],
            dst_ref=got.at[k],
            send_sem=send_a.at[k],
            recv_sem=recv_a.at[k],
            device_id={"region": peer},
            device_id_type=MESH,
        )

    width = 2 if regions % 2 == 0 else 1
    count = regions // width
    high, low = me // width, lax.rem(me, width)

    def at(k, low):
        return lax.rem(high + count - k, count) * width + low

    def along(k, source):
        return pltpu.make_async_remote_copy(
            src_ref=all_ref.at[source],
            dst_ref=all_ref.at[source],
            send_sem=send_b.at[k],
            recv_sem=recv_b.at[k],
            device_id={"region": lax.rem(high + k, count) * width + low},
            device_id_type=MESH,
        )

    def across(k, source):
        return pltpu.make_async_remote_copy(
            src_ref=all_ref.at[source],
            dst_ref=all_ref.at[source],
            send_sem=send_c.at[k],
            recv_sem=recv_c.at[k],
            device_id={"region": high * width + 1 - low},
            device_id_type=MESH,
        )

    firsts = [first(k) for k in range(1, regions)]
    for copy in firsts:
        copy.start()

    pair_count = pairs_ref.shape[0]

    def turn(g, carry):
        for j in range(TURNS):
            turned_ref[g * TURNS + j] = turned_pair(pairs_ref[g * TURNS + j])
        return carry

    rounds = pair_count // TURNS
    lax.fori_loop(0, rounds // 2, turn, 0)
    evolved = part_ref[me].astype(F32)
    for k in range(1, regions):
        firsts[k - 1].wait_recv()
        evolved = evolved + got[k].astype(F32)
    misfit = (inv * (evolved - obs)).astype(BF16)
    all_ref[me] = misfit
    seconds = [along(k, me) for k in range(1, count)]
    for copy in seconds:
        copy.start()
    if width == 2:
        seconds.append(across(0, me))
        seconds[-1].start()
    own_ref[...] = lax.dot_general(
        table, misfit, (((0,), (0,)), ((), ())), preferred_element_type=F32
    ).astype(BF16)
    lax.fori_loop(rounds // 2, rounds * 3 // 4, turn, 0)
    for k in range(1, count):
        along(k, at(k, low)).wait_recv()
        if width == 2:
            seconds.append(across(k, at(k, low)))
            seconds[-1].start()
    lax.fori_loop(rounds * 3 // 4, rounds, turn, 0)
    if width == 2:
        for k in range(count):
            across(k, at(k, 1 - low)).wait_recv()
    for copy in firsts + seconds:
        copy.wait_send()


def adjoint_kernel(index_ref, turned_ref, misfit_ref, own_ref, acc, misfit_out):
    products(index_ref, turned_ref, misfit_ref, acc, 2, 3)
    misfit_out[...] = own_ref[...]


def gradient_kernel(acc_ref, blend_ref, mix_ref, grad_ref, mine, away, got, send_sem, recv_sem):
    me = lax.axis_index("window")
    other = 1 - me
    slabs, cells, ens = grad_ref.shape
    slices = 2 * slabs
    blocks = cells // BLOCK
    barrier = pltpu.get_barrier_semaphore()
    pl.semaphore_signal(barrier, inc=1, device_id={"window": other}, device_id_type=MESH)
    high, low = spread(blend_ref[...], CELLS_AT_ONCE)
    mix = mix_ref[...]
    pl.semaphore_wait(barrier, 1)

    def send(block):
        return pltpu.make_async_remote_copy(
            src_ref=away.at[block],
            dst_ref=got.at[block],
            send_sem=send_sem.at[block],
            recv_sem=recv_sem.at[block],
            device_id={"window": other},
            device_id_type=MESH,
        )

    def pull(block):
        for within in range(BLOCK // (2 * CELLS_AT_ONCE)):
            sides = []
            for half in range(2):
                start = (2 * within + half) * CELLS_AT_ONCE
                rows = [acc_ref[t * blocks + block, pl.ds(start, CELLS_AT_ONCE), :] for t in range(slices)]
                sides.append(jnp.concatenate(rows, axis=0))
            rhs = jnp.concatenate(sides, axis=1)
            rhs_high = rhs.astype(BF16)
            rhs_low = (rhs - rhs_high.astype(F32)).astype(BF16)
            dims = (((0,), (0,)), ((), ()))
            out = lax.dot_general(high, rhs_high, dims, preferred_element_type=F32)
            out = out + lax.dot_general(low, rhs_high, dims, preferred_element_type=F32)
            out = (out + lax.dot_general(high, rhs_low, dims, preferred_element_type=F32)).astype(BF16)
            for half in range(2):
                start = (2 * within + half) * CELLS_AT_ONCE
                piece = out[:, half * ens : (half + 1) * ens].reshape(slices, CELLS_AT_ONCE, ens)
                first, second = piece[:slabs], piece[slabs:]
                mine[block, :, pl.ds(start, CELLS_AT_ONCE), :] = jnp.where(me == 0, first, second)
                away[block, :, pl.ds(start, CELLS_AT_ONCE), :] = jnp.where(me == 0, second, first)

    def finish(block):
        send(block).wait_recv()
        total = (mine[block].astype(F32) + got[block].astype(F32)).astype(BF16).reshape(slabs * BLOCK, ens)
        grad = jnp.dot(total, mix, preferred_element_type=F32).astype(BF16)
        grad_ref[:, pl.ds(block * BLOCK, BLOCK), :] = grad.reshape(slabs, BLOCK, ens)

    for block in range(blocks):
        pull(block)
        send(block).start()
        if block >= LAG:
            finish(block - LAG)
    for block in range(blocks - LAG, blocks):
        finish(block)
    for block in range(blocks):
        send(block).wait_send()


def vmem():
    return pl.BlockSpec(memory_space=pltpu.VMEM)


def hbm():
    return pl.BlockSpec(memory_space=pltpu.HBM)


def stay(x):
    return pltpu.with_memory_space_constraint(x, pltpu.HBM)


def shards(
    regions,
    flux,
    blend,
    footprints,
    receptor_block,
    cell_block,
    slice_index,
    live_counts,
    observed,
    inv_var,
    prior_mix,
):
    slabs, cells, ens = flux.shape
    slices = blend.shape[0]
    cell_blocks = cells // BLOCK
    panel_total = slices * cell_blocks
    slots = footprints.shape[1]
    rows = observed.shape[1]
    own_blocks = rows // BLOCK
    window_blocks = own_blocks * regions

    panels, pairs, index = pl.pallas_call(
        functools.partial(blend_kernel, window_blocks),
        out_shape=(
            jax.ShapeDtypeStruct((slices, cells, ens), BF16),
            jax.ShapeDtypeStruct((slots // 2, BLOCK, 2 * BLOCK), BF16),
            jax.ShapeDtypeStruct((4, slots), jnp.int32),
        ),
        in_specs=[hbm()] * 3 + [vmem()] + [hbm()] * 3,
        out_specs=(vmem(), vmem(), vmem()),
        scratch_shapes=[
            pltpu.VMEM((slices, cells, ens), BF16),
            pltpu.VMEM((slots, BLOCK * BLOCK), BF16),
            pltpu.VMEM((slices, slices), F32),
            pltpu.VMEM((1, slots), jnp.int32),
            pltpu.VMEM((1, slots), jnp.int32),
            pltpu.VMEM((1, slots), jnp.int32),
            pltpu.SemaphoreType.DMA((4,)),
            pltpu.SemaphoreType.DMA((LOADS,)),
            pltpu.SemaphoreType.DMA((PIECES,)),
            pltpu.SemaphoreType.DMA((PIECES,)),
            pltpu.SemaphoreType.DMA((PIECES,)),
        ],
        compiler_params=pltpu.CompilerParams(collective_id=0, has_side_effects=True, vmem_limit_bytes=24 << 20),
        name="blend_slices",
    )(
        stay(receptor_block),
        stay(cell_block),
        stay(slice_index),
        live_counts,
        stay(blend),
        stay(flux),
        stay(footprints),
    )

    smem = pl.BlockSpec(memory_space=pltpu.SMEM)
    part = pl.pallas_call(
        forward_kernel,
        out_shape=jax.ShapeDtypeStruct((window_blocks, BLOCK, ens), BF16),
        in_specs=[smem, vmem(), vmem()],
        out_specs=vmem(),
        scratch_shapes=[pltpu.VMEM((window_blocks + 1, BLOCK, ens), F32)],
        compiler_params=pltpu.CompilerParams(vmem_limit_bytes=16 << 20),
        name="forward_blocks",
    )(index, pairs, panels.reshape(panel_total, BLOCK, ens))

    misfit_all, own, turned = pl.pallas_call(
        functools.partial(exchange_kernel, regions),
        out_shape=(
            jax.ShapeDtypeStruct((regions, rows, ens), BF16),
            jax.ShapeDtypeStruct((rows, ens), BF16),
            jax.ShapeDtypeStruct((slots // 2, BLOCK, 2 * BLOCK), BF16),
        ),
        in_specs=[vmem()] * 4,
        out_specs=(vmem(), vmem(), vmem()),
        scratch_shapes=[
            pltpu.VMEM((regions, rows, ens), BF16),
            pltpu.SemaphoreType.DMA((regions,)),
            pltpu.SemaphoreType.DMA((regions,)),
            pltpu.SemaphoreType.DMA((regions,)),
            pltpu.SemaphoreType.DMA((regions,)),
            pltpu.SemaphoreType.DMA((regions,)),
            pltpu.SemaphoreType.DMA((regions,)),
        ],
        compiler_params=pltpu.CompilerParams(collective_id=1, has_side_effects=True, vmem_limit_bytes=16 << 20),
        name="misfit_exchange",
    )(part.reshape(regions, rows, ens), observed[0], inv_var, pairs)

    collected, misfit = pl.pallas_call(
        adjoint_kernel,
        out_shape=(
            jax.ShapeDtypeStruct((panel_total + 1, BLOCK, ens), F32),
            jax.ShapeDtypeStruct((rows, ens), BF16),
        ),
        in_specs=[smem, vmem(), vmem(), vmem()],
        out_specs=(vmem(), vmem()),
        compiler_params=pltpu.CompilerParams(vmem_limit_bytes=16 << 20),
        name="adjoint_blocks",
    )(index, turned, misfit_all.reshape(window_blocks, BLOCK, ens), own)

    blocks_shape = (cell_blocks, slabs, BLOCK, ens)
    gradient = pl.pallas_call(
        gradient_kernel,
        out_shape=jax.ShapeDtypeStruct((slabs, cells, ens), BF16),
        in_specs=[vmem(), vmem(), vmem()],
        out_specs=vmem(),
        scratch_shapes=[
            pltpu.VMEM(blocks_shape, BF16),
            pltpu.VMEM(blocks_shape, BF16),
            pltpu.VMEM(blocks_shape, BF16),
            pltpu.SemaphoreType.DMA((cell_blocks,)),
            pltpu.SemaphoreType.DMA((cell_blocks,)),
        ],
        compiler_params=pltpu.CompilerParams(collective_id=2, has_side_effects=True, vmem_limit_bytes=16 << 20),
        name="gradient_exchange",
    )(collected, blend, prior_mix)
    return misfit[None], gradient


def table_for(rows):
    row = lax.broadcasted_iota(jnp.int32, (rows, rows), 0)
    col = lax.broadcasted_iota(jnp.int32, (rows, rows), 1)
    inner = row % BLOCK
    return (row // BLOCK) * BLOCK + (inner % HALF) * 2 + inner // HALF == col


def spread_own_first(matrix, width, me):
    size = matrix.shape[0]
    full = size * width
    row = lax.broadcasted_iota(jnp.int32, (full, size), 0) // width
    col = lax.broadcasted_iota(jnp.int32, (full, size), 1)
    pick = (row == col).astype(BF16)
    pick_own = ((row + me * (size // 2)) % size == col).astype(BF16)
    row_f = lax.broadcasted_iota(jnp.int32, (full, full), 0)
    col_f = lax.broadcasted_iota(jnp.int32, (full, full), 1)
    same = row_f % width == col_f % width
    high = matrix.astype(BF16)
    low = (matrix - high.astype(F32)).astype(BF16)
    nt = (((1,), (1,)), ((), ()))
    blend, pull = [], []
    for part in (high, low):
        tall = jnp.dot(pick, part, preferred_element_type=F32).astype(BF16)
        wide = lax.dot_general(tall, pick_own, nt, preferred_element_type=F32)
        blend.append(jnp.where(same, wide, 0.0).astype(BF16))
        tall = lax.dot_general(pick_own, part, nt, preferred_element_type=F32).astype(BF16)
        wide = lax.dot_general(tall, pick, nt, preferred_element_type=F32)
        pull.append(jnp.where(same, wide, 0.0).astype(BF16))
    return blend, pull


def slot_rows(raw, base):
    return raw[pl.ds(base, SUB), :].reshape(SUB, HALF, 2 * BLOCK)


def place_kernel(
    window_blocks,
    cell_blocks,
    recv_hbm,
    cell_hbm,
    slice_hbm,
    live_ref,
    fp_hbm,
    dense_ref,
    raw,
    recv_ref,
    cell_ref,
    slice_ref,
    dest_ref,
    dest_smem,
    sums,
    small_sem,
    fp_sem,
    dest_sem,
):
    slots = raw.shape[0]
    total = dense_ref.shape[0] - 1
    panels = total // window_blocks
    smalls = [
        pltpu.make_async_copy(source, target, small_sem.at[k])
        for k, (source, target) in enumerate(((recv_hbm, recv_ref), (cell_hbm, cell_ref), (slice_hbm, slice_ref)))
    ]
    for copy in smalls:
        copy.start()
    part = slots // LOADS
    loads = []
    for k in range(LOADS):
        span = pl.ds(k * part, part)
        loads.append(pltpu.make_async_copy(fp_hbm.at[0, span, :], raw.at[span, :], fp_sem.at[k]))
        loads[-1].start()

    def clear(g, carry):
        dense_ref[pl.ds(g * CLEAR, CLEAR)] = jnp.zeros((CLEAR,) + dense_ref.shape[1:], BF16)
        return carry

    lax.fori_loop(0, total // CLEAR // 2, clear, 0)
    dense_ref[total] = jnp.zeros(dense_ref.shape[1:], BF16)
    for copy in smalls:
        copy.wait()
    live = lax.broadcasted_iota(jnp.int32, recv_ref.shape, 1) < live_ref[...]
    panel = slice_ref[...] * cell_blocks + cell_ref[...]
    dest_ref[...] = jnp.where(live, panel * window_blocks + recv_ref[...], total)
    index = pltpu.make_async_copy(dest_ref, dest_smem, dest_sem.at[0])
    index.start()
    row = lax.broadcasted_iota(jnp.int32, (panels, slots), 0)
    named = (row == jnp.where(live, panel, -1)).astype(BF16)
    row = lax.broadcasted_iota(jnp.int32, (window_blocks, slots), 0)
    heard = (row == recv_ref[...]).astype(BF16)
    counts = lax.dot_general(named, heard, (((1,), (1,)), ((), ())), preferred_element_type=F32)
    most = jnp.max(counts)
    lax.fori_loop(total // CLEAR // 2, total // CLEAR, clear, 0)
    index.wait()

    @pl.when(most <= MOST)
    def _():
        for k in range(LOADS):
            loads[k].wait()

            def body(g, carry):
                for sub in range(SUBS):
                    base = pl.multiple_of(k * part + (g * SUBS + sub) * SUB, SUB)
                    x = slot_rows(raw, base)
                    for j in range(0, SUB, 2):
                        one, two = dest_smem[0, base + j], dest_smem[0, base + j + 1]
                        first, second = dense_ref[one], dense_ref[two]
                        again = jnp.where(one == two, x[j], jnp.zeros_like(x[j]))
                        dense_ref[one] = first + x[j]
                        dense_ref[two] = second + again + x[j + 1]
                return carry

            lax.fori_loop(0, part // SUB // SUBS, body, 0)

    @pl.when(most > MOST)
    def _():
        for k in range(LOADS):
            loads[k].wait()
        chunk = sums.shape[0] - 1

        def span(c, carry):
            sums[...] = jnp.zeros_like(sums)

            def body(g, carry):
                base = pl.multiple_of(g * SUB, SUB)
                x = slot_rows(raw, base)
                for j in range(SUB):
                    to = dest_smem[0, base + j] - c * chunk
                    to = jnp.where((to >= 0) & (to < chunk), to, chunk)
                    sums[to] += x[j].astype(F32)
                return carry

            lax.fori_loop(0, slots // SUB, body, 0)

            def store(g, carry):
                dense_ref[c * chunk + g] = sums[g].astype(BF16)
                return carry

            lax.fori_loop(0, chunk, store, 0)
            return carry

        lax.fori_loop(0, total // chunk, span, 0)


def whole_kernel(
    regions,
    dense_ref,
    flux_ref,
    other_ref,
    blend_ref,
    obs_ref,
    inv_ref,
    mix_ref,
    own_ref,
    grad_ref,
    panels,
    acc,
    part,
    got,
    all_ref,
    tiles,
    back,
    mine,
    away,
    pulled,
    send_a,
    recv_a,
    send_b,
    recv_b,
    send_c,
    recv_c,
    send_w,
    recv_w,
):
    me = lax.axis_index("region")
    win = lax.axis_index("window")
    rows, ens = obs_ref.shape
    slabs, cells, _ = flux_ref.shape
    slices = 2 * slabs
    own_blocks = rows // BLOCK
    q_blocks = own_blocks * regions
    cell_blocks = cells // BLOCK
    panel_total = slices * cell_blocks

    barrier = pltpu.get_barrier_semaphore()
    for k in range(1, regions):
        peer = lax.rem(me + k, regions)
        pl.semaphore_signal(barrier, inc=1, device_id={"region": peer}, device_id_type=MESH)
    pl.semaphore_signal(barrier, inc=1, device_id={"window": 1 - win}, device_id_type=MESH)

    (high, low), (pull_high, pull_low) = spread_own_first(blend_ref[...], CELLS_AT_ONCE, win)
    table = table_for(rows)
    obs = jnp.dot(table.astype(BF16), obs_ref[...], preferred_element_type=F32)
    inv = jnp.sum(jnp.where(table, inv_ref[...], 0.0), axis=1, keepdims=True)

    def group(g, carry):
        sides = []
        for half in range(2):
            start = pl.multiple_of((2 * g + half) * CELLS_AT_ONCE, CELLS_AT_ONCE)
            for ref in (flux_ref, other_ref):
                sides.append(ref[:, pl.ds(start, CELLS_AT_ONCE), :].reshape(slabs * CELLS_AT_ONCE, ens))
        rhs = jnp.concatenate(
            [jnp.concatenate(sides[:2], axis=0), jnp.concatenate(sides[2:], axis=0)], axis=1
        )
        out = jnp.dot(high, rhs, preferred_element_type=F32) + jnp.dot(low, rhs, preferred_element_type=F32)
        out = out.astype(BF16)
        for half in range(2):
            start = pl.multiple_of((2 * g + half) * CELLS_AT_ONCE, CELLS_AT_ONCE)
            panels[:, pl.ds(start, CELLS_AT_ONCE), :] = out[:, half * ens : (half + 1) * ens].reshape(
                slices, CELLS_AT_ONCE, ens
            )
        return carry

    lax.fori_loop(0, cells // (2 * CELLS_AT_ONCE), group, 0, unroll=4)

    acc[...] = jnp.zeros_like(acc)

    def forward(g, carry):
        left, right = [], []
        for u in range(AT_ONCE):
            panel = g * AT_ONCE + u
            left.append(dense_ref[pl.ds(panel * q_blocks, q_blocks)].reshape(q_blocks * HALF, 2 * BLOCK))
            cell = (u % cell_blocks) * BLOCK
            one = panels[g * (AT_ONCE // cell_blocks) + u // cell_blocks, cell : cell + BLOCK, :]
            right.append(both(one, one))
        acc[...] += jnp.dot(
            jnp.concatenate(left, axis=1), jnp.concatenate(right, axis=0), preferred_element_type=F32
        )
        return carry

    lax.fori_loop(0, panel_total // AT_ONCE, forward, 0)
    for q in range(q_blocks):
        for side in range(2):
            start = (q % own_blocks) * BLOCK + side * HALF
            part[q // own_blocks, start : start + HALF, :] = acc[
                q * HALF : (q + 1) * HALF, side * ens : (side + 1) * ens
            ].astype(BF16)

    pl.semaphore_wait(barrier, regions)

    def first(k):
        peer = lax.rem(me + k, regions)
        return pltpu.make_async_remote_copy(
            src_ref=part.at[peer],
            dst_ref=got.at[k],
            send_sem=send_a.at[k],
            recv_sem=recv_a.at[k],
            device_id={"region": peer},
            device_id_type=MESH,
        )

    firsts = [first(k) for k in range(1, regions)]
    for copy in firsts:
        copy.start()

    lower = lax.broadcasted_iota(jnp.int32, (HALF, 2 * BLOCK), 1) < BLOCK

    def pair_up(k, carry):
        for q in range(q_blocks):
            one = dense_ref[2 * k * q_blocks + q]
            two = dense_ref[(2 * k + 1) * q_blocks + q]
            tiles[k, pl.ds(q * BLOCK, HALF), :] = jnp.where(lower, one, halves_swapped(two))
            tiles[k, pl.ds(q * BLOCK + HALF, HALF), :] = jnp.where(lower, halves_swapped(one), two)
        return carry

    lax.fori_loop(0, panel_total // 2, pair_up, 0)

    width = 2 if regions % 2 == 0 else 1
    count = regions // width
    far, near = me // width, lax.rem(me, width)

    def at(k, near):
        return lax.rem(far + count - k, count) * width + near

    def along(k, source):
        return pltpu.make_async_remote_copy(
            src_ref=all_ref.at[source],
            dst_ref=all_ref.at[source],
            send_sem=send_b.at[k],
            recv_sem=recv_b.at[k],
            device_id={"region": lax.rem(far + k, count) * width + near},
            device_id_type=MESH,
        )

    def across(k, source):
        return pltpu.make_async_remote_copy(
            src_ref=all_ref.at[source],
            dst_ref=all_ref.at[source],
            send_sem=send_c.at[k],
            recv_sem=recv_c.at[k],
            device_id={"region": far * width + 1 - near},
            device_id_type=MESH,
        )

    evolved = part[me].astype(F32)
    for k in range(1, regions):
        firsts[k - 1].wait_recv()
        evolved = evolved + got[k].astype(F32)
    misfit = (inv * (evolved - obs)).astype(BF16)
    all_ref[me] = misfit.T
    seconds = [along(k, me) for k in range(1, count)]
    for copy in seconds:
        copy.start()
    if width == 2:
        seconds.append(across(0, me))
        seconds[-1].start()
    own_ref[...] = lax.dot_general(
        table.astype(BF16), misfit, (((0,), (0,)), ((), ())), preferred_element_type=F32
    ).astype(BF16)
    for k in range(1, count):
        along(k, at(k, near)).wait_recv()
        if width == 2:
            seconds.append(across(k, at(k, near)))
            seconds[-1].start()
    if width == 2:
        for k in range(count):
            across(k, at(k, 1 - near)).wait_recv()

    turned = jnp.concatenate([all_ref[k] for k in range(regions)], axis=1)
    mix = mix_ref[...]
    columns = 2 * BLOCK
    steps = cells // columns

    def send(step):
        return pltpu.make_async_remote_copy(
            src_ref=away.at[step],
            dst_ref=pulled.at[step],
            send_sem=send_w.at[step],
            recv_sem=recv_w.at[step],
            device_id={"window": 1 - win},
            device_id_type=MESH,
        )

    def adjoint(step):
        for half in range(2):
            right = [tiles[(half * slabs + t) * steps + step] for t in range(slabs)]
            out = jnp.dot(turned, jnp.concatenate(right, axis=1), preferred_element_type=F32).astype(BF16)
            for t in range(slabs):
                back[half * slabs + t] = out[:, t * columns : (t + 1) * columns]
        for e in range(0, ens, 2 * CELLS_AT_ONCE):
            rhs = jnp.concatenate(
                [
                    back[:, e + h * CELLS_AT_ONCE : e + (h + 1) * CELLS_AT_ONCE, :].reshape(
                        slices * CELLS_AT_ONCE, columns
                    )
                    for h in range(2)
                ],
                axis=1,
            )
            out = jnp.dot(pull_high, rhs, preferred_element_type=F32)
            out = (out + jnp.dot(pull_low, rhs, preferred_element_type=F32)).astype(BF16)
            for h in range(2):
                piece = out[:, h * columns : (h + 1) * columns].reshape(slices, CELLS_AT_ONCE, columns)
                at_e = e + h * CELLS_AT_ONCE
                mine[step, :, at_e : at_e + CELLS_AT_ONCE, :] = piece[:slabs]
                away[step, :, at_e : at_e + CELLS_AT_ONCE, :] = piece[slabs:]

    def finish(step):
        send(step).wait_recv()
        total = (mine[step].astype(F32) + pulled[step].astype(F32)).astype(BF16)
        flat = jnp.concatenate([total[s].T for s in range(slabs)], axis=0)
        grad = jnp.dot(flat, mix, preferred_element_type=F32).astype(BF16)
        grad_ref[:, step * columns : (step + 1) * columns, :] = grad.reshape(slabs, columns, ens)

    for step in range(steps):
        adjoint(step)
        send(step).start()
        if step >= DENSE_LAG:
            finish(step - DENSE_LAG)
    for step in range(steps - DENSE_LAG, steps):
        finish(step)
    for step in range(steps):
        send(step).wait_send()
    for copy in firsts + seconds:
        copy.wait_send()


def dense_shards(
    regions,
    flux,
    blend,
    footprints,
    receptor_block,
    cell_block,
    slice_index,
    live_counts,
    observed,
    inv_var,
    prior_mix,
):
    slabs, cells, ens = flux.shape
    slices = blend.shape[0]
    cell_blocks = cells // BLOCK
    panel_total = slices * cell_blocks
    slots = footprints.shape[1]
    rows = observed.shape[1]
    window_blocks = rows // BLOCK * regions
    total = panel_total * window_blocks
    columns = 2 * BLOCK
    steps = cells // columns

    other = lax.ppermute(flux, "window", [(0, 1), (1, 0)])
    dense = pl.pallas_call(
        functools.partial(place_kernel, window_blocks, cell_blocks),
        out_shape=jax.ShapeDtypeStruct((total + 1, HALF, 2 * BLOCK), BF16),
        in_specs=[hbm()] * 3 + [vmem()] + [hbm()],
        out_specs=vmem(),
        scratch_shapes=[
            pltpu.VMEM((slots, BLOCK * BLOCK), BF16),
            pltpu.VMEM((1, slots), jnp.int32),
            pltpu.VMEM((1, slots), jnp.int32),
            pltpu.VMEM((1, slots), jnp.int32),
            pltpu.VMEM((1, slots), jnp.int32),
            pltpu.SMEM((1, slots), jnp.int32),
            pltpu.VMEM((total // 8 + 1, HALF, 2 * BLOCK), F32),
            pltpu.SemaphoreType.DMA((3,)),
            pltpu.SemaphoreType.DMA((LOADS,)),
            pltpu.SemaphoreType.DMA((1,)),
        ],
        compiler_params=pltpu.CompilerParams(vmem_limit_bytes=20 << 20),
        cost_estimate=pl.CostEstimate(flops=0, bytes_accessed=24 << 20, transcendentals=0),
        name="place_blocks",
    )(stay(receptor_block), stay(cell_block), stay(slice_index), live_counts, stay(footprints))

    misfit, gradient = pl.pallas_call(
        functools.partial(whole_kernel, regions),
        out_shape=(
            jax.ShapeDtypeStruct((rows, ens), BF16),
            jax.ShapeDtypeStruct((slabs, cells, ens), BF16),
        ),
        in_specs=[vmem()] * 7,
        out_specs=(vmem(), vmem()),
        scratch_shapes=[
            pltpu.VMEM((slices, cells, ens), BF16),
            pltpu.VMEM((window_blocks * HALF, 2 * ens), F32),
            pltpu.VMEM((regions, rows, ens), BF16),
            pltpu.VMEM((regions, rows, ens), BF16),
            pltpu.VMEM((regions, ens, rows), BF16),
            pltpu.VMEM((panel_total // 2, window_blocks * BLOCK, columns), BF16),
            pltpu.VMEM((slices, ens, columns), BF16),
            pltpu.VMEM((steps, slabs, ens, columns), BF16),
            pltpu.VMEM((steps, slabs, ens, columns), BF16),
            pltpu.VMEM((steps, slabs, ens, columns), BF16),
        ]
        + [pltpu.SemaphoreType.DMA((regions,))] * 6
        + [pltpu.SemaphoreType.DMA((steps,))] * 2,
        compiler_params=pltpu.CompilerParams(collective_id=3, has_side_effects=True, vmem_limit_bytes=30 << 20),
        name="transport",
    )(dense, flux, other, blend, observed[0], inv_var, prior_mix)
    return misfit[None], gradient


def solution(mesh):
    in_specs = (
        P(("group", "window"), "region", None),
        P(),
        P(("group", "window"), "region", None),
        P(("group", "window"), "region"),
        P(("group", "window"), "region"),
        P(("group", "window"), "region"),
        P(("group", "window"), "region"),
        P(("group", "window"), "region", None),
        P(("group", "window"), "region"),
        P(),
    )
    out_specs = (P(("group", "window"), "region", None), P(("group", "window"), "region", None))

    def either(*args):
        regions = mesh.shape["region"]
        blocks = args[7].shape[1] // BLOCK * regions
        return (dense_shards if blocks <= DENSE_BLOCKS else shards)(regions, *args)

    return jax.shard_map(
        either,
        mesh=mesh,
        in_specs=in_specs,
        out_specs=out_specs,
        check_vma=False,
    )
```

```python
import functools

import jax
import jax.numpy as jnp
from jax import lax
from jax.experimental import pallas as pl
from jax.experimental.pallas import tpu as pltpu
from jax.sharding import PartitionSpec as P

BLOCK = 64
MESH = pl.DeviceIdType.MESH
F32 = jnp.float32
BF16 = jnp.bfloat16
SUB = 16
SUBS = 4
CELLS_AT_ONCE = 16
PIECES = 4
LOADS = 8
PAIRS = 32
TURNS = 32
LAG = 2
HALF = BLOCK // 2
CLEAR = 32
MOST = 16
AT_ONCE = 32
DENSE_LAG = 1
DENSE_BLOCKS = 16


def spread(matrix, width):
    size = matrix.shape[0]
    full = size * width
    row = lax.broadcasted_iota(jnp.int32, (full, size), 0)
    col = lax.broadcasted_iota(jnp.int32, (full, size), 1)
    pick = (row // width == col).astype(BF16)
    row_f = lax.broadcasted_iota(jnp.int32, (full, full), 0)
    col_f = lax.broadcasted_iota(jnp.int32, (full, full), 1)
    same = row_f % width == col_f % width
    high = matrix.astype(BF16)
    low = (matrix - high.astype(F32)).astype(BF16)
    parts = []
    for part in (high, low):
        tall = jnp.dot(pick, part, preferred_element_type=F32).astype(BF16)
        wide = lax.dot_general(tall, pick, (((1,), (1,)), ((), ())), preferred_element_type=F32)
        parts.append(jnp.where(same, wide, 0.0).astype(BF16))
    return parts


def halves_swapped(x):
    return pltpu.roll(x, BLOCK, 1)


def blend_kernel(
    window_blocks,
    recv_hbm,
    cell_hbm,
    slice_hbm,
    live_ref,
    blend_hbm,
    flux_hbm,
    fp_hbm,
    panels_ref,
    pairs_ref,
    index_ref,
    full,
    raw,
    blend_ref,
    recv_ref,
    cell_ref,
    slice_ref,
    small_sem,
    fp_sem,
    local_sem,
    send_sem,
    recv_sem,
):
    me = lax.axis_index("window")
    other = 1 - me
    slabs, cells, ens = flux_hbm.shape
    slices = panels_ref.shape[0]
    slots = raw.shape[0]
    barrier = pltpu.get_barrier_semaphore()
    pl.semaphore_signal(barrier, inc=1, device_id={"window": other}, device_id_type=MESH)
    smalls = [
        pltpu.make_async_copy(source, target, small_sem.at[k])
        for k, (source, target) in enumerate(
            ((blend_hbm, blend_ref), (recv_hbm, recv_ref), (cell_hbm, cell_ref), (slice_hbm, slice_ref))
        )
    ]
    for copy in smalls:
        copy.start()
    piece = cells // PIECES
    locals_, sends, loads = [], [], []
    for k in range(PIECES):
        span = pl.ds(k * piece, piece)
        locals_.append(
            pltpu.make_async_copy(
                flux_hbm.at[:, span, :], full.at[pl.ds(me * slabs, slabs), span, :], local_sem.at[k]
            )
        )
        locals_[-1].start()
    part = slots // LOADS
    for k in range(LOADS):
        span = pl.ds(k * part, part)
        loads.append(pltpu.make_async_copy(fp_hbm.at[0, span, :], raw.at[span, :], fp_sem.at[k]))
    loads[0].start()
    pl.semaphore_wait(barrier, 1)
    for k in range(PIECES):
        span = pl.ds(k * piece, piece)
        sends.append(
            pltpu.make_async_remote_copy(
                src_ref=flux_hbm.at[:, span, :],
                dst_ref=full.at[pl.ds(me * slabs, slabs), span, :],
                send_sem=send_sem.at[k],
                recv_sem=recv_sem.at[k],
                device_id={"window": other},
                device_id_type=MESH,
            )
        )
        sends[-1].start()
    for k in range(1, LOADS):
        loads[k].start()

    for copy in smalls:
        copy.wait()
    cell_blocks = cells // BLOCK
    live = lax.broadcasted_iota(jnp.int32, recv_ref.shape, 1) < live_ref[...]
    panel = slice_ref[...] * cell_blocks + cell_ref[...]
    index_ref[pl.ds(0, 1), :] = jnp.where(live, recv_ref[...], window_blocks)
    index_ref[pl.ds(1, 1), :] = jnp.where(live, panel, 0)
    index_ref[pl.ds(2, 1), :] = jnp.where(live, panel, slices * cell_blocks)
    index_ref[pl.ds(3, 1), :] = jnp.where(live, recv_ref[...], 0)
    high, low = spread(blend_ref[...], CELLS_AT_ONCE)

    def arrange(k):
        loads[k].wait()

        def body(g, carry):
            lower = lax.broadcasted_iota(jnp.int32, (BLOCK // 2, 2 * BLOCK), 1) < BLOCK
            for sub in range(SUBS):
                base = pl.multiple_of(k * part + g * SUBS * SUB + sub * SUB, SUB)
                x = raw[pl.ds(base, SUB), :].reshape(SUB, BLOCK // 2, 2 * BLOCK)
                for j in range(0, SUB, 2):
                    one, two = x[j], x[j + 1]
                    even = jnp.where(lower, one, halves_swapped(two))
                    odd = jnp.where(lower, halves_swapped(one), two)
                    place = k * (part // 2) + (g * SUBS + sub) * (SUB // 2) + j // 2
                    pairs_ref[place] = jnp.concatenate([even, odd], axis=0)
            return carry

        lax.fori_loop(0, part // SUB // SUBS, body, 0)

    for k in range(LOADS // 2):
        arrange(k)
    for k in range(PIECES):
        locals_[k].wait()
        sends[k].wait_recv()

        def group(g, carry, k=k):
            sides = []
            for half in range(2):
                start = pl.multiple_of(k * piece + g * 2 * CELLS_AT_ONCE + half * CELLS_AT_ONCE, CELLS_AT_ONCE)
                sides.append(full[:, pl.ds(start, CELLS_AT_ONCE), :].reshape(slices * CELLS_AT_ONCE, ens))
            rhs = jnp.concatenate(sides, axis=1)
            out = jnp.dot(high, rhs, preferred_element_type=F32) + jnp.dot(low, rhs, preferred_element_type=F32)
            out = out.astype(BF16)
            for half in range(2):
                start = pl.multiple_of(k * piece + g * 2 * CELLS_AT_ONCE + half * CELLS_AT_ONCE, CELLS_AT_ONCE)
                panels_ref[:, pl.ds(start, CELLS_AT_ONCE), :] = out[:, half * ens : (half + 1) * ens].reshape(
                    slices, CELLS_AT_ONCE, ens
                )
            return carry

        lax.fori_loop(0, piece // (2 * CELLS_AT_ONCE), group, 0, unroll=2)
    for k in range(LOADS // 2, LOADS):
        arrange(k)
    for k in range(PIECES):
        sends[k].wait_send()


def both(one, two):
    zero = jnp.zeros_like(one)
    return jnp.concatenate(
        [jnp.concatenate([one, zero], axis=1), jnp.concatenate([zero, two], axis=1)], axis=0
    )


def products(index_ref, left_ref, right_ref, acc, to, source):
    acc[...] = jnp.zeros_like(acc)
    ens = acc.shape[2]

    def body(g, carry):
        for j in range(PAIRS):
            pair = g * PAIRS + j
            one = right_ref[index_ref[source, 2 * pair]]
            two = right_ref[index_ref[source, 2 * pair + 1]]
            out = jnp.dot(left_ref[pair], both(one, two), preferred_element_type=F32)
            acc[index_ref[to, 2 * pair]] += out[:, :ens]
            acc[index_ref[to, 2 * pair + 1]] += out[:, ens:]
        return carry

    lax.fori_loop(0, left_ref.shape[0] // PAIRS, body, 0)


def forward_kernel(index_ref, pairs_ref, panels_ref, part_ref, acc):
    products(index_ref, pairs_ref, panels_ref, acc, 0, 1)
    part_ref[...] = acc[pl.ds(0, part_ref.shape[0])].astype(BF16)


def turned_pair(x):
    t = x.T
    return jnp.concatenate([t[:BLOCK], t[BLOCK:]], axis=1)


def exchange_kernel(
    regions, part_ref, obs_ref, inv_ref, pairs_ref, all_ref, own_ref, turned_ref, got, send_a, recv_a, send_b, recv_b, send_c, recv_c
):
    me = lax.axis_index("region")
    rows, ens = obs_ref.shape
    barrier = pltpu.get_barrier_semaphore()
    for k in range(1, regions):
        peer = lax.rem(me + k, regions)
        pl.semaphore_signal(barrier, inc=1, device_id={"region": peer}, device_id_type=MESH)
    row = lax.broadcasted_iota(jnp.int32, (rows, rows), 0)
    col = lax.broadcasted_iota(jnp.int32, (rows, rows), 1)
    inner = row % BLOCK
    half = BLOCK // 2
    picked = (row // BLOCK) * BLOCK + (inner % half) * 2 + inner // half == col
    table = picked.astype(BF16)
    obs = jnp.dot(table, obs_ref[...], preferred_element_type=F32)
    inv = jnp.sum(jnp.where(picked, inv_ref[...], 0.0), axis=1, keepdims=True)
    pl.semaphore_wait(barrier, regions - 1)

    def first(k):
        peer = lax.rem(me + k, regions)
        return pltpu.make_async_remote_copy(
            src_ref=part_ref.at[peer],
            dst_ref=got.at[k],
            send_sem=send_a.at[k],
            recv_sem=recv_a.at[k],
            device_id={"region": peer},
            device_id_type=MESH,
        )

    width = 2 if regions % 2 == 0 else 1
    count = regions // width
    high, low = me // width, lax.rem(me, width)

    def at(k, low):
        return lax.rem(high + count - k, count) * width + low

    def along(k, source):
        return pltpu.make_async_remote_copy(
            src_ref=all_ref.at[source],
            dst_ref=all_ref.at[source],
            send_sem=send_b.at[k],
            recv_sem=recv_b.at[k],
            device_id={"region": lax.rem(high + k, count) * width + low},
            device_id_type=MESH,
        )

    def across(k, source):
        return pltpu.make_async_remote_copy(
            src_ref=all_ref.at[source],
            dst_ref=all_ref.at[source],
            send_sem=send_c.at[k],
            recv_sem=recv_c.at[k],
            device_id={"region": high * width + 1 - low},
            device_id_type=MESH,
        )

    firsts = [first(k) for k in range(1, regions)]
    for copy in firsts:
        copy.start()

    pair_count = pairs_ref.shape[0]

    def turn(g, carry):
        for j in range(TURNS):
            turned_ref[g * TURNS + j] = turned_pair(pairs_ref[g * TURNS + j])
        return carry

    rounds = pair_count // TURNS
    lax.fori_loop(0, rounds // 2, turn, 0)
    evolved = part_ref[me].astype(F32)
    for k in range(1, regions):
        firsts[k - 1].wait_recv()
        evolved = evolved + got[k].astype(F32)
    misfit = (inv * (evolved - obs)).astype(BF16)
    all_ref[me] = misfit
    seconds = [along(k, me) for k in range(1, count)]
    for copy in seconds:
        copy.start()
    if width == 2:
        seconds.append(across(0, me))
        seconds[-1].start()
    own_ref[...] = lax.dot_general(
        table, misfit, (((0,), (0,)), ((), ())), preferred_element_type=F32
    ).astype(BF16)
    lax.fori_loop(rounds // 2, rounds * 3 // 4, turn, 0)
    for k in range(1, count):
        along(k, at(k, low)).wait_recv()
        if width == 2:
            seconds.append(across(k, at(k, low)))
            seconds[-1].start()
    lax.fori_loop(rounds * 3 // 4, rounds, turn, 0)
    if width == 2:
        for k in range(count):
            across(k, at(k, 1 - low)).wait_recv()
    for copy in firsts + seconds:
        copy.wait_send()


def adjoint_kernel(index_ref, turned_ref, misfit_ref, own_ref, acc, misfit_out):
    products(index_ref, turned_ref, misfit_ref, acc, 2, 3)
    misfit_out[...] = own_ref[...]


def gradient_kernel(acc_ref, blend_ref, mix_ref, grad_ref, mine, away, got, send_sem, recv_sem):
    me = lax.axis_index("window")
    other = 1 - me
    slabs, cells, ens = grad_ref.shape
    slices = 2 * slabs
    blocks = cells // BLOCK
    barrier = pltpu.get_barrier_semaphore()
    pl.semaphore_signal(barrier, inc=1, device_id={"window": other}, device_id_type=MESH)
    high, low = spread(blend_ref[...], CELLS_AT_ONCE)
    mix = mix_ref[...]
    pl.semaphore_wait(barrier, 1)

    def send(block):
        return pltpu.make_async_remote_copy(
            src_ref=away.at[block],
            dst_ref=got.at[block],
            send_sem=send_sem.at[block],
            recv_sem=recv_sem.at[block],
            device_id={"window": other},
            device_id_type=MESH,
        )

    def pull(block):
        for within in range(BLOCK // (2 * CELLS_AT_ONCE)):
            sides = []
            for half in range(2):
                start = (2 * within + half) * CELLS_AT_ONCE
                rows = [acc_ref[t * blocks + block, pl.ds(start, CELLS_AT_ONCE), :] for t in range(slices)]
                sides.append(jnp.concatenate(rows, axis=0))
            rhs = jnp.concatenate(sides, axis=1)
            rhs_high = rhs.astype(BF16)
            rhs_low = (rhs - rhs_high.astype(F32)).astype(BF16)
            dims = (((0,), (0,)), ((), ()))
            out = lax.dot_general(high, rhs_high, dims, preferred_element_type=F32)
            out = out + lax.dot_general(low, rhs_high, dims, preferred_element_type=F32)
            out = (out + lax.dot_general(high, rhs_low, dims, preferred_element_type=F32)).astype(BF16)
            for half in range(2):
                start = (2 * within + half) * CELLS_AT_ONCE
                piece = out[:, half * ens : (half + 1) * ens].reshape(slices, CELLS_AT_ONCE, ens)
                first, second = piece[:slabs], piece[slabs:]
                mine[block, :, pl.ds(start, CELLS_AT_ONCE), :] = jnp.where(me == 0, first, second)
                away[block, :, pl.ds(start, CELLS_AT_ONCE), :] = jnp.where(me == 0, second, first)

    def finish(block):
        send(block).wait_recv()
        total = (mine[block].astype(F32) + got[block].astype(F32)).astype(BF16).reshape(slabs * BLOCK, ens)
        grad = jnp.dot(total, mix, preferred_element_type=F32).astype(BF16)
        grad_ref[:, pl.ds(block * BLOCK, BLOCK), :] = grad.reshape(slabs, BLOCK, ens)

    for block in range(blocks):
        pull(block)
        send(block).start()
        if block >= LAG:
            finish(block - LAG)
    for block in range(blocks - LAG, blocks):
        finish(block)
    for block in range(blocks):
        send(block).wait_send()


def vmem():
    return pl.BlockSpec(memory_space=pltpu.VMEM)


def hbm():
    return pl.BlockSpec(memory_space=pltpu.HBM)


def stay(x):
    return pltpu.with_memory_space_constraint(x, pltpu.HBM)


def shards(
    regions,
    flux,
    blend,
    footprints,
    receptor_block,
    cell_block,
    slice_index,
    live_counts,
    observed,
    inv_var,
    prior_mix,
):
    slabs, cells, ens = flux.shape
    slices = blend.shape[0]
    cell_blocks = cells // BLOCK
    panel_total = slices * cell_blocks
    slots = footprints.shape[1]
    rows = observed.shape[1]
    own_blocks = rows // BLOCK
    window_blocks = own_blocks * regions

    panels, pairs, index = pl.pallas_call(
        functools.partial(blend_kernel, window_blocks),
        out_shape=(
            jax.ShapeDtypeStruct((slices, cells, ens), BF16),
            jax.ShapeDtypeStruct((slots // 2, BLOCK, 2 * BLOCK), BF16),
            jax.ShapeDtypeStruct((4, slots), jnp.int32),
        ),
        in_specs=[hbm()] * 3 + [vmem()] + [hbm()] * 3,
        out_specs=(vmem(), vmem(), vmem()),
        scratch_shapes=[
            pltpu.VMEM((slices, cells, ens), BF16),
            pltpu.VMEM((slots, BLOCK * BLOCK), BF16),
            pltpu.VMEM((slices, slices), F32),
            pltpu.VMEM((1, slots), jnp.int32),
            pltpu.VMEM((1, slots), jnp.int32),
            pltpu.VMEM((1, slots), jnp.int32),
            pltpu.SemaphoreType.DMA((4,)),
            pltpu.SemaphoreType.DMA((LOADS,)),
            pltpu.SemaphoreType.DMA((PIECES,)),
            pltpu.SemaphoreType.DMA((PIECES,)),
            pltpu.SemaphoreType.DMA((PIECES,)),
        ],
        compiler_params=pltpu.CompilerParams(collective_id=0, has_side_effects=True, vmem_limit_bytes=24 << 20),
        name="blend_slices",
    )(
        stay(receptor_block),
        stay(cell_block),
        stay(slice_index),
        live_counts,
        stay(blend),
        stay(flux),
        stay(footprints),
    )

    smem = pl.BlockSpec(memory_space=pltpu.SMEM)
    part = pl.pallas_call(
        forward_kernel,
        out_shape=jax.ShapeDtypeStruct((window_blocks, BLOCK, ens), BF16),
        in_specs=[smem, vmem(), vmem()],
        out_specs=vmem(),
        scratch_shapes=[pltpu.VMEM((window_blocks + 1, BLOCK, ens), F32)],
        compiler_params=pltpu.CompilerParams(vmem_limit_bytes=16 << 20),
        name="forward_blocks",
    )(index, pairs, panels.reshape(panel_total, BLOCK, ens))

    misfit_all, own, turned = pl.pallas_call(
        functools.partial(exchange_kernel, regions),
        out_shape=(
            jax.ShapeDtypeStruct((regions, rows, ens), BF16),
            jax.ShapeDtypeStruct((rows, ens), BF16),
            jax.ShapeDtypeStruct((slots // 2, BLOCK, 2 * BLOCK), BF16),
        ),
        in_specs=[vmem()] * 4,
        out_specs=(vmem(), vmem(), vmem()),
        scratch_shapes=[
            pltpu.VMEM((regions, rows, ens), BF16),
            pltpu.SemaphoreType.DMA((regions,)),
            pltpu.SemaphoreType.DMA((regions,)),
            pltpu.SemaphoreType.DMA((regions,)),
            pltpu.SemaphoreType.DMA((regions,)),
            pltpu.SemaphoreType.DMA((regions,)),
            pltpu.SemaphoreType.DMA((regions,)),
        ],
        compiler_params=pltpu.CompilerParams(collective_id=1, has_side_effects=True, vmem_limit_bytes=16 << 20),
        name="misfit_exchange",
    )(part.reshape(regions, rows, ens), observed[0], inv_var, pairs)

    collected, misfit = pl.pallas_call(
        adjoint_kernel,
        out_shape=(
            jax.ShapeDtypeStruct((panel_total + 1, BLOCK, ens), F32),
            jax.ShapeDtypeStruct((rows, ens), BF16),
        ),
        in_specs=[smem, vmem(), vmem(), vmem()],
        out_specs=(vmem(), vmem()),
        compiler_params=pltpu.CompilerParams(vmem_limit_bytes=16 << 20),
        name="adjoint_blocks",
    )(index, turned, misfit_all.reshape(window_blocks, BLOCK, ens), own)

    blocks_shape = (cell_blocks, slabs, BLOCK, ens)
    gradient = pl.pallas_call(
        gradient_kernel,
        out_shape=jax.ShapeDtypeStruct((slabs, cells, ens), BF16),
        in_specs=[vmem(), vmem(), vmem()],
        out_specs=vmem(),
        scratch_shapes=[
            pltpu.VMEM(blocks_shape, BF16),
            pltpu.VMEM(blocks_shape, BF16),
            pltpu.VMEM(blocks_shape, BF16),
            pltpu.SemaphoreType.DMA((cell_blocks,)),
            pltpu.SemaphoreType.DMA((cell_blocks,)),
        ],
        compiler_params=pltpu.CompilerParams(collective_id=2, has_side_effects=True, vmem_limit_bytes=16 << 20),
        name="gradient_exchange",
    )(collected, blend, prior_mix)
    return misfit[None], gradient


def table_for(rows):
    row = lax.broadcasted_iota(jnp.int32, (rows, rows), 0)
    col = lax.broadcasted_iota(jnp.int32, (rows, rows), 1)
    inner = row % BLOCK
    return (row // BLOCK) * BLOCK + (inner % HALF) * 2 + inner // HALF == col


def spread_own_first(matrix, width, me, pulling):
    size = matrix.shape[0]
    full = size * width
    row = lax.broadcasted_iota(jnp.int32, (full, size), 0) // width
    col = lax.broadcasted_iota(jnp.int32, (full, size), 1)
    pick = (row == col).astype(BF16)
    pick_own = ((row + me * (size // 2)) % size == col).astype(BF16)
    row_f = lax.broadcasted_iota(jnp.int32, (full, full), 0)
    col_f = lax.broadcasted_iota(jnp.int32, (full, full), 1)
    same = row_f % width == col_f % width
    high = matrix.astype(BF16)
    low = (matrix - high.astype(F32)).astype(BF16)
    nt = (((1,), (1,)), ((), ()))
    parts = []
    for part in (high, low):
        if pulling:
            tall = lax.dot_general(pick_own, part, nt, preferred_element_type=F32).astype(BF16)
            wide = lax.dot_general(tall, pick, nt, preferred_element_type=F32)
        else:
            tall = jnp.dot(pick, part, preferred_element_type=F32).astype(BF16)
            wide = lax.dot_general(tall, pick_own, nt, preferred_element_type=F32)
        parts.append(jnp.where(same, wide, 0.0).astype(BF16))
    return parts


def slot_rows(raw, base):
    return raw[pl.ds(base, SUB), :].reshape(SUB, HALF, 2 * BLOCK)


def place_kernel(
    window_blocks,
    cell_blocks,
    recv_hbm,
    cell_hbm,
    slice_hbm,
    live_ref,
    fp_hbm,
    dense_ref,
    raw,
    recv_ref,
    cell_ref,
    slice_ref,
    dest_ref,
    dest_smem,
    sums,
    small_sem,
    fp_sem,
    dest_sem,
):
    slots = raw.shape[0]
    total = dense_ref.shape[0] - 1
    panels = total // window_blocks
    smalls = [
        pltpu.make_async_copy(source, target, small_sem.at[k])
        for k, (source, target) in enumerate(((recv_hbm, recv_ref), (cell_hbm, cell_ref), (slice_hbm, slice_ref)))
    ]
    for copy in smalls:
        copy.start()
    part = slots // LOADS
    loads = []
    for k in range(LOADS):
        span = pl.ds(k * part, part)
        loads.append(pltpu.make_async_copy(fp_hbm.at[0, span, :], raw.at[span, :], fp_sem.at[k]))
        loads[-1].start()

    def clear(g, carry):
        dense_ref[pl.ds(g * CLEAR, CLEAR)] = jnp.zeros((CLEAR,) + dense_ref.shape[1:], BF16)
        return carry

    lax.fori_loop(0, total // CLEAR // 2, clear, 0)
    dense_ref[total] = jnp.zeros(dense_ref.shape[1:], BF16)
    for copy in smalls:
        copy.wait()
    live = lax.broadcasted_iota(jnp.int32, recv_ref.shape, 1) < live_ref[...]
    panel = slice_ref[...] * cell_blocks + cell_ref[...]
    dest_ref[...] = jnp.where(live, panel * window_blocks + recv_ref[...], total)
    index = pltpu.make_async_copy(dest_ref, dest_smem, dest_sem.at[0])
    index.start()
    row = lax.broadcasted_iota(jnp.int32, (panels, slots), 0)
    named = (row == jnp.where(live, panel, -1)).astype(BF16)
    row = lax.broadcasted_iota(jnp.int32, (window_blocks, slots), 0)
    heard = (row == recv_ref[...]).astype(BF16)
    counts = lax.dot_general(named, heard, (((1,), (1,)), ((), ())), preferred_element_type=F32)
    most = jnp.max(counts)
    lax.fori_loop(total // CLEAR // 2, total // CLEAR, clear, 0)
    index.wait()

    @pl.when(most <= MOST)
    def _():
        for k in range(LOADS):
            loads[k].wait()

            def body(g, carry):
                for sub in range(SUBS):
                    base = pl.multiple_of(k * part + (g * SUBS + sub) * SUB, SUB)
                    x = slot_rows(raw, base)
                    for j in range(0, SUB, 2):
                        one, two = dest_smem[0, base + j], dest_smem[0, base + j + 1]
                        first, second = dense_ref[one], dense_ref[two]
                        again = jnp.where(one == two, x[j], jnp.zeros_like(x[j]))
                        dense_ref[one] = first + x[j]
                        dense_ref[two] = second + again + x[j + 1]
                return carry

            lax.fori_loop(0, part // SUB // SUBS, body, 0)

    @pl.when(most > MOST)
    def _():
        for k in range(LOADS):
            loads[k].wait()
        chunk = sums.shape[0] - 1

        def span(c, carry):
            sums[...] = jnp.zeros_like(sums)

            def body(g, carry):
                base = pl.multiple_of(g * SUB, SUB)
                x = slot_rows(raw, base)
                for j in range(SUB):
                    to = dest_smem[0, base + j] - c * chunk
                    to = jnp.where((to >= 0) & (to < chunk), to, chunk)
                    sums[to] += x[j].astype(F32)
                return carry

            lax.fori_loop(0, slots // SUB, body, 0)

            def store(g, carry):
                dense_ref[c * chunk + g] = sums[g].astype(BF16)
                return carry

            lax.fori_loop(0, chunk, store, 0)
            return carry

        lax.fori_loop(0, total // chunk, span, 0)


def whole_kernel(
    regions,
    dense_ref,
    flux_ref,
    other_ref,
    blend_ref,
    obs_ref,
    inv_ref,
    mix_ref,
    own_ref,
    grad_ref,
    panels,
    acc,
    part,
    got,
    all_ref,
    tiles,
    sums,
    back,
    mine,
    away,
    pulled,
    send_a,
    recv_a,
    send_b,
    recv_b,
    send_w,
    recv_w,
):
    me = lax.axis_index("region")
    win = lax.axis_index("window")
    rows, ens = obs_ref.shape
    slabs, cells, _ = flux_ref.shape
    slices = 2 * slabs
    own_blocks = rows // BLOCK
    q_blocks = own_blocks * regions
    cell_blocks = cells // BLOCK
    panel_total = slices * cell_blocks

    barrier = pltpu.get_barrier_semaphore()
    for k in range(1, regions):
        peer = lax.rem(me + k, regions)
        pl.semaphore_signal(barrier, inc=1, device_id={"region": peer}, device_id_type=MESH)
    pl.semaphore_signal(barrier, inc=1, device_id={"window": 1 - win}, device_id_type=MESH)

    high, low = spread_own_first(blend_ref[...], CELLS_AT_ONCE, win, False)

    def group(g, carry):
        sides = []
        for half in range(2):
            start = pl.multiple_of((2 * g + half) * CELLS_AT_ONCE, CELLS_AT_ONCE)
            for ref in (flux_ref, other_ref):
                sides.append(ref[:, pl.ds(start, CELLS_AT_ONCE), :].reshape(slabs * CELLS_AT_ONCE, ens))
        rhs = jnp.concatenate(
            [jnp.concatenate(sides[:2], axis=0), jnp.concatenate(sides[2:], axis=0)], axis=1
        )
        out = jnp.dot(high, rhs, preferred_element_type=F32) + jnp.dot(low, rhs, preferred_element_type=F32)
        out = out.astype(BF16)
        for half in range(2):
            start = pl.multiple_of((2 * g + half) * CELLS_AT_ONCE, CELLS_AT_ONCE)
            panels[:, pl.ds(start, CELLS_AT_ONCE), :] = out[:, half * ens : (half + 1) * ens].reshape(
                slices, CELLS_AT_ONCE, ens
            )
        return carry

    lax.fori_loop(0, cells // (2 * CELLS_AT_ONCE), group, 0, unroll=4)

    group_size = regions // 2
    near = (me // group_size) * group_size
    far = group_size - near
    span = group_size * own_blocks

    def forward(first_region):
        acc[...] = jnp.zeros_like(acc)

        def body(g, carry):
            left, right = [], []
            for u in range(AT_ONCE):
                start = (g * AT_ONCE + u) * q_blocks + first_region * own_blocks
                left.append(dense_ref[pl.ds(start, span)].reshape(span * HALF, 2 * BLOCK))
                cell = (u % cell_blocks) * BLOCK
                one = panels[g * (AT_ONCE // cell_blocks) + u // cell_blocks, cell : cell + BLOCK, :]
                right.append(both(one, one))
            acc[...] += jnp.dot(
                jnp.concatenate(left, axis=1), jnp.concatenate(right, axis=0), preferred_element_type=F32
            )
            return carry

        lax.fori_loop(0, panel_total // AT_ONCE, body, 0)
        for q in range(span):
            for side in range(2):
                start = (q % own_blocks) * BLOCK + side * HALF
                part[first_region + q // own_blocks, start : start + HALF, :] = acc[
                    q * HALF : (q + 1) * HALF, side * ens : (side + 1) * ens
                ].astype(BF16)

    def reduce_copy(source, to):
        return pltpu.make_async_remote_copy(
            src_ref=part.at[to],
            dst_ref=got.at[source],
            send_sem=send_a.at[to],
            recv_sem=recv_a.at[source],
            device_id={"region": to},
            device_id_type=MESH,
        )

    def gather_copy(source, to):
        return pltpu.make_async_remote_copy(
            src_ref=all_ref.at[source],
            dst_ref=all_ref.at[source],
            send_sem=send_b.at[to],
            recv_sem=recv_b.at[source],
            device_id={"region": to},
            device_id_type=MESH,
        )

    fars = [far + (me - near + k) % group_size for k in range(group_size)]
    nears = [near + (me - near + k) % group_size for k in range(1, group_size)]

    forward(far)
    pl.semaphore_wait(barrier, regions)
    for peer in fars:
        reduce_copy(me, peer).start()
    forward(near)
    for peer in nears:
        reduce_copy(me, peer).start()

    lower = lax.broadcasted_iota(jnp.int32, (HALF, 2 * BLOCK), 1) < BLOCK

    def pair_up(g, carry):
        for k in range(2):
            for q in range(q_blocks):
                one = dense_ref[(4 * g + 2 * k) * q_blocks + q]
                two = dense_ref[(4 * g + 2 * k + 1) * q_blocks + q]
                swapped = halves_swapped(jnp.where(lower, two, one))
                tiles[2 * g + k, pl.ds(q * BLOCK, HALF), :] = jnp.where(lower, one, swapped)
                tiles[2 * g + k, pl.ds(q * BLOCK + HALF, HALF), :] = jnp.where(lower, swapped, two)
        return carry

    table = table_for(rows)
    obs = jnp.dot(table.astype(BF16), obs_ref[...], preferred_element_type=F32)
    inv = jnp.sum(jnp.where(table, inv_ref[...], 0.0), axis=1, keepdims=True)
    rounds = panel_total // 4
    lax.fori_loop(0, rounds // 2, pair_up, 0)

    evolved = part[me].astype(F32)
    for peer in nears + fars:
        reduce_copy(peer, me).wait_recv()
        evolved = evolved + got[peer].astype(F32)
    misfit = (inv * (evolved - obs)).astype(BF16)
    all_ref[me] = misfit.T
    for peer in fars + nears:
        gather_copy(me, peer).start()
    own_ref[...] = lax.dot_general(
        table.astype(BF16), misfit, (((0,), (0,)), ((), ())), preferred_element_type=F32
    ).astype(BF16)
    lax.fori_loop(rounds // 2, rounds, pair_up, 0)
    pull_high, pull_low = spread_own_first(blend_ref[...], CELLS_AT_ONCE, win, True)

    mix = mix_ref[...]
    columns = 2 * BLOCK
    steps = cells // columns

    def send(step):
        return pltpu.make_async_remote_copy(
            src_ref=away.at[step],
            dst_ref=pulled.at[step],
            send_sem=send_w.at[step],
            recv_sem=recv_w.at[step],
            device_id={"window": 1 - win},
            device_id_type=MESH,
        )

    def product(step, half, first_region, turned):
        right = [
            tiles[(half * slabs + t) * steps + step, pl.ds(first_region * rows, group_size * rows), :]
            for t in range(slabs)
        ]
        return jnp.dot(turned, jnp.concatenate(right, axis=1), preferred_element_type=F32)

    for peer in nears:
        gather_copy(peer, me).wait_recv()
    turned_near = jnp.concatenate([all_ref[near + k] for k in range(group_size)], axis=1)
    for step in range(steps):
        for half in range(2):
            sums[step, half] = product(step, half, near, turned_near)
    for peer in fars:
        gather_copy(peer, me).wait_recv()
    turned_far = jnp.concatenate([all_ref[far + k] for k in range(group_size)], axis=1)

    def adjoint(step):
        for half in range(2):
            out = (sums[step, half] + product(step, half, far, turned_far)).astype(BF16)
            for t in range(slabs):
                back[half * slabs + t] = out[:, t * columns : (t + 1) * columns]
        for e in range(0, ens, 2 * CELLS_AT_ONCE):
            rhs = jnp.concatenate(
                [
                    back[:, e + h * CELLS_AT_ONCE : e + (h + 1) * CELLS_AT_ONCE, :].reshape(
                        slices * CELLS_AT_ONCE, columns
                    )
                    for h in range(2)
                ],
                axis=1,
            )
            out = jnp.dot(pull_high, rhs, preferred_element_type=F32)
            out = (out + jnp.dot(pull_low, rhs, preferred_element_type=F32)).astype(BF16)
            for h in range(2):
                piece = out[:, h * columns : (h + 1) * columns].reshape(slices, CELLS_AT_ONCE, columns)
                at_e = e + h * CELLS_AT_ONCE
                mine[step, :, at_e : at_e + CELLS_AT_ONCE, :] = piece[:slabs]
                away[step, :, at_e : at_e + CELLS_AT_ONCE, :] = piece[slabs:]

    def finish(step):
        send(step).wait_recv()
        total = (mine[step].astype(F32) + pulled[step].astype(F32)).astype(BF16)
        flat = jnp.concatenate([total[s].T for s in range(slabs)], axis=0)
        grad = jnp.dot(flat, mix, preferred_element_type=F32).astype(BF16)
        grad_ref[:, step * columns : (step + 1) * columns, :] = grad.reshape(slabs, columns, ens)

    for step in range(steps):
        adjoint(step)
        send(step).start()
        if step >= DENSE_LAG:
            finish(step - DENSE_LAG)
    for step in range(steps - DENSE_LAG, steps):
        finish(step)
    for step in range(steps):
        send(step).wait_send()
    for peer in nears + fars:
        reduce_copy(me, peer).wait_send()
        gather_copy(me, peer).wait_send()


def dense_shards(
    regions,
    flux,
    blend,
    footprints,
    receptor_block,
    cell_block,
    slice_index,
    live_counts,
    observed,
    inv_var,
    prior_mix,
):
    slabs, cells, ens = flux.shape
    slices = blend.shape[0]
    cell_blocks = cells // BLOCK
    panel_total = slices * cell_blocks
    slots = footprints.shape[1]
    rows = observed.shape[1]
    window_blocks = rows // BLOCK * regions
    total = panel_total * window_blocks
    columns = 2 * BLOCK
    steps = cells // columns

    other = lax.ppermute(flux, "window", [(0, 1), (1, 0)])
    dense = pl.pallas_call(
        functools.partial(place_kernel, window_blocks, cell_blocks),
        out_shape=jax.ShapeDtypeStruct((total + 1, HALF, 2 * BLOCK), BF16),
        in_specs=[hbm()] * 3 + [vmem()] + [hbm()],
        out_specs=vmem(),
        scratch_shapes=[
            pltpu.VMEM((slots, BLOCK * BLOCK), BF16),
            pltpu.VMEM((1, slots), jnp.int32),
            pltpu.VMEM((1, slots), jnp.int32),
            pltpu.VMEM((1, slots), jnp.int32),
            pltpu.VMEM((1, slots), jnp.int32),
            pltpu.SMEM((1, slots), jnp.int32),
            pltpu.VMEM((total // 8 + 1, HALF, 2 * BLOCK), F32),
            pltpu.SemaphoreType.DMA((3,)),
            pltpu.SemaphoreType.DMA((LOADS,)),
            pltpu.SemaphoreType.DMA((1,)),
        ],
        compiler_params=pltpu.CompilerParams(vmem_limit_bytes=20 << 20),
        cost_estimate=pl.CostEstimate(flops=0, bytes_accessed=24 << 20, transcendentals=0),
        name="place_blocks",
    )(stay(receptor_block), stay(cell_block), stay(slice_index), live_counts, stay(footprints))

    misfit, gradient = pl.pallas_call(
        functools.partial(whole_kernel, regions),
        out_shape=(
            jax.ShapeDtypeStruct((rows, ens), BF16),
            jax.ShapeDtypeStruct((slabs, cells, ens), BF16),
        ),
        in_specs=[vmem()] * 7,
        out_specs=(vmem(), vmem()),
        scratch_shapes=[
            pltpu.VMEM((slices, cells, ens), BF16),
            pltpu.VMEM((window_blocks // 2 * HALF, 2 * ens), F32),
            pltpu.VMEM((regions, rows, ens), BF16),
            pltpu.VMEM((regions, rows, ens), BF16),
            pltpu.VMEM((regions, ens, rows), BF16),
            pltpu.VMEM((panel_total // 2, window_blocks * BLOCK, columns), BF16),
            pltpu.VMEM((steps, 2, ens, slabs * columns), F32),
            pltpu.VMEM((slices, ens, columns), BF16),
            pltpu.VMEM((steps, slabs, ens, columns), BF16),
            pltpu.VMEM((steps, slabs, ens, columns), BF16),
            pltpu.VMEM((steps, slabs, ens, columns), BF16),
        ]
        + [pltpu.SemaphoreType.DMA((regions,))] * 4
        + [pltpu.SemaphoreType.DMA((steps,))] * 2,
        compiler_params=pltpu.CompilerParams(collective_id=3, has_side_effects=True, vmem_limit_bytes=34 << 20),
        name="transport",
    )(dense, flux, other, blend, observed[0], inv_var, prior_mix)
    return misfit[None], gradient


def solution(mesh):
    in_specs = (
        P(("group", "window"), "region", None),
        P(),
        P(("group", "window"), "region", None),
        P(("group", "window"), "region"),
        P(("group", "window"), "region"),
        P(("group", "window"), "region"),
        P(("group", "window"), "region"),
        P(("group", "window"), "region", None),
        P(("group", "window"), "region"),
        P(),
    )
    out_specs = (P(("group", "window"), "region", None), P(("group", "window"), "region", None))

    def either(*args):
        regions = mesh.shape["region"]
        blocks = args[7].shape[1] // BLOCK * regions
        return (dense_shards if blocks <= DENSE_BLOCKS and regions % 2 == 0 else shards)(regions, *args)

    return jax.shard_map(
        either,
        mesh=mesh,
        in_specs=in_specs,
        out_specs=out_specs,
        check_vma=False,
    )
```

```python
import functools

import jax
import jax.numpy as jnp
from jax import lax
from jax.experimental import pallas as pl
from jax.experimental.pallas import tpu as pltpu
from jax.sharding import PartitionSpec as P

BLOCK = 64
MESH = pl.DeviceIdType.MESH
F32 = jnp.float32
BF16 = jnp.bfloat16
SUB = 16
SUBS = 4
CELLS_AT_ONCE = 16
PIECES = 4
LOADS = 8
PAIRS = 32
TURNS = 32
LAG = 2
HALF = BLOCK // 2
CLEAR = 32
MOST = 16
DENSE_SUBS = 4
AT_ONCE = 32
DENSE_LAG = 3
DENSE_VMEM = 28 << 20
DENSE_BLOCKS = 16


def spread(matrix, width):
    size = matrix.shape[0]
    full = size * width
    row = lax.broadcasted_iota(jnp.int32, (full, size), 0)
    col = lax.broadcasted_iota(jnp.int32, (full, size), 1)
    pick = (row // width == col).astype(BF16)
    row_f = lax.broadcasted_iota(jnp.int32, (full, full), 0)
    col_f = lax.broadcasted_iota(jnp.int32, (full, full), 1)
    same = row_f % width == col_f % width
    high = matrix.astype(BF16)
    low = (matrix - high.astype(F32)).astype(BF16)
    parts = []
    for part in (high, low):
        tall = jnp.dot(pick, part, preferred_element_type=F32).astype(BF16)
        wide = lax.dot_general(tall, pick, (((1,), (1,)), ((), ())), preferred_element_type=F32)
        parts.append(jnp.where(same, wide, 0.0).astype(BF16))
    return parts


def halves_swapped(x):
    return pltpu.roll(x, BLOCK, 1)


def blend_kernel(
    window_blocks,
    recv_hbm,
    cell_hbm,
    slice_hbm,
    live_ref,
    blend_hbm,
    flux_hbm,
    fp_hbm,
    panels_ref,
    pairs_ref,
    index_ref,
    full,
    raw,
    blend_ref,
    recv_ref,
    cell_ref,
    slice_ref,
    small_sem,
    fp_sem,
    local_sem,
    send_sem,
    recv_sem,
):
    me = lax.axis_index("window")
    other = 1 - me
    slabs, cells, ens = flux_hbm.shape
    slices = panels_ref.shape[0]
    slots = raw.shape[0]
    barrier = pltpu.get_barrier_semaphore()
    pl.semaphore_signal(barrier, inc=1, device_id={"window": other}, device_id_type=MESH)
    smalls = [
        pltpu.make_async_copy(source, target, small_sem.at[k])
        for k, (source, target) in enumerate(
            ((blend_hbm, blend_ref), (recv_hbm, recv_ref), (cell_hbm, cell_ref), (slice_hbm, slice_ref))
        )
    ]
    for copy in smalls:
        copy.start()
    piece = cells // PIECES
    locals_, sends, loads = [], [], []
    for k in range(PIECES):
        span = pl.ds(k * piece, piece)
        locals_.append(
            pltpu.make_async_copy(
                flux_hbm.at[:, span, :], full.at[pl.ds(me * slabs, slabs), span, :], local_sem.at[k]
            )
        )
        locals_[-1].start()
    part = slots // LOADS
    for k in range(LOADS):
        span = pl.ds(k * part, part)
        loads.append(pltpu.make_async_copy(fp_hbm.at[0, span, :], raw.at[span, :], fp_sem.at[k]))
    loads[0].start()
    pl.semaphore_wait(barrier, 1)
    for k in range(PIECES):
        span = pl.ds(k * piece, piece)
        sends.append(
            pltpu.make_async_remote_copy(
                src_ref=flux_hbm.at[:, span, :],
                dst_ref=full.at[pl.ds(me * slabs, slabs), span, :],
                send_sem=send_sem.at[k],
                recv_sem=recv_sem.at[k],
                device_id={"window": other},
                device_id_type=MESH,
            )
        )
        sends[-1].start()
    for k in range(1, LOADS):
        loads[k].start()

    for copy in smalls:
        copy.wait()
    cell_blocks = cells // BLOCK
    live = lax.broadcasted_iota(jnp.int32, recv_ref.shape, 1) < live_ref[...]
    panel = slice_ref[...] * cell_blocks + cell_ref[...]
    index_ref[pl.ds(0, 1), :] = jnp.where(live, recv_ref[...], window_blocks)
    index_ref[pl.ds(1, 1), :] = jnp.where(live, panel, 0)
    index_ref[pl.ds(2, 1), :] = jnp.where(live, panel, slices * cell_blocks)
    index_ref[pl.ds(3, 1), :] = jnp.where(live, recv_ref[...], 0)
    high, low = spread(blend_ref[...], CELLS_AT_ONCE)

    def arrange(k):
        loads[k].wait()

        def body(g, carry):
            lower = lax.broadcasted_iota(jnp.int32, (BLOCK // 2, 2 * BLOCK), 1) < BLOCK
            for sub in range(SUBS):
                base = pl.multiple_of(k * part + g * SUBS * SUB + sub * SUB, SUB)
                x = raw[pl.ds(base, SUB), :].reshape(SUB, BLOCK // 2, 2 * BLOCK)
                for j in range(0, SUB, 2):
                    one, two = x[j], x[j + 1]
                    even = jnp.where(lower, one, halves_swapped(two))
                    odd = jnp.where(lower, halves_swapped(one), two)
                    place = k * (part // 2) + (g * SUBS + sub) * (SUB // 2) + j // 2
                    pairs_ref[place] = jnp.concatenate([even, odd], axis=0)
            return carry

        lax.fori_loop(0, part // SUB // SUBS, body, 0)

    for k in range(LOADS // 2):
        arrange(k)
    for k in range(PIECES):
        locals_[k].wait()
        sends[k].wait_recv()

        def group(g, carry, k=k):
            sides = []
            for half in range(2):
                start = pl.multiple_of(k * piece + g * 2 * CELLS_AT_ONCE + half * CELLS_AT_ONCE, CELLS_AT_ONCE)
                sides.append(full[:, pl.ds(start, CELLS_AT_ONCE), :].reshape(slices * CELLS_AT_ONCE, ens))
            rhs = jnp.concatenate(sides, axis=1)
            out = jnp.dot(high, rhs, preferred_element_type=F32) + jnp.dot(low, rhs, preferred_element_type=F32)
            out = out.astype(BF16)
            for half in range(2):
                start = pl.multiple_of(k * piece + g * 2 * CELLS_AT_ONCE + half * CELLS_AT_ONCE, CELLS_AT_ONCE)
                panels_ref[:, pl.ds(start, CELLS_AT_ONCE), :] = out[:, half * ens : (half + 1) * ens].reshape(
                    slices, CELLS_AT_ONCE, ens
                )
            return carry

        lax.fori_loop(0, piece // (2 * CELLS_AT_ONCE), group, 0, unroll=2)
    for k in range(LOADS // 2, LOADS):
        arrange(k)
    for k in range(PIECES):
        sends[k].wait_send()


def both(one, two):
    zero = jnp.zeros_like(one)
    return jnp.concatenate(
        [jnp.concatenate([one, zero], axis=1), jnp.concatenate([zero, two], axis=1)], axis=0
    )


def products(index_ref, left_ref, right_ref, acc, to, source):
    acc[...] = jnp.zeros_like(acc)
    ens = acc.shape[2]

    def body(g, carry):
        for j in range(PAIRS):
            pair = g * PAIRS + j
            one = right_ref[index_ref[source, 2 * pair]]
            two = right_ref[index_ref[source, 2 * pair + 1]]
            out = jnp.dot(left_ref[pair], both(one, two), preferred_element_type=F32)
            acc[index_ref[to, 2 * pair]] += out[:, :ens]
            acc[index_ref[to, 2 * pair + 1]] += out[:, ens:]
        return carry

    lax.fori_loop(0, left_ref.shape[0] // PAIRS, body, 0)


def forward_kernel(index_ref, pairs_ref, panels_ref, part_ref, acc):
    products(index_ref, pairs_ref, panels_ref, acc, 0, 1)
    part_ref[...] = acc[pl.ds(0, part_ref.shape[0])].astype(BF16)


def turned_pair(x):
    t = x.T
    return jnp.concatenate([t[:BLOCK], t[BLOCK:]], axis=1)


def exchange_kernel(
    regions, part_ref, obs_ref, inv_ref, pairs_ref, all_ref, own_ref, turned_ref, got, send_a, recv_a, send_b, recv_b, send_c, recv_c
):
    me = lax.axis_index("region")
    rows, ens = obs_ref.shape
    barrier = pltpu.get_barrier_semaphore()
    for k in range(1, regions):
        peer = lax.rem(me + k, regions)
        pl.semaphore_signal(barrier, inc=1, device_id={"region": peer}, device_id_type=MESH)
    row = lax.broadcasted_iota(jnp.int32, (rows, rows), 0)
    col = lax.broadcasted_iota(jnp.int32, (rows, rows), 1)
    inner = row % BLOCK
    half = BLOCK // 2
    picked = (row // BLOCK) * BLOCK + (inner % half) * 2 + inner // half == col
    table = picked.astype(BF16)
    obs = jnp.dot(table, obs_ref[...], preferred_element_type=F32)
    inv = jnp.sum(jnp.where(picked, inv_ref[...], 0.0), axis=1, keepdims=True)
    pl.semaphore_wait(barrier, regions - 1)

    def first(k):
        peer = lax.rem(me + k, regions)
        return pltpu.make_async_remote_copy(
            src_ref=part_ref.at[peer],
            dst_ref=got.at[k],
            send_sem=send_a.at[k],
            recv_sem=recv_a.at[k],
            device_id={"region": peer},
            device_id_type=MESH,
        )

    width = 2 if regions % 2 == 0 else 1
    count = regions // width
    high, low = me // width, lax.rem(me, width)

    def at(k, low):
        return lax.rem(high + count - k, count) * width + low

    def along(k, source):
        return pltpu.make_async_remote_copy(
            src_ref=all_ref.at[source],
            dst_ref=all_ref.at[source],
            send_sem=send_b.at[k],
            recv_sem=recv_b.at[k],
            device_id={"region": lax.rem(high + k, count) * width + low},
            device_id_type=MESH,
        )

    def across(k, source):
        return pltpu.make_async_remote_copy(
            src_ref=all_ref.at[source],
            dst_ref=all_ref.at[source],
            send_sem=send_c.at[k],
            recv_sem=recv_c.at[k],
            device_id={"region": high * width + 1 - low},
            device_id_type=MESH,
        )

    firsts = [first(k) for k in range(1, regions)]
    for copy in firsts:
        copy.start()

    pair_count = pairs_ref.shape[0]

    def turn(g, carry):
        for j in range(TURNS):
            turned_ref[g * TURNS + j] = turned_pair(pairs_ref[g * TURNS + j])
        return carry

    rounds = pair_count // TURNS
    lax.fori_loop(0, rounds // 2, turn, 0)
    evolved = part_ref[me].astype(F32)
    for k in range(1, regions):
        firsts[k - 1].wait_recv()
        evolved = evolved + got[k].astype(F32)
    misfit = (inv * (evolved - obs)).astype(BF16)
    all_ref[me] = misfit
    seconds = [along(k, me) for k in range(1, count)]
    for copy in seconds:
        copy.start()
    if width == 2:
        seconds.append(across(0, me))
        seconds[-1].start()
    own_ref[...] = lax.dot_general(
        table, misfit, (((0,), (0,)), ((), ())), preferred_element_type=F32
    ).astype(BF16)
    lax.fori_loop(rounds // 2, rounds * 3 // 4, turn, 0)
    for k in range(1, count):
        along(k, at(k, low)).wait_recv()
        if width == 2:
            seconds.append(across(k, at(k, low)))
            seconds[-1].start()
    lax.fori_loop(rounds * 3 // 4, rounds, turn, 0)
    if width == 2:
        for k in range(count):
            across(k, at(k, 1 - low)).wait_recv()
    for copy in firsts + seconds:
        copy.wait_send()


def adjoint_kernel(index_ref, turned_ref, misfit_ref, own_ref, acc, misfit_out):
    products(index_ref, turned_ref, misfit_ref, acc, 2, 3)
    misfit_out[...] = own_ref[...]


def gradient_kernel(acc_ref, blend_ref, mix_ref, grad_ref, mine, away, got, send_sem, recv_sem):
    me = lax.axis_index("window")
    other = 1 - me
    slabs, cells, ens = grad_ref.shape
    slices = 2 * slabs
    blocks = cells // BLOCK
    barrier = pltpu.get_barrier_semaphore()
    pl.semaphore_signal(barrier, inc=1, device_id={"window": other}, device_id_type=MESH)
    high, low = spread(blend_ref[...], CELLS_AT_ONCE)
    mix = mix_ref[...]
    pl.semaphore_wait(barrier, 1)

    def send(block):
        return pltpu.make_async_remote_copy(
            src_ref=away.at[block],
            dst_ref=got.at[block],
            send_sem=send_sem.at[block],
            recv_sem=recv_sem.at[block],
            device_id={"window": other},
            device_id_type=MESH,
        )

    def pull(block):
        for within in range(BLOCK // (2 * CELLS_AT_ONCE)):
            sides = []
            for half in range(2):
                start = (2 * within + half) * CELLS_AT_ONCE
                rows = [acc_ref[t * blocks + block, pl.ds(start, CELLS_AT_ONCE), :] for t in range(slices)]
                sides.append(jnp.concatenate(rows, axis=0))
            rhs = jnp.concatenate(sides, axis=1)
            rhs_high = rhs.astype(BF16)
            rhs_low = (rhs - rhs_high.astype(F32)).astype(BF16)
            dims = (((0,), (0,)), ((), ()))
            out = lax.dot_general(high, rhs_high, dims, preferred_element_type=F32)
            out = out + lax.dot_general(low, rhs_high, dims, preferred_element_type=F32)
            out = (out + lax.dot_general(high, rhs_low, dims, preferred_element_type=F32)).astype(BF16)
            for half in range(2):
                start = (2 * within + half) * CELLS_AT_ONCE
                piece = out[:, half * ens : (half + 1) * ens].reshape(slices, CELLS_AT_ONCE, ens)
                first, second = piece[:slabs], piece[slabs:]
                mine[block, :, pl.ds(start, CELLS_AT_ONCE), :] = jnp.where(me == 0, first, second)
                away[block, :, pl.ds(start, CELLS_AT_ONCE), :] = jnp.where(me == 0, second, first)

    def finish(block):
        send(block).wait_recv()
        total = (mine[block].astype(F32) + got[block].astype(F32)).astype(BF16).reshape(slabs * BLOCK, ens)
        grad = jnp.dot(total, mix, preferred_element_type=F32).astype(BF16)
        grad_ref[:, pl.ds(block * BLOCK, BLOCK), :] = grad.reshape(slabs, BLOCK, ens)

    for block in range(blocks):
        pull(block)
        send(block).start()
        if block >= LAG:
            finish(block - LAG)
    for block in range(blocks - LAG, blocks):
        finish(block)
    for block in range(blocks):
        send(block).wait_send()


def vmem():
    return pl.BlockSpec(memory_space=pltpu.VMEM)


def hbm():
    return pl.BlockSpec(memory_space=pltpu.HBM)


def stay(x):
    return pltpu.with_memory_space_constraint(x, pltpu.HBM)


def shards(
    regions,
    flux,
    blend,
    footprints,
    receptor_block,
    cell_block,
    slice_index,
    live_counts,
    observed,
    inv_var,
    prior_mix,
):
    slabs, cells, ens = flux.shape
    slices = blend.shape[0]
    cell_blocks = cells // BLOCK
    panel_total = slices * cell_blocks
    slots = footprints.shape[1]
    rows = observed.shape[1]
    own_blocks = rows // BLOCK
    window_blocks = own_blocks * regions

    panels, pairs, index = pl.pallas_call(
        functools.partial(blend_kernel, window_blocks),
        out_shape=(
            jax.ShapeDtypeStruct((slices, cells, ens), BF16),
            jax.ShapeDtypeStruct((slots // 2, BLOCK, 2 * BLOCK), BF16),
            jax.ShapeDtypeStruct((4, slots), jnp.int32),
        ),
        in_specs=[hbm()] * 3 + [vmem()] + [hbm()] * 3,
        out_specs=(vmem(), vmem(), vmem()),
        scratch_shapes=[
            pltpu.VMEM((slices, cells, ens), BF16),
            pltpu.VMEM((slots, BLOCK * BLOCK), BF16),
            pltpu.VMEM((slices, slices), F32),
            pltpu.VMEM((1, slots), jnp.int32),
            pltpu.VMEM((1, slots), jnp.int32),
            pltpu.VMEM((1, slots), jnp.int32),
            pltpu.SemaphoreType.DMA((4,)),
            pltpu.SemaphoreType.DMA((LOADS,)),
            pltpu.SemaphoreType.DMA((PIECES,)),
            pltpu.SemaphoreType.DMA((PIECES,)),
            pltpu.SemaphoreType.DMA((PIECES,)),
        ],
        compiler_params=pltpu.CompilerParams(collective_id=0, has_side_effects=True, vmem_limit_bytes=24 << 20),
        name="blend_slices",
    )(
        stay(receptor_block),
        stay(cell_block),
        stay(slice_index),
        live_counts,
        stay(blend),
        stay(flux),
        stay(footprints),
    )

    smem = pl.BlockSpec(memory_space=pltpu.SMEM)
    part = pl.pallas_call(
        forward_kernel,
        out_shape=jax.ShapeDtypeStruct((window_blocks, BLOCK, ens), BF16),
        in_specs=[smem, vmem(), vmem()],
        out_specs=vmem(),
        scratch_shapes=[pltpu.VMEM((window_blocks + 1, BLOCK, ens), F32)],
        compiler_params=pltpu.CompilerParams(vmem_limit_bytes=16 << 20),
        name="forward_blocks",
    )(index, pairs, panels.reshape(panel_total, BLOCK, ens))

    misfit_all, own, turned = pl.pallas_call(
        functools.partial(exchange_kernel, regions),
        out_shape=(
            jax.ShapeDtypeStruct((regions, rows, ens), BF16),
            jax.ShapeDtypeStruct((rows, ens), BF16),
            jax.ShapeDtypeStruct((slots // 2, BLOCK, 2 * BLOCK), BF16),
        ),
        in_specs=[vmem()] * 4,
        out_specs=(vmem(), vmem(), vmem()),
        scratch_shapes=[
            pltpu.VMEM((regions, rows, ens), BF16),
            pltpu.SemaphoreType.DMA((regions,)),
            pltpu.SemaphoreType.DMA((regions,)),
            pltpu.SemaphoreType.DMA((regions,)),
            pltpu.SemaphoreType.DMA((regions,)),
            pltpu.SemaphoreType.DMA((regions,)),
            pltpu.SemaphoreType.DMA((regions,)),
        ],
        compiler_params=pltpu.CompilerParams(collective_id=1, has_side_effects=True, vmem_limit_bytes=16 << 20),
        name="misfit_exchange",
    )(part.reshape(regions, rows, ens), observed[0], inv_var, pairs)

    collected, misfit = pl.pallas_call(
        adjoint_kernel,
        out_shape=(
            jax.ShapeDtypeStruct((panel_total + 1, BLOCK, ens), F32),
            jax.ShapeDtypeStruct((rows, ens), BF16),
        ),
        in_specs=[smem, vmem(), vmem(), vmem()],
        out_specs=(vmem(), vmem()),
        compiler_params=pltpu.CompilerParams(vmem_limit_bytes=16 << 20),
        name="adjoint_blocks",
    )(index, turned, misfit_all.reshape(window_blocks, BLOCK, ens), own)

    blocks_shape = (cell_blocks, slabs, BLOCK, ens)
    gradient = pl.pallas_call(
        gradient_kernel,
        out_shape=jax.ShapeDtypeStruct((slabs, cells, ens), BF16),
        in_specs=[vmem(), vmem(), vmem()],
        out_specs=vmem(),
        scratch_shapes=[
            pltpu.VMEM(blocks_shape, BF16),
            pltpu.VMEM(blocks_shape, BF16),
            pltpu.VMEM(blocks_shape, BF16),
            pltpu.SemaphoreType.DMA((cell_blocks,)),
            pltpu.SemaphoreType.DMA((cell_blocks,)),
        ],
        compiler_params=pltpu.CompilerParams(collective_id=2, has_side_effects=True, vmem_limit_bytes=16 << 20),
        name="gradient_exchange",
    )(collected, blend, prior_mix)
    return misfit[None], gradient


def table_for(rows):
    row = lax.broadcasted_iota(jnp.int32, (rows, rows), 0)
    col = lax.broadcasted_iota(jnp.int32, (rows, rows), 1)
    inner = row % BLOCK
    return (row // BLOCK) * BLOCK + (inner % HALF) * 2 + inner // HALF == col


def spread_own_first(matrix, width, me, pulling):
    size = matrix.shape[0]
    full = size * width
    row = lax.broadcasted_iota(jnp.int32, (full, size), 0) // width
    col = lax.broadcasted_iota(jnp.int32, (full, size), 1)
    pick = (row == col).astype(BF16)
    pick_own = ((row + me * (size // 2)) % size == col).astype(BF16)
    row_f = lax.broadcasted_iota(jnp.int32, (full, full), 0)
    col_f = lax.broadcasted_iota(jnp.int32, (full, full), 1)
    same = row_f % width == col_f % width
    high = matrix.astype(BF16)
    low = (matrix - high.astype(F32)).astype(BF16)
    nt = (((1,), (1,)), ((), ()))
    parts = []
    for part in (high, low):
        if pulling:
            tall = lax.dot_general(pick_own, part, nt, preferred_element_type=F32).astype(BF16)
            wide = lax.dot_general(tall, pick, nt, preferred_element_type=F32)
        else:
            tall = jnp.dot(pick, part, preferred_element_type=F32).astype(BF16)
            wide = lax.dot_general(tall, pick_own, nt, preferred_element_type=F32)
        parts.append(jnp.where(same, wide, 0.0).astype(BF16))
    return parts


def slot_rows(raw, base):
    tiles = [raw[pl.ds(base, SUB), i * 2 * BLOCK : (i + 1) * 2 * BLOCK] for i in range(HALF)]
    return jnp.transpose(jnp.stack(tiles, axis=0), (1, 0, 2))


def place_kernel(
    window_blocks,
    cell_blocks,
    recv_hbm,
    cell_hbm,
    slice_hbm,
    live_ref,
    blend_hbm,
    flux_hbm,
    fp_hbm,
    dense_ref,
    spread_ref,
    flux_ref,
    raw,
    recv_ref,
    cell_ref,
    slice_ref,
    blend_ref,
    dest_ref,
    dest_smem,
    sums,
    small_sem,
    fp_sem,
    dest_sem,
):
    slots = raw.shape[0]
    total = dense_ref.shape[0] - 1
    panels = total // window_blocks
    smalls = [
        pltpu.make_async_copy(source, target, small_sem.at[k])
        for k, (source, target) in enumerate(
            (
                (recv_hbm, recv_ref),
                (cell_hbm, cell_ref),
                (slice_hbm, slice_ref),
                (blend_hbm, blend_ref),
            )
        )
    ]
    for copy in smalls:
        copy.start()
    part = slots // LOADS
    loads = []
    for k in range(LOADS):
        span = pl.ds(k * part, part)
        loads.append(pltpu.make_async_copy(fp_hbm.at[0, span, :], raw.at[span, :], fp_sem.at[k]))
        loads[-1].start()

    flux_copy = pltpu.make_async_copy(flux_hbm, flux_ref, dest_sem.at[1])
    flux_copy.start()

    def clear(g, carry):
        dense_ref[pl.ds(g * CLEAR, CLEAR)] = jnp.zeros((CLEAR,) + dense_ref.shape[1:], BF16)
        return carry

    lax.fori_loop(0, total // CLEAR // 2, clear, 0)
    dense_ref[total] = jnp.zeros(dense_ref.shape[1:], BF16)
    for copy in smalls:
        copy.wait()
    live = lax.broadcasted_iota(jnp.int32, recv_ref.shape, 1) < live_ref[0, 0]
    panel = slice_ref[...] * cell_blocks + cell_ref[...]
    dest_ref[...] = jnp.where(live, panel * window_blocks + recv_ref[...], total)
    index = pltpu.make_async_copy(dest_ref, dest_smem, dest_sem.at[0])
    index.start()
    high, low = spread_own_first(blend_ref[...], CELLS_AT_ONCE, lax.axis_index("window"), False)
    spread_ref[0] = high
    spread_ref[1] = low
    row = lax.broadcasted_iota(jnp.int32, (panels, slots), 0)
    named = (row == jnp.where(live, panel, -1)).astype(BF16)
    row = lax.broadcasted_iota(jnp.int32, (window_blocks, slots), 0)
    heard = (row == recv_ref[...]).astype(BF16)
    counts = lax.dot_general(named, heard, (((1,), (1,)), ((), ())), preferred_element_type=F32)
    most = jnp.max(counts)
    lax.fori_loop(total // CLEAR // 2, total // CLEAR, clear, 0)
    index.wait()
    flux_copy.wait()

    @pl.when(most <= MOST)
    def _():
        for k in range(LOADS):
            loads[k].wait()

            def body(g, carry):
                for sub in range(DENSE_SUBS):
                    base = pl.multiple_of(k * part + (g * DENSE_SUBS + sub) * SUB, SUB)
                    x = slot_rows(raw, base)
                    for j in range(0, SUB, 2):
                        one, two = dest_smem[0, base + j], dest_smem[0, base + j + 1]
                        first, second = dense_ref[one], dense_ref[two]
                        again = jnp.where(one == two, x[j], jnp.zeros_like(x[j]))
                        dense_ref[one] = first + x[j]
                        dense_ref[two] = second + again + x[j + 1]
                return carry

            lax.fori_loop(0, part // SUB // DENSE_SUBS, body, 0)

    @pl.when(most > MOST)
    def _():
        for k in range(LOADS):
            loads[k].wait()
        chunk = sums.shape[0] - 1

        def span(c, carry):
            sums[...] = jnp.zeros_like(sums)

            def body(g, carry):
                base = pl.multiple_of(g * SUB, SUB)
                x = slot_rows(raw, base)
                for j in range(SUB):
                    to = dest_smem[0, base + j] - c * chunk
                    to = jnp.where((to >= 0) & (to < chunk), to, chunk)
                    sums[to] += x[j].astype(F32)
                return carry

            lax.fori_loop(0, slots // SUB, body, 0)

            def store(g, carry):
                dense_ref[c * chunk + g] = sums[g].astype(BF16)
                return carry

            lax.fori_loop(0, chunk, store, 0)
            return carry

        lax.fori_loop(0, total // chunk, span, 0)


def final_kernel(grad_ref, last_ref, mix_ref, own_ref, grad_hbm, own_hbm, flat, sem):
    slabs, cells, ens = grad_ref.shape
    columns = last_ref.shape[2]
    early = cells - columns
    done = pltpu.make_async_copy(grad_ref.at[:, pl.ds(0, early), :], grad_hbm.at[:, pl.ds(0, early), :], sem.at[0])
    done.start()
    own = pltpu.make_async_copy(own_ref, own_hbm, sem.at[1])
    own.start()
    flat[...] = mixed(last_ref[...], mix_ref[...])
    rest = pltpu.make_async_copy(flat, grad_hbm.at[:, pl.ds(early, columns), :], sem.at[2])
    rest.start()
    done.wait()
    own.wait()
    rest.wait()


def mixed(total, mix):
    slabs, ens, columns = total.shape
    flat = jnp.concatenate([total[s].T for s in range(slabs)], axis=0)
    return jnp.dot(flat, mix, preferred_element_type=F32).astype(BF16).reshape(slabs, columns, ens)


def whole_kernel(
    regions,
    dense_ref,
    flux_ref,
    other_ref,
    spread_ref,
    obs_hbm,
    inv_hbm,
    mix_hbm,
    blend_hbm,
    own_ref,
    grad_ref,
    last_ref,
    mix_ref,
    obs_ref,
    inv_ref,
    blend_ref,
    panels,
    acc,
    part,
    got,
    all_ref,
    tiles,
    sums,
    back,
    mine,
    away,
    pulled,
    send_a,
    recv_a,
    send_b,
    recv_b,
    send_w,
    recv_w,
    small_sem,
):
    me = lax.axis_index("region")
    win = lax.axis_index("window")
    rows, ens = obs_ref.shape
    slabs, cells, _ = flux_ref.shape
    slices = 2 * slabs
    own_blocks = rows // BLOCK
    q_blocks = own_blocks * regions
    cell_blocks = cells // BLOCK
    panel_total = slices * cell_blocks

    barrier = pltpu.get_barrier_semaphore()
    for k in range(1, regions):
        peer = lax.rem(me + k, regions)
        pl.semaphore_signal(barrier, inc=1, device_id={"region": peer}, device_id_type=MESH)
    pl.semaphore_signal(barrier, inc=1, device_id={"window": 1 - win}, device_id_type=MESH)

    smalls = [
        pltpu.make_async_copy(source, target, small_sem.at[k])
        for k, (source, target) in enumerate(((obs_hbm, obs_ref), (inv_hbm, inv_ref), (mix_hbm, mix_ref), (blend_hbm, blend_ref)))
    ]
    for copy in smalls:
        copy.start()
    high, low = spread_ref[0], spread_ref[1]

    def group(g, carry):
        sides = []
        for half in range(2):
            start = pl.multiple_of((2 * g + half) * CELLS_AT_ONCE, CELLS_AT_ONCE)
            for ref in (flux_ref, other_ref):
                sides.append(ref[:, pl.ds(start, CELLS_AT_ONCE), :].reshape(slabs * CELLS_AT_ONCE, ens))
        rhs = jnp.concatenate(
            [jnp.concatenate(sides[:2], axis=0), jnp.concatenate(sides[2:], axis=0)], axis=1
        )
        out = jnp.dot(high, rhs, preferred_element_type=F32) + jnp.dot(low, rhs, preferred_element_type=F32)
        out = out.astype(BF16)
        for half in range(2):
            start = pl.multiple_of((2 * g + half) * CELLS_AT_ONCE, CELLS_AT_ONCE)
            panels[:, pl.ds(start, CELLS_AT_ONCE), :] = out[:, half * ens : (half + 1) * ens].reshape(
                slices, CELLS_AT_ONCE, ens
            )
        return carry

    lax.fori_loop(0, cells // (2 * CELLS_AT_ONCE), group, 0, unroll=4)

    group_size = regions // 2
    near = (me // group_size) * group_size
    far = group_size - near
    span = group_size * own_blocks

    def forward(first_region):
        acc[...] = jnp.zeros_like(acc)

        def body(g, carry):
            left, right = [], []
            for u in range(AT_ONCE):
                start = (g * AT_ONCE + u) * q_blocks + first_region * own_blocks
                left.append(dense_ref[pl.ds(start, span)].reshape(span * HALF, 2 * BLOCK))
                cell = (u % cell_blocks) * BLOCK
                one = panels[g * (AT_ONCE // cell_blocks) + u // cell_blocks, cell : cell + BLOCK, :]
                right.append(both(one, one))
            acc[...] += jnp.dot(
                jnp.concatenate(left, axis=1), jnp.concatenate(right, axis=0), preferred_element_type=F32
            )
            return carry

        lax.fori_loop(0, panel_total // AT_ONCE, body, 0)
        for q in range(span):
            for side in range(2):
                start = (q % own_blocks) * BLOCK + side * HALF
                part[first_region + q // own_blocks, start : start + HALF, :] = acc[
                    q * HALF : (q + 1) * HALF, side * ens : (side + 1) * ens
                ].astype(BF16)

    def reduce_copy(source, to):
        return pltpu.make_async_remote_copy(
            src_ref=part.at[to],
            dst_ref=got.at[source],
            send_sem=send_a.at[to],
            recv_sem=recv_a.at[source],
            device_id={"region": to},
            device_id_type=MESH,
        )

    def gather_copy(source, to):
        return pltpu.make_async_remote_copy(
            src_ref=all_ref.at[source],
            dst_ref=all_ref.at[source],
            send_sem=send_b.at[to],
            recv_sem=recv_b.at[source],
            device_id={"region": to},
            device_id_type=MESH,
        )

    fars = [far + (me - near + k) % group_size for k in range(group_size)]
    nears = [near + (me - near + k) % group_size for k in range(1, group_size)]

    forward(far)
    pl.semaphore_wait(barrier, regions)
    for peer in fars:
        reduce_copy(me, peer).start()
    forward(near)
    for peer in nears:
        reduce_copy(me, peer).start()

    lower = lax.broadcasted_iota(jnp.int32, (HALF, 2 * BLOCK), 1) < BLOCK

    def pair_up(g, carry):
        for k in range(2):
            for q in range(q_blocks):
                one = dense_ref[(4 * g + 2 * k) * q_blocks + q]
                two = dense_ref[(4 * g + 2 * k + 1) * q_blocks + q]
                swapped = halves_swapped(jnp.where(lower, two, one))
                tiles[2 * g + k, pl.ds(q * BLOCK, HALF), :] = jnp.where(lower, one, swapped)
                tiles[2 * g + k, pl.ds(q * BLOCK + HALF, HALF), :] = jnp.where(lower, swapped, two)
        return carry

    for copy in smalls:
        copy.wait()
    table = table_for(rows)
    obs = jnp.dot(table.astype(BF16), obs_ref[...], preferred_element_type=F32)
    inv = jnp.sum(jnp.where(table, inv_ref[...], 0.0), axis=1, keepdims=True)
    rounds = panel_total // 4
    lax.fori_loop(0, rounds // 2, pair_up, 0)

    evolved = part[me].astype(F32)
    for peer in nears + fars:
        reduce_copy(peer, me).wait_recv()
        evolved = evolved + got[peer].astype(F32)
    misfit = (inv * (evolved - obs)).astype(BF16)
    all_ref[me] = misfit.T
    for peer in fars + nears:
        gather_copy(me, peer).start()
    own_ref[...] = lax.dot_general(
        table.astype(BF16), misfit, (((0,), (0,)), ((), ())), preferred_element_type=F32
    ).astype(BF16)
    lax.fori_loop(rounds // 2, rounds, pair_up, 0)
    pull_high, pull_low = spread_own_first(blend_ref[...], CELLS_AT_ONCE, win, True)

    mix = mix_ref[...]
    columns = 2 * BLOCK
    steps = cells // columns

    def send(step):
        return pltpu.make_async_remote_copy(
            src_ref=away.at[step],
            dst_ref=pulled.at[step],
            send_sem=send_w.at[step],
            recv_sem=recv_w.at[step],
            device_id={"window": 1 - win},
            device_id_type=MESH,
        )

    def product(step, half, first_region, turned):
        right = [
            tiles[(half * slabs + t) * steps + step, pl.ds(first_region * rows, group_size * rows), :]
            for t in range(slabs)
        ]
        return jnp.dot(turned, jnp.concatenate(right, axis=1), preferred_element_type=F32)

    for peer in nears:
        gather_copy(peer, me).wait_recv()
    turned_near = jnp.concatenate([all_ref[near + k] for k in range(group_size)], axis=1)
    for step in range(steps):
        for half in range(2):
            sums[step, half] = product(step, half, near, turned_near)
    for peer in fars:
        gather_copy(peer, me).wait_recv()
    turned_far = jnp.concatenate([all_ref[far + k] for k in range(group_size)], axis=1)

    def adjoint(step):
        for half in range(2):
            out = (sums[step, half] + product(step, half, far, turned_far)).astype(BF16)
            for t in range(slabs):
                back[half * slabs + t] = out[:, t * columns : (t + 1) * columns]
        for e in range(0, ens, 2 * CELLS_AT_ONCE):
            rhs = jnp.concatenate(
                [
                    back[:, e + h * CELLS_AT_ONCE : e + (h + 1) * CELLS_AT_ONCE, :].reshape(
                        slices * CELLS_AT_ONCE, columns
                    )
                    for h in range(2)
                ],
                axis=1,
            )
            out = jnp.dot(pull_high, rhs, preferred_element_type=F32)
            out = (out + jnp.dot(pull_low, rhs, preferred_element_type=F32)).astype(BF16)
            for h in range(2):
                piece = out[:, h * columns : (h + 1) * columns].reshape(slices, CELLS_AT_ONCE, columns)
                at_e = e + h * CELLS_AT_ONCE
                mine[step, :, at_e : at_e + CELLS_AT_ONCE, :] = piece[:slabs]
                away[step, :, at_e : at_e + CELLS_AT_ONCE, :] = piece[slabs:]

    def finish(step):
        send(step).wait_recv()
        total = (mine[step].astype(F32) + pulled[step].astype(F32)).astype(BF16)
        if step == steps - 1:
            last_ref[...] = total
        else:
            grad_ref[:, step * columns : (step + 1) * columns, :] = mixed(total, mix)

    for step in range(steps):
        adjoint(step)
        send(step).start()
        if step >= DENSE_LAG:
            finish(step - DENSE_LAG)
    for step in range(steps - DENSE_LAG, steps):
        finish(step)
    for step in range(steps):
        send(step).wait_send()
    for peer in nears + fars:
        reduce_copy(me, peer).wait_send()
        gather_copy(me, peer).wait_send()


def dense_shards(
    regions,
    flux,
    blend,
    footprints,
    receptor_block,
    cell_block,
    slice_index,
    live_counts,
    observed,
    inv_var,
    prior_mix,
):
    slabs, cells, ens = flux.shape
    slices = blend.shape[0]
    cell_blocks = cells // BLOCK
    panel_total = slices * cell_blocks
    slots = footprints.shape[1]
    rows = observed.shape[1]
    window_blocks = rows // BLOCK * regions
    total = panel_total * window_blocks
    columns = 2 * BLOCK
    steps = cells // columns

    other = lax.ppermute(flux, "window", [(0, 1), (1, 0)])
    dense, kernels, near_flux = pl.pallas_call(
        functools.partial(place_kernel, window_blocks, cell_blocks),
        out_shape=(
            jax.ShapeDtypeStruct((total + 1, HALF, 2 * BLOCK), BF16),
            jax.ShapeDtypeStruct((2, slices * CELLS_AT_ONCE, slices * CELLS_AT_ONCE), BF16),
            jax.ShapeDtypeStruct((slabs, cells, ens), BF16),
        ),
        in_specs=[hbm()] * 3 + [pl.BlockSpec(memory_space=pltpu.SMEM)] + [hbm()] * 3,
        out_specs=(vmem(), vmem(), vmem()),
        scratch_shapes=[
            pltpu.VMEM((slots, BLOCK * BLOCK), BF16),
            pltpu.VMEM((1, slots), jnp.int32),
            pltpu.VMEM((1, slots), jnp.int32),
            pltpu.VMEM((1, slots), jnp.int32),
            pltpu.VMEM((slices, slices), F32),
            pltpu.VMEM((1, slots), jnp.int32),
            pltpu.SMEM((1, slots), jnp.int32),
            pltpu.VMEM((total // 8 + 1, HALF, 2 * BLOCK), F32),
            pltpu.SemaphoreType.DMA((4,)),
            pltpu.SemaphoreType.DMA((LOADS,)),
            pltpu.SemaphoreType.DMA((2,)),
        ],
        compiler_params=pltpu.CompilerParams(vmem_limit_bytes=DENSE_VMEM),
        cost_estimate=pl.CostEstimate(flops=0, bytes_accessed=24 << 20, transcendentals=0),
        name="place_blocks",
    )(stay(receptor_block), stay(cell_block), stay(slice_index), live_counts, stay(blend), stay(flux), stay(footprints))

    misfit, gradient, last, mix = pl.pallas_call(
        functools.partial(whole_kernel, regions),
        out_shape=(
            jax.ShapeDtypeStruct((rows, ens), BF16),
            jax.ShapeDtypeStruct((slabs, cells, ens), BF16),
            jax.ShapeDtypeStruct((slabs, ens, columns), BF16),
            jax.ShapeDtypeStruct(prior_mix.shape, BF16),
        ),
        in_specs=[vmem()] * 4 + [hbm()] * 4,
        out_specs=(vmem(), vmem(), vmem(), vmem()),
        scratch_shapes=[
            pltpu.VMEM((rows, ens), BF16),
            pltpu.VMEM((1, rows), F32),
            pltpu.VMEM((slices, slices), F32),
            pltpu.VMEM((slices, cells, ens), BF16),
            pltpu.VMEM((window_blocks // 2 * HALF, 2 * ens), F32),
            pltpu.VMEM((regions, rows, ens), BF16),
            pltpu.VMEM((regions, rows, ens), BF16),
            pltpu.VMEM((regions, ens, rows), BF16),
            pltpu.VMEM((panel_total // 2, window_blocks * BLOCK, columns), BF16),
            pltpu.VMEM((steps, 2, ens, slabs * columns), F32),
            pltpu.VMEM((slices, ens, columns), BF16),
            pltpu.VMEM((steps, slabs, ens, columns), BF16),
            pltpu.VMEM((steps, slabs, ens, columns), BF16),
            pltpu.VMEM((steps, slabs, ens, columns), BF16),
        ]
        + [pltpu.SemaphoreType.DMA((regions,))] * 4
        + [pltpu.SemaphoreType.DMA((steps,))] * 2
        + [pltpu.SemaphoreType.DMA((4,))],
        compiler_params=pltpu.CompilerParams(collective_id=3, has_side_effects=True, vmem_limit_bytes=DENSE_VMEM),
        name="transport",
    )(dense, near_flux, other, kernels, stay(observed[0]), stay(inv_var), stay(prior_mix), stay(blend))

    gradient, misfit = pl.pallas_call(
        final_kernel,
        out_shape=(
            jax.ShapeDtypeStruct((slabs, cells, ens), BF16),
            jax.ShapeDtypeStruct((rows, ens), BF16),
        ),
        in_specs=[vmem()] * 4,
        out_specs=(hbm(), hbm()),
        scratch_shapes=[pltpu.VMEM((slabs, columns, ens), BF16), pltpu.SemaphoreType.DMA((3,))],
        compiler_params=pltpu.CompilerParams(vmem_limit_bytes=4 << 20),
        name="final_mix",
    )(gradient, last, mix, misfit)
    return misfit[None], gradient


def solution(mesh):
    in_specs = (
        P(("group", "window"), "region", None),
        P(),
        P(("group", "window"), "region", None),
        P(("group", "window"), "region"),
        P(("group", "window"), "region"),
        P(("group", "window"), "region"),
        P(("group", "window"), "region"),
        P(("group", "window"), "region", None),
        P(("group", "window"), "region"),
        P(),
    )
    out_specs = (P(("group", "window"), "region", None), P(("group", "window"), "region", None))

    def either(*args):
        regions = mesh.shape["region"]
        blocks = args[7].shape[1] // BLOCK * regions
        return (dense_shards if blocks <= DENSE_BLOCKS and regions % 2 == 0 else shards)(regions, *args)

    return jax.shard_map(
        either,
        mesh=mesh,
        in_specs=in_specs,
        out_specs=out_specs,
        check_vma=False,
    )
```

```python
import functools

import jax
import jax.numpy as jnp
from jax import lax
from jax.experimental import pallas as pl
from jax.experimental.pallas import tpu as pltpu
from jax.sharding import PartitionSpec as P

BLOCK = 64
MESH = pl.DeviceIdType.MESH
F32 = jnp.float32
BF16 = jnp.bfloat16
SUB = 16
SUBS = 4
CELLS_AT_ONCE = 16
PIECES = 4
LOADS = 8
PAIRS = 32
TURNS = 32
LAG = 2
HALF = BLOCK // 2
CLEAR = 32
MOST = 16
DENSE_SUBS = 4
AT_ONCE = 32
DENSE_LAG = 3
DENSE_VMEM = 33 << 20
DENSE_BLOCKS = 16


def spread(matrix, width):
    size = matrix.shape[0]
    full = size * width
    row = lax.broadcasted_iota(jnp.int32, (full, size), 0)
    col = lax.broadcasted_iota(jnp.int32, (full, size), 1)
    pick = (row // width == col).astype(BF16)
    row_f = lax.broadcasted_iota(jnp.int32, (full, full), 0)
    col_f = lax.broadcasted_iota(jnp.int32, (full, full), 1)
    same = row_f % width == col_f % width
    high = matrix.astype(BF16)
    low = (matrix - high.astype(F32)).astype(BF16)
    parts = []
    for part in (high, low):
        tall = jnp.dot(pick, part, preferred_element_type=F32).astype(BF16)
        wide = lax.dot_general(tall, pick, (((1,), (1,)), ((), ())), preferred_element_type=F32)
        parts.append(jnp.where(same, wide, 0.0).astype(BF16))
    return parts


def halves_swapped(x):
    return pltpu.roll(x, BLOCK, 1)


def blend_kernel(
    window_blocks,
    recv_hbm,
    cell_hbm,
    slice_hbm,
    live_ref,
    blend_hbm,
    flux_hbm,
    fp_hbm,
    panels_ref,
    pairs_ref,
    index_ref,
    full,
    raw,
    blend_ref,
    recv_ref,
    cell_ref,
    slice_ref,
    small_sem,
    fp_sem,
    local_sem,
    send_sem,
    recv_sem,
):
    me = lax.axis_index("window")
    other = 1 - me
    slabs, cells, ens = flux_hbm.shape
    slices = panels_ref.shape[0]
    slots = raw.shape[0]
    barrier = pltpu.get_barrier_semaphore()
    pl.semaphore_signal(barrier, inc=1, device_id={"window": other}, device_id_type=MESH)
    smalls = [
        pltpu.make_async_copy(source, target, small_sem.at[k])
        for k, (source, target) in enumerate(
            ((blend_hbm, blend_ref), (recv_hbm, recv_ref), (cell_hbm, cell_ref), (slice_hbm, slice_ref))
        )
    ]
    for copy in smalls:
        copy.start()
    piece = cells // PIECES
    locals_, sends, loads = [], [], []
    for k in range(PIECES):
        span = pl.ds(k * piece, piece)
        locals_.append(
            pltpu.make_async_copy(
                flux_hbm.at[:, span, :], full.at[pl.ds(me * slabs, slabs), span, :], local_sem.at[k]
            )
        )
        locals_[-1].start()
    part = slots // LOADS
    for k in range(LOADS):
        span = pl.ds(k * part, part)
        loads.append(pltpu.make_async_copy(fp_hbm.at[0, span, :], raw.at[span, :], fp_sem.at[k]))
    loads[0].start()
    pl.semaphore_wait(barrier, 1)
    for k in range(PIECES):
        span = pl.ds(k * piece, piece)
        sends.append(
            pltpu.make_async_remote_copy(
                src_ref=flux_hbm.at[:, span, :],
                dst_ref=full.at[pl.ds(me * slabs, slabs), span, :],
                send_sem=send_sem.at[k],
                recv_sem=recv_sem.at[k],
                device_id={"window": other},
                device_id_type=MESH,
            )
        )
        sends[-1].start()
    for k in range(1, LOADS):
        loads[k].start()

    for copy in smalls:
        copy.wait()
    cell_blocks = cells // BLOCK
    live = lax.broadcasted_iota(jnp.int32, recv_ref.shape, 1) < live_ref[...]
    panel = slice_ref[...] * cell_blocks + cell_ref[...]
    index_ref[pl.ds(0, 1), :] = jnp.where(live, recv_ref[...], window_blocks)
    index_ref[pl.ds(1, 1), :] = jnp.where(live, panel, 0)
    index_ref[pl.ds(2, 1), :] = jnp.where(live, panel, slices * cell_blocks)
    index_ref[pl.ds(3, 1), :] = jnp.where(live, recv_ref[...], 0)
    high, low = spread(blend_ref[...], CELLS_AT_ONCE)

    def arrange(k):
        loads[k].wait()

        def body(g, carry):
            lower = lax.broadcasted_iota(jnp.int32, (BLOCK // 2, 2 * BLOCK), 1) < BLOCK
            for sub in range(SUBS):
                base = pl.multiple_of(k * part + g * SUBS * SUB + sub * SUB, SUB)
                x = raw[pl.ds(base, SUB), :].reshape(SUB, BLOCK // 2, 2 * BLOCK)
                for j in range(0, SUB, 2):
                    one, two = x[j], x[j + 1]
                    even = jnp.where(lower, one, halves_swapped(two))
                    odd = jnp.where(lower, halves_swapped(one), two)
                    place = k * (part // 2) + (g * SUBS + sub) * (SUB // 2) + j // 2
                    pairs_ref[place] = jnp.concatenate([even, odd], axis=0)
            return carry

        lax.fori_loop(0, part // SUB // SUBS, body, 0)

    for k in range(LOADS // 2):
        arrange(k)
    for k in range(PIECES):
        locals_[k].wait()
        sends[k].wait_recv()

        def group(g, carry, k=k):
            sides = []
            for half in range(2):
                start = pl.multiple_of(k * piece + g * 2 * CELLS_AT_ONCE + half * CELLS_AT_ONCE, CELLS_AT_ONCE)
                sides.append(full[:, pl.ds(start, CELLS_AT_ONCE), :].reshape(slices * CELLS_AT_ONCE, ens))
            rhs = jnp.concatenate(sides, axis=1)
            out = jnp.dot(high, rhs, preferred_element_type=F32) + jnp.dot(low, rhs, preferred_element_type=F32)
            out = out.astype(BF16)
            for half in range(2):
                start = pl.multiple_of(k * piece + g * 2 * CELLS_AT_ONCE + half * CELLS_AT_ONCE, CELLS_AT_ONCE)
                panels_ref[:, pl.ds(start, CELLS_AT_ONCE), :] = out[:, half * ens : (half + 1) * ens].reshape(
                    slices, CELLS_AT_ONCE, ens
                )
            return carry

        lax.fori_loop(0, piece // (2 * CELLS_AT_ONCE), group, 0, unroll=2)
    for k in range(LOADS // 2, LOADS):
        arrange(k)
    for k in range(PIECES):
        sends[k].wait_send()


def both(one, two):
    zero = jnp.zeros_like(one)
    return jnp.concatenate(
        [jnp.concatenate([one, zero], axis=1), jnp.concatenate([zero, two], axis=1)], axis=0
    )


def products(index_ref, left_ref, right_ref, acc, to, source):
    acc[...] = jnp.zeros_like(acc)
    ens = acc.shape[2]

    def body(g, carry):
        for j in range(PAIRS):
            pair = g * PAIRS + j
            one = right_ref[index_ref[source, 2 * pair]]
            two = right_ref[index_ref[source, 2 * pair + 1]]
            out = jnp.dot(left_ref[pair], both(one, two), preferred_element_type=F32)
            acc[index_ref[to, 2 * pair]] += out[:, :ens]
            acc[index_ref[to, 2 * pair + 1]] += out[:, ens:]
        return carry

    lax.fori_loop(0, left_ref.shape[0] // PAIRS, body, 0)


def forward_kernel(index_ref, pairs_ref, panels_ref, part_ref, acc):
    products(index_ref, pairs_ref, panels_ref, acc, 0, 1)
    part_ref[...] = acc[pl.ds(0, part_ref.shape[0])].astype(BF16)


def turned_pair(x):
    t = x.T
    return jnp.concatenate([t[:BLOCK], t[BLOCK:]], axis=1)


def exchange_kernel(
    regions, part_ref, obs_ref, inv_ref, pairs_ref, all_ref, own_ref, turned_ref, got, send_a, recv_a, send_b, recv_b, send_c, recv_c
):
    me = lax.axis_index("region")
    rows, ens = obs_ref.shape
    barrier = pltpu.get_barrier_semaphore()
    for k in range(1, regions):
        peer = lax.rem(me + k, regions)
        pl.semaphore_signal(barrier, inc=1, device_id={"region": peer}, device_id_type=MESH)
    row = lax.broadcasted_iota(jnp.int32, (rows, rows), 0)
    col = lax.broadcasted_iota(jnp.int32, (rows, rows), 1)
    inner = row % BLOCK
    half = BLOCK // 2
    picked = (row // BLOCK) * BLOCK + (inner % half) * 2 + inner // half == col
    table = picked.astype(BF16)
    obs = jnp.dot(table, obs_ref[...], preferred_element_type=F32)
    inv = jnp.sum(jnp.where(picked, inv_ref[...], 0.0), axis=1, keepdims=True)
    pl.semaphore_wait(barrier, regions - 1)

    def first(k):
        peer = lax.rem(me + k, regions)
        return pltpu.make_async_remote_copy(
            src_ref=part_ref.at[peer],
            dst_ref=got.at[k],
            send_sem=send_a.at[k],
            recv_sem=recv_a.at[k],
            device_id={"region": peer},
            device_id_type=MESH,
        )

    width = 2 if regions % 2 == 0 else 1
    count = regions // width
    high, low = me // width, lax.rem(me, width)

    def at(k, low):
        return lax.rem(high + count - k, count) * width + low

    def along(k, source):
        return pltpu.make_async_remote_copy(
            src_ref=all_ref.at[source],
            dst_ref=all_ref.at[source],
            send_sem=send_b.at[k],
            recv_sem=recv_b.at[k],
            device_id={"region": lax.rem(high + k, count) * width + low},
            device_id_type=MESH,
        )

    def across(k, source):
        return pltpu.make_async_remote_copy(
            src_ref=all_ref.at[source],
            dst_ref=all_ref.at[source],
            send_sem=send_c.at[k],
            recv_sem=recv_c.at[k],
            device_id={"region": high * width + 1 - low},
            device_id_type=MESH,
        )

    firsts = [first(k) for k in range(1, regions)]
    for copy in firsts:
        copy.start()

    pair_count = pairs_ref.shape[0]

    def turn(g, carry):
        for j in range(TURNS):
            turned_ref[g * TURNS + j] = turned_pair(pairs_ref[g * TURNS + j])
        return carry

    rounds = pair_count // TURNS
    lax.fori_loop(0, rounds // 2, turn, 0)
    evolved = part_ref[me].astype(F32)
    for k in range(1, regions):
        firsts[k - 1].wait_recv()
        evolved = evolved + got[k].astype(F32)
    misfit = (inv * (evolved - obs)).astype(BF16)
    all_ref[me] = misfit
    seconds = [along(k, me) for k in range(1, count)]
    for copy in seconds:
        copy.start()
    if width == 2:
        seconds.append(across(0, me))
        seconds[-1].start()
    own_ref[...] = lax.dot_general(
        table, misfit, (((0,), (0,)), ((), ())), preferred_element_type=F32
    ).astype(BF16)
    lax.fori_loop(rounds // 2, rounds * 3 // 4, turn, 0)
    for k in range(1, count):
        along(k, at(k, low)).wait_recv()
        if width == 2:
            seconds.append(across(k, at(k, low)))
            seconds[-1].start()
    lax.fori_loop(rounds * 3 // 4, rounds, turn, 0)
    if width == 2:
        for k in range(count):
            across(k, at(k, 1 - low)).wait_recv()
    for copy in firsts + seconds:
        copy.wait_send()


def adjoint_kernel(index_ref, turned_ref, misfit_ref, own_ref, acc, misfit_out):
    products(index_ref, turned_ref, misfit_ref, acc, 2, 3)
    misfit_out[...] = own_ref[...]


def gradient_kernel(acc_ref, blend_ref, mix_ref, grad_ref, mine, away, got, send_sem, recv_sem):
    me = lax.axis_index("window")
    other = 1 - me
    slabs, cells, ens = grad_ref.shape
    slices = 2 * slabs
    blocks = cells // BLOCK
    barrier = pltpu.get_barrier_semaphore()
    pl.semaphore_signal(barrier, inc=1, device_id={"window": other}, device_id_type=MESH)
    high, low = spread(blend_ref[...], CELLS_AT_ONCE)
    mix = mix_ref[...]
    pl.semaphore_wait(barrier, 1)

    def send(block):
        return pltpu.make_async_remote_copy(
            src_ref=away.at[block],
            dst_ref=got.at[block],
            send_sem=send_sem.at[block],
            recv_sem=recv_sem.at[block],
            device_id={"window": other},
            device_id_type=MESH,
        )

    def pull(block):
        for within in range(BLOCK // (2 * CELLS_AT_ONCE)):
            sides = []
            for half in range(2):
                start = (2 * within + half) * CELLS_AT_ONCE
                rows = [acc_ref[t * blocks + block, pl.ds(start, CELLS_AT_ONCE), :] for t in range(slices)]
                sides.append(jnp.concatenate(rows, axis=0))
            rhs = jnp.concatenate(sides, axis=1)
            rhs_high = rhs.astype(BF16)
            rhs_low = (rhs - rhs_high.astype(F32)).astype(BF16)
            dims = (((0,), (0,)), ((), ()))
            out = lax.dot_general(high, rhs_high, dims, preferred_element_type=F32)
            out = out + lax.dot_general(low, rhs_high, dims, preferred_element_type=F32)
            out = (out + lax.dot_general(high, rhs_low, dims, preferred_element_type=F32)).astype(BF16)
            for half in range(2):
                start = (2 * within + half) * CELLS_AT_ONCE
                piece = out[:, half * ens : (half + 1) * ens].reshape(slices, CELLS_AT_ONCE, ens)
                first, second = piece[:slabs], piece[slabs:]
                mine[block, :, pl.ds(start, CELLS_AT_ONCE), :] = jnp.where(me == 0, first, second)
                away[block, :, pl.ds(start, CELLS_AT_ONCE), :] = jnp.where(me == 0, second, first)

    def finish(block):
        send(block).wait_recv()
        total = (mine[block].astype(F32) + got[block].astype(F32)).astype(BF16).reshape(slabs * BLOCK, ens)
        grad = jnp.dot(total, mix, preferred_element_type=F32).astype(BF16)
        grad_ref[:, pl.ds(block * BLOCK, BLOCK), :] = grad.reshape(slabs, BLOCK, ens)

    for block in range(blocks):
        pull(block)
        send(block).start()
        if block >= LAG:
            finish(block - LAG)
    for block in range(blocks - LAG, blocks):
        finish(block)
    for block in range(blocks):
        send(block).wait_send()


def vmem():
    return pl.BlockSpec(memory_space=pltpu.VMEM)


def hbm():
    return pl.BlockSpec(memory_space=pltpu.HBM)


def stay(x):
    return pltpu.with_memory_space_constraint(x, pltpu.HBM)


def shards(
    regions,
    flux,
    blend,
    footprints,
    receptor_block,
    cell_block,
    slice_index,
    live_counts,
    observed,
    inv_var,
    prior_mix,
):
    slabs, cells, ens = flux.shape
    slices = blend.shape[0]
    cell_blocks = cells // BLOCK
    panel_total = slices * cell_blocks
    slots = footprints.shape[1]
    rows = observed.shape[1]
    own_blocks = rows // BLOCK
    window_blocks = own_blocks * regions

    panels, pairs, index = pl.pallas_call(
        functools.partial(blend_kernel, window_blocks),
        out_shape=(
            jax.ShapeDtypeStruct((slices, cells, ens), BF16),
            jax.ShapeDtypeStruct((slots // 2, BLOCK, 2 * BLOCK), BF16),
            jax.ShapeDtypeStruct((4, slots), jnp.int32),
        ),
        in_specs=[hbm()] * 3 + [vmem()] + [hbm()] * 3,
        out_specs=(vmem(), vmem(), vmem()),
        scratch_shapes=[
            pltpu.VMEM((slices, cells, ens), BF16),
            pltpu.VMEM((slots, BLOCK * BLOCK), BF16),
            pltpu.VMEM((slices, slices), F32),
            pltpu.VMEM((1, slots), jnp.int32),
            pltpu.VMEM((1, slots), jnp.int32),
            pltpu.VMEM((1, slots), jnp.int32),
            pltpu.SemaphoreType.DMA((4,)),
            pltpu.SemaphoreType.DMA((LOADS,)),
            pltpu.SemaphoreType.DMA((PIECES,)),
            pltpu.SemaphoreType.DMA((PIECES,)),
            pltpu.SemaphoreType.DMA((PIECES,)),
        ],
        compiler_params=pltpu.CompilerParams(collective_id=0, has_side_effects=True, vmem_limit_bytes=24 << 20),
        name="blend_slices",
    )(
        stay(receptor_block),
        stay(cell_block),
        stay(slice_index),
        live_counts,
        stay(blend),
        stay(flux),
        stay(footprints),
    )

    smem = pl.BlockSpec(memory_space=pltpu.SMEM)
    part = pl.pallas_call(
        forward_kernel,
        out_shape=jax.ShapeDtypeStruct((window_blocks, BLOCK, ens), BF16),
        in_specs=[smem, vmem(), vmem()],
        out_specs=vmem(),
        scratch_shapes=[pltpu.VMEM((window_blocks + 1, BLOCK, ens), F32)],
        compiler_params=pltpu.CompilerParams(vmem_limit_bytes=16 << 20),
        name="forward_blocks",
    )(index, pairs, panels.reshape(panel_total, BLOCK, ens))

    misfit_all, own, turned = pl.pallas_call(
        functools.partial(exchange_kernel, regions),
        out_shape=(
            jax.ShapeDtypeStruct((regions, rows, ens), BF16),
            jax.ShapeDtypeStruct((rows, ens), BF16),
            jax.ShapeDtypeStruct((slots // 2, BLOCK, 2 * BLOCK), BF16),
        ),
        in_specs=[vmem()] * 4,
        out_specs=(vmem(), vmem(), vmem()),
        scratch_shapes=[
            pltpu.VMEM((regions, rows, ens), BF16),
            pltpu.SemaphoreType.DMA((regions,)),
            pltpu.SemaphoreType.DMA((regions,)),
            pltpu.SemaphoreType.DMA((regions,)),
            pltpu.SemaphoreType.DMA((regions,)),
            pltpu.SemaphoreType.DMA((regions,)),
            pltpu.SemaphoreType.DMA((regions,)),
        ],
        compiler_params=pltpu.CompilerParams(collective_id=1, has_side_effects=True, vmem_limit_bytes=16 << 20),
        name="misfit_exchange",
    )(part.reshape(regions, rows, ens), observed[0], inv_var, pairs)

    collected, misfit = pl.pallas_call(
        adjoint_kernel,
        out_shape=(
            jax.ShapeDtypeStruct((panel_total + 1, BLOCK, ens), F32),
            jax.ShapeDtypeStruct((rows, ens), BF16),
        ),
        in_specs=[smem, vmem(), vmem(), vmem()],
        out_specs=(vmem(), vmem()),
        compiler_params=pltpu.CompilerParams(vmem_limit_bytes=16 << 20),
        name="adjoint_blocks",
    )(index, turned, misfit_all.reshape(window_blocks, BLOCK, ens), own)

    blocks_shape = (cell_blocks, slabs, BLOCK, ens)
    gradient = pl.pallas_call(
        gradient_kernel,
        out_shape=jax.ShapeDtypeStruct((slabs, cells, ens), BF16),
        in_specs=[vmem(), vmem(), vmem()],
        out_specs=vmem(),
        scratch_shapes=[
            pltpu.VMEM(blocks_shape, BF16),
            pltpu.VMEM(blocks_shape, BF16),
            pltpu.VMEM(blocks_shape, BF16),
            pltpu.SemaphoreType.DMA((cell_blocks,)),
            pltpu.SemaphoreType.DMA((cell_blocks,)),
        ],
        compiler_params=pltpu.CompilerParams(collective_id=2, has_side_effects=True, vmem_limit_bytes=16 << 20),
        name="gradient_exchange",
    )(collected, blend, prior_mix)
    return misfit[None], gradient


def table_for(rows):
    row = lax.broadcasted_iota(jnp.int32, (rows, rows), 0)
    col = lax.broadcasted_iota(jnp.int32, (rows, rows), 1)
    inner = row % BLOCK
    return (row // BLOCK) * BLOCK + (inner % HALF) * 2 + inner // HALF == col


def spread_own_first(matrix, width, me, pulling):
    size = matrix.shape[0]
    full = size * width
    row = lax.broadcasted_iota(jnp.int32, (full, size), 0) // width
    col = lax.broadcasted_iota(jnp.int32, (full, size), 1)
    pick = (row == col).astype(BF16)
    pick_own = ((row + me * (size // 2)) % size == col).astype(BF16)
    row_f = lax.broadcasted_iota(jnp.int32, (full, full), 0)
    col_f = lax.broadcasted_iota(jnp.int32, (full, full), 1)
    same = row_f % width == col_f % width
    high = matrix.astype(BF16)
    low = (matrix - high.astype(F32)).astype(BF16)
    nt = (((1,), (1,)), ((), ()))
    parts = []
    for part in (high, low):
        if pulling:
            tall = lax.dot_general(pick_own, part, nt, preferred_element_type=F32).astype(BF16)
            wide = lax.dot_general(tall, pick, nt, preferred_element_type=F32)
        else:
            tall = jnp.dot(pick, part, preferred_element_type=F32).astype(BF16)
            wide = lax.dot_general(tall, pick_own, nt, preferred_element_type=F32)
        parts.append(jnp.where(same, wide, 0.0).astype(BF16))
    return parts


def slot_rows(raw, base):
    tiles = [raw[pl.ds(base, SUB), i * 2 * BLOCK : (i + 1) * 2 * BLOCK] for i in range(HALF)]
    return jnp.transpose(jnp.stack(tiles, axis=0), (1, 0, 2))


def place_kernel(
    window_blocks,
    cell_blocks,
    recv_hbm,
    cell_hbm,
    slice_hbm,
    live_ref,
    blend_hbm,
    flux_hbm,
    fp_hbm,
    dense_ref,
    spread_ref,
    flux_ref,
    raw,
    recv_ref,
    cell_ref,
    slice_ref,
    blend_ref,
    dest_ref,
    dest_smem,
    sums,
    small_sem,
    fp_sem,
    dest_sem,
):
    slots = raw.shape[0]
    total = dense_ref.shape[0] - 1
    panels = total // window_blocks
    smalls = [
        pltpu.make_async_copy(source, target, small_sem.at[k])
        for k, (source, target) in enumerate(
            (
                (recv_hbm, recv_ref),
                (cell_hbm, cell_ref),
                (slice_hbm, slice_ref),
                (blend_hbm, blend_ref),
            )
        )
    ]
    for copy in smalls:
        copy.start()
    part = slots // LOADS
    loads = []
    for k in range(LOADS):
        span = pl.ds(k * part, part)
        loads.append(pltpu.make_async_copy(fp_hbm.at[0, span, :], raw.at[span, :], fp_sem.at[k]))
        loads[-1].start()

    flux_copy = pltpu.make_async_copy(flux_hbm, flux_ref, dest_sem.at[1])
    flux_copy.start()

    def clear(g, carry):
        dense_ref[pl.ds(g * CLEAR, CLEAR)] = jnp.zeros((CLEAR,) + dense_ref.shape[1:], BF16)
        return carry

    lax.fori_loop(0, total // CLEAR // 2, clear, 0)
    dense_ref[total] = jnp.zeros(dense_ref.shape[1:], BF16)
    for copy in smalls:
        copy.wait()
    live = lax.broadcasted_iota(jnp.int32, recv_ref.shape, 1) < live_ref[0, 0]
    panel = slice_ref[...] * cell_blocks + cell_ref[...]
    dest_ref[...] = jnp.where(live, panel * window_blocks + recv_ref[...], total)
    index = pltpu.make_async_copy(dest_ref, dest_smem, dest_sem.at[0])
    index.start()
    high, low = spread_own_first(blend_ref[...], CELLS_AT_ONCE, lax.axis_index("window"), False)
    spread_ref[0] = high
    spread_ref[1] = low
    row = lax.broadcasted_iota(jnp.int32, (panels, slots), 0)
    named = (row == jnp.where(live, panel, -1)).astype(BF16)
    row = lax.broadcasted_iota(jnp.int32, (window_blocks, slots), 0)
    heard = (row == recv_ref[...]).astype(BF16)
    counts = lax.dot_general(named, heard, (((1,), (1,)), ((), ())), preferred_element_type=F32)
    most = jnp.max(counts)
    lax.fori_loop(total // CLEAR // 2, total // CLEAR, clear, 0)
    index.wait()
    flux_copy.wait()

    @pl.when(most <= MOST)
    def _():
        for k in range(LOADS):
            loads[k].wait()

            def body(g, carry):
                for sub in range(DENSE_SUBS):
                    base = pl.multiple_of(k * part + (g * DENSE_SUBS + sub) * SUB, SUB)
                    x = slot_rows(raw, base)
                    for j in range(0, SUB, 2):
                        one, two = dest_smem[0, base + j], dest_smem[0, base + j + 1]
                        first, second = dense_ref[one], dense_ref[two]
                        again = jnp.where(one == two, x[j], jnp.zeros_like(x[j]))
                        dense_ref[one] = first + x[j]
                        dense_ref[two] = second + again + x[j + 1]
                return carry

            lax.fori_loop(0, part // SUB // DENSE_SUBS, body, 0)

    @pl.when(most > MOST)
    def _():
        for k in range(LOADS):
            loads[k].wait()
        chunk = sums.shape[0] - 1

        def span(c, carry):
            sums[...] = jnp.zeros_like(sums)

            def body(g, carry):
                base = pl.multiple_of(g * SUB, SUB)
                x = slot_rows(raw, base)
                for j in range(SUB):
                    to = dest_smem[0, base + j] - c * chunk
                    to = jnp.where((to >= 0) & (to < chunk), to, chunk)
                    sums[to] += x[j].astype(F32)
                return carry

            lax.fori_loop(0, slots // SUB, body, 0)

            def store(g, carry):
                dense_ref[c * chunk + g] = sums[g].astype(BF16)
                return carry

            lax.fori_loop(0, chunk, store, 0)
            return carry

        lax.fori_loop(0, total // chunk, span, 0)


def final_kernel(grad_ref, last_ref, mix_ref, own_ref, grad_hbm, own_hbm, flat, sem):
    slabs, cells, ens = grad_ref.shape
    columns = last_ref.shape[2]
    early = cells - columns
    done = pltpu.make_async_copy(grad_ref.at[:, pl.ds(0, early), :], grad_hbm.at[:, pl.ds(0, early), :], sem.at[0])
    done.start()
    own = pltpu.make_async_copy(own_ref, own_hbm, sem.at[1])
    own.start()
    flat[...] = mixed(last_ref[...], mix_ref[...])
    rest = pltpu.make_async_copy(flat, grad_hbm.at[:, pl.ds(early, columns), :], sem.at[2])
    rest.start()
    done.wait()
    own.wait()
    rest.wait()


def mixed(total, mix):
    slabs, ens, columns = total.shape
    flat = jnp.concatenate([total[s].T for s in range(slabs)], axis=0)
    return jnp.dot(flat, mix, preferred_element_type=F32).astype(BF16).reshape(slabs, columns, ens)


def whole_kernel(
    regions,
    dense_ref,
    flux_ref,
    other_ref,
    spread_ref,
    obs_hbm,
    inv_hbm,
    mix_hbm,
    blend_hbm,
    own_ref,
    grad_ref,
    last_ref,
    mix_ref,
    obs_ref,
    inv_ref,
    blend_ref,
    panels,
    acc,
    part,
    got,
    all_ref,
    tiles,
    sums,
    back,
    mine,
    away,
    pulled,
    send_a,
    recv_a,
    send_b,
    recv_b,
    send_w,
    recv_w,
    small_sem,
):
    me = lax.axis_index("region")
    win = lax.axis_index("window")
    rows, ens = obs_ref.shape
    slabs, cells, _ = flux_ref.shape
    slices = 2 * slabs
    own_blocks = rows // BLOCK
    q_blocks = own_blocks * regions
    cell_blocks = cells // BLOCK
    panel_total = slices * cell_blocks

    barrier = pltpu.get_barrier_semaphore()
    for k in range(1, regions):
        peer = lax.rem(me + k, regions)
        pl.semaphore_signal(barrier, inc=1, device_id={"region": peer}, device_id_type=MESH)
    pl.semaphore_signal(barrier, inc=1, device_id={"window": 1 - win}, device_id_type=MESH)

    smalls = [
        pltpu.make_async_copy(source, target, small_sem.at[k])
        for k, (source, target) in enumerate(((obs_hbm, obs_ref), (inv_hbm, inv_ref), (mix_hbm, mix_ref), (blend_hbm, blend_ref)))
    ]
    for copy in smalls:
        copy.start()
    high, low = spread_ref[0], spread_ref[1]

    def group(g, carry):
        sides = []
        for half in range(2):
            start = pl.multiple_of((2 * g + half) * CELLS_AT_ONCE, CELLS_AT_ONCE)
            for ref in (flux_ref, other_ref):
                sides.append(ref[:, pl.ds(start, CELLS_AT_ONCE), :].reshape(slabs * CELLS_AT_ONCE, ens))
        rhs = jnp.concatenate(
            [jnp.concatenate(sides[:2], axis=0), jnp.concatenate(sides[2:], axis=0)], axis=1
        )
        out = jnp.dot(high, rhs, preferred_element_type=F32) + jnp.dot(low, rhs, preferred_element_type=F32)
        out = out.astype(BF16)
        for half in range(2):
            start = pl.multiple_of((2 * g + half) * CELLS_AT_ONCE, CELLS_AT_ONCE)
            panels[:, pl.ds(start, CELLS_AT_ONCE), :] = out[:, half * ens : (half + 1) * ens].reshape(
                slices, CELLS_AT_ONCE, ens
            )
        return carry

    lax.fori_loop(0, cells // (2 * CELLS_AT_ONCE), group, 0, unroll=8)

    group_size = regions // 2
    near = (me // group_size) * group_size
    far = group_size - near
    span = group_size * own_blocks

    tall = own_blocks * HALF

    def forward(targets):
        high_rows = len(targets) * tall
        acc[pl.ds(0, high_rows), :] = jnp.zeros((high_rows, 2 * ens), F32)

        def body(g, carry):
            left, right = [], []
            for u in range(AT_ONCE):
                start = (g * AT_ONCE + u) * q_blocks
                left.append(
                    jnp.concatenate(
                        [
                            dense_ref[pl.ds(start + to * own_blocks, own_blocks)].reshape(tall, 2 * BLOCK)
                            for to in targets
                        ],
                        axis=0,
                    )
                )
                cell = (u % cell_blocks) * BLOCK
                one = panels[g * (AT_ONCE // cell_blocks) + u // cell_blocks, cell : cell + BLOCK, :]
                right.append(both(one, one))
            acc[pl.ds(0, high_rows), :] += jnp.dot(
                jnp.concatenate(left, axis=1), jnp.concatenate(right, axis=0), preferred_element_type=F32
            )
            return carry

        lax.fori_loop(0, panel_total // AT_ONCE, body, 0)
        for k, to in enumerate(targets):
            for q in range(own_blocks):
                for par in range(2):
                    start = q * BLOCK + par * HALF
                    part[to, start : start + HALF, :] = acc[
                        k * tall + q * HALF : k * tall + (q + 1) * HALF, par * ens : (par + 1) * ens
                    ].astype(BF16)

    def reduce_copy(source, to):
        return pltpu.make_async_remote_copy(
            src_ref=part.at[to],
            dst_ref=got.at[source],
            send_sem=send_a.at[to],
            recv_sem=recv_a.at[source],
            device_id={"region": to},
            device_id_type=MESH,
        )

    def gather_copy(source, to):
        return pltpu.make_async_remote_copy(
            src_ref=all_ref.at[source],
            dst_ref=all_ref.at[source],
            send_sem=send_b.at[to],
            recv_sem=recv_b.at[source],
            device_id={"region": to},
            device_id_type=MESH,
        )

    pairs_half = group_size // 2
    height, side = me // 2, lax.rem(me, 2)
    offset = height - near // 2
    near_pairs = [near // 2 + lax.rem(offset + k, pairs_half) for k in range(pairs_half)]
    far_pairs = [far // 2 + lax.rem(2 * pairs_half - 1 - offset + k, pairs_half) for k in range(pairs_half)]
    nears = [2 * height + 1 - side]
    for pair in near_pairs[1:]:
        nears += [2 * pair + side, 2 * pair + 1 - side]
    fars = []
    for pair in far_pairs:
        fars += [2 * pair + side, 2 * pair + 1 - side]

    forward(fars)
    pl.semaphore_wait(barrier, regions)
    for peer in fars:
        reduce_copy(me, peer).start()
    forward([me] + nears)
    for peer in nears:
        reduce_copy(me, peer).start()

    lower = lax.broadcasted_iota(jnp.int32, (HALF, 2 * BLOCK), 1) < BLOCK

    def pair_up(g, carry):
        for k in range(2):
            for q in range(q_blocks):
                one = dense_ref[(4 * g + 2 * k) * q_blocks + q]
                two = dense_ref[(4 * g + 2 * k + 1) * q_blocks + q]
                swapped = halves_swapped(jnp.where(lower, two, one))
                tiles[2 * g + k, pl.ds(q * BLOCK, HALF), :] = jnp.where(lower, one, swapped)
                tiles[2 * g + k, pl.ds(q * BLOCK + HALF, HALF), :] = jnp.where(lower, swapped, two)
        return carry

    for copy in smalls:
        copy.wait()
    table = table_for(rows)
    obs = jnp.dot(table.astype(BF16), obs_ref[...], preferred_element_type=F32)
    inv = jnp.sum(jnp.where(table, inv_ref[...], 0.0), axis=1, keepdims=True)
    rounds = panel_total // 4
    lax.fori_loop(0, rounds // 2, pair_up, 0)

    evolved = part[me].astype(F32)
    for peer in nears + fars:
        reduce_copy(peer, me).wait_recv()
        evolved = evolved + got[peer].astype(F32)
    misfit = (inv * (evolved - obs)).astype(BF16)
    all_ref[me] = misfit.T
    for peer in fars + nears:
        gather_copy(me, peer).start()
    own_ref[...] = lax.dot_general(
        table.astype(BF16), misfit, (((0,), (0,)), ((), ())), preferred_element_type=F32
    ).astype(BF16)
    lax.fori_loop(rounds // 2, rounds, pair_up, 0)
    pull_high, pull_low = spread_own_first(blend_ref[...], CELLS_AT_ONCE, win, True)

    mix = mix_ref[...]
    columns = 2 * BLOCK
    steps = cells // columns

    def send(step):
        return pltpu.make_async_remote_copy(
            src_ref=away.at[step],
            dst_ref=pulled.at[step],
            send_sem=send_w.at[step],
            recv_sem=recv_w.at[step],
            device_id={"window": 1 - win},
            device_id_type=MESH,
        )

    def product(step, half, pair, turned):
        right = [
            tiles[(half * slabs + t) * steps + step, pl.ds(pl.multiple_of(pair * 2 * rows, rows), 2 * rows), :]
            for t in range(slabs)
        ]
        return jnp.dot(turned, jnp.concatenate(right, axis=1), preferred_element_type=F32)

    ordered = near_pairs + far_pairs
    for n, pair in enumerate(ordered):
        for near_side in (1 - side, side) if n else (1 - side,):
            gather_copy(2 * pair + near_side, me).wait_recv()
        turned = jnp.concatenate([all_ref[2 * pair], all_ref[2 * pair + 1]], axis=1)
        if n < len(ordered) - 1:
            for step in range(steps):
                for half in range(2):
                    out = product(step, half, pair, turned)
                    sums[step, half] = sums[step, half] + out if n else out

    def adjoint(step):
        for half in range(2):
            out = (sums[step, half] + product(step, half, ordered[-1], turned)).astype(BF16)
            for t in range(slabs):
                back[half * slabs + t] = out[:, t * columns : (t + 1) * columns]
        for e in range(0, ens, 2 * CELLS_AT_ONCE):
            rhs = jnp.concatenate(
                [
                    back[:, e + h * CELLS_AT_ONCE : e + (h + 1) * CELLS_AT_ONCE, :].reshape(
                        slices * CELLS_AT_ONCE, columns
                    )
                    for h in range(2)
                ],
                axis=1,
            )
            out = jnp.dot(pull_high, rhs, preferred_element_type=F32)
            out = (out + jnp.dot(pull_low, rhs, preferred_element_type=F32)).astype(BF16)
            for h in range(2):
                piece = out[:, h * columns : (h + 1) * columns].reshape(slices, CELLS_AT_ONCE, columns)
                at_e = e + h * CELLS_AT_ONCE
                mine[step, :, at_e : at_e + CELLS_AT_ONCE, :] = piece[:slabs]
                away[step, :, at_e : at_e + CELLS_AT_ONCE, :] = piece[slabs:]

    def finish(step):
        send(step).wait_recv()
        total = (mine[step].astype(F32) + pulled[step].astype(F32)).astype(BF16)
        if step == steps - 1:
            last_ref[...] = total
        else:
            grad_ref[:, step * columns : (step + 1) * columns, :] = mixed(total, mix)

    for step in range(steps):
        adjoint(step)
        send(step).start()
        if step >= DENSE_LAG:
            finish(step - DENSE_LAG)
    for step in range(steps - DENSE_LAG, steps):
        finish(step)
    for step in range(steps):
        send(step).wait_send()
    for peer in nears + fars:
        reduce_copy(me, peer).wait_send()
        gather_copy(me, peer).wait_send()


def dense_shards(
    regions,
    flux,
    blend,
    footprints,
    receptor_block,
    cell_block,
    slice_index,
    live_counts,
    observed,
    inv_var,
    prior_mix,
):
    slabs, cells, ens = flux.shape
    slices = blend.shape[0]
    cell_blocks = cells // BLOCK
    panel_total = slices * cell_blocks
    slots = footprints.shape[1]
    rows = observed.shape[1]
    window_blocks = rows // BLOCK * regions
    total = panel_total * window_blocks
    columns = 2 * BLOCK
    steps = cells // columns

    other = lax.ppermute(flux, "window", [(0, 1), (1, 0)])
    dense, kernels, near_flux = pl.pallas_call(
        functools.partial(place_kernel, window_blocks, cell_blocks),
        out_shape=(
            jax.ShapeDtypeStruct((total + 1, HALF, 2 * BLOCK), BF16),
            jax.ShapeDtypeStruct((2, slices * CELLS_AT_ONCE, slices * CELLS_AT_ONCE), BF16),
            jax.ShapeDtypeStruct((slabs, cells, ens), BF16),
        ),
        in_specs=[hbm()] * 3 + [pl.BlockSpec(memory_space=pltpu.SMEM)] + [hbm()] * 3,
        out_specs=(vmem(), vmem(), vmem()),
        scratch_shapes=[
            pltpu.VMEM((slots, BLOCK * BLOCK), BF16),
            pltpu.VMEM((1, slots), jnp.int32),
            pltpu.VMEM((1, slots), jnp.int32),
            pltpu.VMEM((1, slots), jnp.int32),
            pltpu.VMEM((slices, slices), F32),
            pltpu.VMEM((1, slots), jnp.int32),
            pltpu.SMEM((1, slots), jnp.int32),
            pltpu.VMEM((total // 8 + 1, HALF, 2 * BLOCK), F32),
            pltpu.SemaphoreType.DMA((4,)),
            pltpu.SemaphoreType.DMA((LOADS,)),
            pltpu.SemaphoreType.DMA((2,)),
        ],
        compiler_params=pltpu.CompilerParams(vmem_limit_bytes=DENSE_VMEM),
        cost_estimate=pl.CostEstimate(flops=0, bytes_accessed=24 << 20, transcendentals=0),
        name="place_blocks",
    )(stay(receptor_block), stay(cell_block), stay(slice_index), live_counts, stay(blend), stay(flux), stay(footprints))

    misfit, gradient, last, mix = pl.pallas_call(
        functools.partial(whole_kernel, regions),
        out_shape=(
            jax.ShapeDtypeStruct((rows, ens), BF16),
            jax.ShapeDtypeStruct((slabs, cells, ens), BF16),
            jax.ShapeDtypeStruct((slabs, ens, columns), BF16),
            jax.ShapeDtypeStruct(prior_mix.shape, BF16),
        ),
        in_specs=[vmem()] * 4 + [hbm()] * 4,
        out_specs=(vmem(), vmem(), vmem(), vmem()),
        scratch_shapes=[
            pltpu.VMEM((rows, ens), BF16),
            pltpu.VMEM((1, rows), F32),
            pltpu.VMEM((slices, slices), F32),
            pltpu.VMEM((slices, cells, ens), BF16),
            pltpu.VMEM((window_blocks // 2 * HALF, 2 * ens), F32),
            pltpu.VMEM((regions, rows, ens), BF16),
            pltpu.VMEM((regions, rows, ens), BF16),
            pltpu.VMEM((regions, ens, rows), BF16),
            pltpu.VMEM((panel_total // 2, window_blocks * BLOCK, columns), BF16),
            pltpu.VMEM((steps, 2, ens, slabs * columns), F32),
            pltpu.VMEM((slices, ens, columns), BF16),
            pltpu.VMEM((steps, slabs, ens, columns), BF16),
            pltpu.VMEM((steps, slabs, ens, columns), BF16),
            pltpu.VMEM((steps, slabs, ens, columns), BF16),
        ]
        + [pltpu.SemaphoreType.DMA((regions,))] * 4
        + [pltpu.SemaphoreType.DMA((steps,))] * 2
        + [pltpu.SemaphoreType.DMA((4,))],
        compiler_params=pltpu.CompilerParams(collective_id=3, has_side_effects=True, vmem_limit_bytes=DENSE_VMEM),
        name="transport",
    )(dense, near_flux, other, kernels, stay(observed[0]), stay(inv_var), stay(prior_mix), stay(blend))

    gradient, misfit = pl.pallas_call(
        final_kernel,
        out_shape=(
            jax.ShapeDtypeStruct((slabs, cells, ens), BF16),
            jax.ShapeDtypeStruct((rows, ens), BF16),
        ),
        in_specs=[vmem()] * 4,
        out_specs=(hbm(), hbm()),
        scratch_shapes=[pltpu.VMEM((slabs, columns, ens), BF16), pltpu.SemaphoreType.DMA((3,))],
        compiler_params=pltpu.CompilerParams(vmem_limit_bytes=4 << 20),
        name="final_mix",
    )(gradient, last, mix, misfit)
    return misfit[None], gradient


def solution(mesh):
    in_specs = (
        P(("group", "window"), "region", None),
        P(),
        P(("group", "window"), "region", None),
        P(("group", "window"), "region"),
        P(("group", "window"), "region"),
        P(("group", "window"), "region"),
        P(("group", "window"), "region"),
        P(("group", "window"), "region", None),
        P(("group", "window"), "region"),
        P(),
    )
    out_specs = (P(("group", "window"), "region", None), P(("group", "window"), "region", None))

    def either(*args):
        regions = mesh.shape["region"]
        blocks = args[7].shape[1] // BLOCK * regions
        return (dense_shards if blocks <= DENSE_BLOCKS and regions % 4 == 0 else shards)(regions, *args)

    return jax.shard_map(
        either,
        mesh=mesh,
        in_specs=in_specs,
        out_specs=out_specs,
        check_vma=False,
    )
```

```python
import functools

import jax
import jax.numpy as jnp
from jax import lax
from jax.experimental import pallas as pl
from jax.experimental.pallas import tpu as pltpu
from jax.sharding import PartitionSpec as P

BLOCK = 64
MESH = pl.DeviceIdType.MESH
F32 = jnp.float32
BF16 = jnp.bfloat16
SUB = 16
SUBS = 4
CELLS_AT_ONCE = 16
PIECES = 4
LOADS = 8
PAIRS = 32
TURNS = 32
LAG = 2
HALF = BLOCK // 2
CLEAR = 64
MOST = 16
DENSE_SUBS = 4
AT_ONCE = 32
DENSE_LAG = 3
DENSE_VMEM = 33 << 20
DENSE_BLOCKS = 16


def spread(matrix, width):
    size = matrix.shape[0]
    full = size * width
    row = lax.broadcasted_iota(jnp.int32, (full, size), 0)
    col = lax.broadcasted_iota(jnp.int32, (full, size), 1)
    pick = (row // width == col).astype(BF16)
    row_f = lax.broadcasted_iota(jnp.int32, (full, full), 0)
    col_f = lax.broadcasted_iota(jnp.int32, (full, full), 1)
    same = row_f % width == col_f % width
    high = matrix.astype(BF16)
    low = (matrix - high.astype(F32)).astype(BF16)
    parts = []
    for part in (high, low):
        tall = jnp.dot(pick, part, preferred_element_type=F32).astype(BF16)
        wide = lax.dot_general(tall, pick, (((1,), (1,)), ((), ())), preferred_element_type=F32)
        parts.append(jnp.where(same, wide, 0.0).astype(BF16))
    return parts


def halves_swapped(x):
    return pltpu.roll(x, BLOCK, 1)


def blend_kernel(
    window_blocks,
    recv_hbm,
    cell_hbm,
    slice_hbm,
    live_ref,
    blend_hbm,
    flux_hbm,
    fp_hbm,
    panels_ref,
    pairs_ref,
    index_ref,
    full,
    raw,
    blend_ref,
    recv_ref,
    cell_ref,
    slice_ref,
    small_sem,
    fp_sem,
    local_sem,
    send_sem,
    recv_sem,
):
    me = lax.axis_index("window")
    other = 1 - me
    slabs, cells, ens = flux_hbm.shape
    slices = panels_ref.shape[0]
    slots = raw.shape[0]
    barrier = pltpu.get_barrier_semaphore()
    pl.semaphore_signal(barrier, inc=1, device_id={"window": other}, device_id_type=MESH)
    smalls = [
        pltpu.make_async_copy(source, target, small_sem.at[k])
        for k, (source, target) in enumerate(
            ((blend_hbm, blend_ref), (recv_hbm, recv_ref), (cell_hbm, cell_ref), (slice_hbm, slice_ref))
        )
    ]
    for copy in smalls:
        copy.start()
    piece = cells // PIECES
    locals_, sends, loads = [], [], []
    for k in range(PIECES):
        span = pl.ds(k * piece, piece)
        locals_.append(
            pltpu.make_async_copy(
                flux_hbm.at[:, span, :], full.at[pl.ds(me * slabs, slabs), span, :], local_sem.at[k]
            )
        )
        locals_[-1].start()
    part = slots // LOADS
    for k in range(LOADS):
        span = pl.ds(k * part, part)
        loads.append(pltpu.make_async_copy(fp_hbm.at[0, span, :], raw.at[span, :], fp_sem.at[k]))
    loads[0].start()
    pl.semaphore_wait(barrier, 1)
    for k in range(PIECES):
        span = pl.ds(k * piece, piece)
        sends.append(
            pltpu.make_async_remote_copy(
                src_ref=flux_hbm.at[:, span, :],
                dst_ref=full.at[pl.ds(me * slabs, slabs), span, :],
                send_sem=send_sem.at[k],
                recv_sem=recv_sem.at[k],
                device_id={"window": other},
                device_id_type=MESH,
            )
        )
        sends[-1].start()
    for k in range(1, LOADS):
        loads[k].start()

    for copy in smalls:
        copy.wait()
    cell_blocks = cells // BLOCK
    live = lax.broadcasted_iota(jnp.int32, recv_ref.shape, 1) < live_ref[...]
    panel = slice_ref[...] * cell_blocks + cell_ref[...]
    index_ref[pl.ds(0, 1), :] = jnp.where(live, recv_ref[...], window_blocks)
    index_ref[pl.ds(1, 1), :] = jnp.where(live, panel, 0)
    index_ref[pl.ds(2, 1), :] = jnp.where(live, panel, slices * cell_blocks)
    index_ref[pl.ds(3, 1), :] = jnp.where(live, recv_ref[...], 0)
    high, low = spread(blend_ref[...], CELLS_AT_ONCE)

    def arrange(k):
        loads[k].wait()

        def body(g, carry):
            lower = lax.broadcasted_iota(jnp.int32, (BLOCK // 2, 2 * BLOCK), 1) < BLOCK
            for sub in range(SUBS):
                base = pl.multiple_of(k * part + g * SUBS * SUB + sub * SUB, SUB)
                x = raw[pl.ds(base, SUB), :].reshape(SUB, BLOCK // 2, 2 * BLOCK)
                for j in range(0, SUB, 2):
                    one, two = x[j], x[j + 1]
                    even = jnp.where(lower, one, halves_swapped(two))
                    odd = jnp.where(lower, halves_swapped(one), two)
                    place = k * (part // 2) + (g * SUBS + sub) * (SUB // 2) + j // 2
                    pairs_ref[place] = jnp.concatenate([even, odd], axis=0)
            return carry

        lax.fori_loop(0, part // SUB // SUBS, body, 0)

    for k in range(LOADS // 2):
        arrange(k)
    for k in range(PIECES):
        locals_[k].wait()
        sends[k].wait_recv()

        def group(g, carry, k=k):
            sides = []
            for half in range(2):
                start = pl.multiple_of(k * piece + g * 2 * CELLS_AT_ONCE + half * CELLS_AT_ONCE, CELLS_AT_ONCE)
                sides.append(full[:, pl.ds(start, CELLS_AT_ONCE), :].reshape(slices * CELLS_AT_ONCE, ens))
            rhs = jnp.concatenate(sides, axis=1)
            out = jnp.dot(high, rhs, preferred_element_type=F32) + jnp.dot(low, rhs, preferred_element_type=F32)
            out = out.astype(BF16)
            for half in range(2):
                start = pl.multiple_of(k * piece + g * 2 * CELLS_AT_ONCE + half * CELLS_AT_ONCE, CELLS_AT_ONCE)
                panels_ref[:, pl.ds(start, CELLS_AT_ONCE), :] = out[:, half * ens : (half + 1) * ens].reshape(
                    slices, CELLS_AT_ONCE, ens
                )
            return carry

        lax.fori_loop(0, piece // (2 * CELLS_AT_ONCE), group, 0, unroll=2)
    for k in range(LOADS // 2, LOADS):
        arrange(k)
    for k in range(PIECES):
        sends[k].wait_send()


def both(one, two):
    zero = jnp.zeros_like(one)
    return jnp.concatenate(
        [jnp.concatenate([one, zero], axis=1), jnp.concatenate([zero, two], axis=1)], axis=0
    )


def products(index_ref, left_ref, right_ref, acc, to, source):
    acc[...] = jnp.zeros_like(acc)
    ens = acc.shape[2]

    def body(g, carry):
        for j in range(PAIRS):
            pair = g * PAIRS + j
            one = right_ref[index_ref[source, 2 * pair]]
            two = right_ref[index_ref[source, 2 * pair + 1]]
            out = jnp.dot(left_ref[pair], both(one, two), preferred_element_type=F32)
            acc[index_ref[to, 2 * pair]] += out[:, :ens]
            acc[index_ref[to, 2 * pair + 1]] += out[:, ens:]
        return carry

    lax.fori_loop(0, left_ref.shape[0] // PAIRS, body, 0)


def forward_kernel(index_ref, pairs_ref, panels_ref, part_ref, acc):
    products(index_ref, pairs_ref, panels_ref, acc, 0, 1)
    part_ref[...] = acc[pl.ds(0, part_ref.shape[0])].astype(BF16)


def turned_pair(x):
    t = x.T
    return jnp.concatenate([t[:BLOCK], t[BLOCK:]], axis=1)


def exchange_kernel(
    regions, part_ref, obs_ref, inv_ref, pairs_ref, all_ref, own_ref, turned_ref, got, send_a, recv_a, send_b, recv_b, send_c, recv_c
):
    me = lax.axis_index("region")
    rows, ens = obs_ref.shape
    barrier = pltpu.get_barrier_semaphore()
    for k in range(1, regions):
        peer = lax.rem(me + k, regions)
        pl.semaphore_signal(barrier, inc=1, device_id={"region": peer}, device_id_type=MESH)
    row = lax.broadcasted_iota(jnp.int32, (rows, rows), 0)
    col = lax.broadcasted_iota(jnp.int32, (rows, rows), 1)
    inner = row % BLOCK
    half = BLOCK // 2
    picked = (row // BLOCK) * BLOCK + (inner % half) * 2 + inner // half == col
    table = picked.astype(BF16)
    obs = jnp.dot(table, obs_ref[...], preferred_element_type=F32)
    inv = jnp.sum(jnp.where(picked, inv_ref[...], 0.0), axis=1, keepdims=True)
    pl.semaphore_wait(barrier, regions - 1)

    def first(k):
        peer = lax.rem(me + k, regions)
        return pltpu.make_async_remote_copy(
            src_ref=part_ref.at[peer],
            dst_ref=got.at[k],
            send_sem=send_a.at[k],
            recv_sem=recv_a.at[k],
            device_id={"region": peer},
            device_id_type=MESH,
        )

    width = 2 if regions % 2 == 0 else 1
    count = regions // width
    high, low = me // width, lax.rem(me, width)

    def at(k, low):
        return lax.rem(high + count - k, count) * width + low

    def along(k, source):
        return pltpu.make_async_remote_copy(
            src_ref=all_ref.at[source],
            dst_ref=all_ref.at[source],
            send_sem=send_b.at[k],
            recv_sem=recv_b.at[k],
            device_id={"region": lax.rem(high + k, count) * width + low},
            device_id_type=MESH,
        )

    def across(k, source):
        return pltpu.make_async_remote_copy(
            src_ref=all_ref.at[source],
            dst_ref=all_ref.at[source],
            send_sem=send_c.at[k],
            recv_sem=recv_c.at[k],
            device_id={"region": high * width + 1 - low},
            device_id_type=MESH,
        )

    firsts = [first(k) for k in range(1, regions)]
    for copy in firsts:
        copy.start()

    pair_count = pairs_ref.shape[0]

    def turn(g, carry):
        for j in range(TURNS):
            turned_ref[g * TURNS + j] = turned_pair(pairs_ref[g * TURNS + j])
        return carry

    rounds = pair_count // TURNS
    lax.fori_loop(0, rounds // 2, turn, 0)
    evolved = part_ref[me].astype(F32)
    for k in range(1, regions):
        firsts[k - 1].wait_recv()
        evolved = evolved + got[k].astype(F32)
    misfit = (inv * (evolved - obs)).astype(BF16)
    all_ref[me] = misfit
    seconds = [along(k, me) for k in range(1, count)]
    for copy in seconds:
        copy.start()
    if width == 2:
        seconds.append(across(0, me))
        seconds[-1].start()
    own_ref[...] = lax.dot_general(
        table, misfit, (((0,), (0,)), ((), ())), preferred_element_type=F32
    ).astype(BF16)
    lax.fori_loop(rounds // 2, rounds * 3 // 4, turn, 0)
    for k in range(1, count):
        along(k, at(k, low)).wait_recv()
        if width == 2:
            seconds.append(across(k, at(k, low)))
            seconds[-1].start()
    lax.fori_loop(rounds * 3 // 4, rounds, turn, 0)
    if width == 2:
        for k in range(count):
            across(k, at(k, 1 - low)).wait_recv()
    for copy in firsts + seconds:
        copy.wait_send()


def adjoint_kernel(index_ref, turned_ref, misfit_ref, own_ref, acc, misfit_out):
    products(index_ref, turned_ref, misfit_ref, acc, 2, 3)
    misfit_out[...] = own_ref[...]


def gradient_kernel(acc_ref, blend_ref, mix_ref, grad_ref, mine, away, got, send_sem, recv_sem):
    me = lax.axis_index("window")
    other = 1 - me
    slabs, cells, ens = grad_ref.shape
    slices = 2 * slabs
    blocks = cells // BLOCK
    barrier = pltpu.get_barrier_semaphore()
    pl.semaphore_signal(barrier, inc=1, device_id={"window": other}, device_id_type=MESH)
    high, low = spread(blend_ref[...], CELLS_AT_ONCE)
    mix = mix_ref[...]
    pl.semaphore_wait(barrier, 1)

    def send(block):
        return pltpu.make_async_remote_copy(
            src_ref=away.at[block],
            dst_ref=got.at[block],
            send_sem=send_sem.at[block],
            recv_sem=recv_sem.at[block],
            device_id={"window": other},
            device_id_type=MESH,
        )

    def pull(block):
        for within in range(BLOCK // (2 * CELLS_AT_ONCE)):
            sides = []
            for half in range(2):
                start = (2 * within + half) * CELLS_AT_ONCE
                rows = [acc_ref[t * blocks + block, pl.ds(start, CELLS_AT_ONCE), :] for t in range(slices)]
                sides.append(jnp.concatenate(rows, axis=0))
            rhs = jnp.concatenate(sides, axis=1)
            rhs_high = rhs.astype(BF16)
            rhs_low = (rhs - rhs_high.astype(F32)).astype(BF16)
            dims = (((0,), (0,)), ((), ()))
            out = lax.dot_general(high, rhs_high, dims, preferred_element_type=F32)
            out = out + lax.dot_general(low, rhs_high, dims, preferred_element_type=F32)
            out = (out + lax.dot_general(high, rhs_low, dims, preferred_element_type=F32)).astype(BF16)
            for half in range(2):
                start = (2 * within + half) * CELLS_AT_ONCE
                piece = out[:, half * ens : (half + 1) * ens].reshape(slices, CELLS_AT_ONCE, ens)
                first, second = piece[:slabs], piece[slabs:]
                mine[block, :, pl.ds(start, CELLS_AT_ONCE), :] = jnp.where(me == 0, first, second)
                away[block, :, pl.ds(start, CELLS_AT_ONCE), :] = jnp.where(me == 0, second, first)

    def finish(block):
        send(block).wait_recv()
        total = (mine[block].astype(F32) + got[block].astype(F32)).astype(BF16).reshape(slabs * BLOCK, ens)
        grad = jnp.dot(total, mix, preferred_element_type=F32).astype(BF16)
        grad_ref[:, pl.ds(block * BLOCK, BLOCK), :] = grad.reshape(slabs, BLOCK, ens)

    for block in range(blocks):
        pull(block)
        send(block).start()
        if block >= LAG:
            finish(block - LAG)
    for block in range(blocks - LAG, blocks):
        finish(block)
    for block in range(blocks):
        send(block).wait_send()


def vmem():
    return pl.BlockSpec(memory_space=pltpu.VMEM)


def hbm():
    return pl.BlockSpec(memory_space=pltpu.HBM)


def stay(x):
    return pltpu.with_memory_space_constraint(x, pltpu.HBM)


def shards(
    regions,
    flux,
    blend,
    footprints,
    receptor_block,
    cell_block,
    slice_index,
    live_counts,
    observed,
    inv_var,
    prior_mix,
):
    slabs, cells, ens = flux.shape
    slices = blend.shape[0]
    cell_blocks = cells // BLOCK
    panel_total = slices * cell_blocks
    slots = footprints.shape[1]
    rows = observed.shape[1]
    own_blocks = rows // BLOCK
    window_blocks = own_blocks * regions

    panels, pairs, index = pl.pallas_call(
        functools.partial(blend_kernel, window_blocks),
        out_shape=(
            jax.ShapeDtypeStruct((slices, cells, ens), BF16),
            jax.ShapeDtypeStruct((slots // 2, BLOCK, 2 * BLOCK), BF16),
            jax.ShapeDtypeStruct((4, slots), jnp.int32),
        ),
        in_specs=[hbm()] * 3 + [vmem()] + [hbm()] * 3,
        out_specs=(vmem(), vmem(), vmem()),
        scratch_shapes=[
            pltpu.VMEM((slices, cells, ens), BF16),
            pltpu.VMEM((slots, BLOCK * BLOCK), BF16),
            pltpu.VMEM((slices, slices), F32),
            pltpu.VMEM((1, slots), jnp.int32),
            pltpu.VMEM((1, slots), jnp.int32),
            pltpu.VMEM((1, slots), jnp.int32),
            pltpu.SemaphoreType.DMA((4,)),
            pltpu.SemaphoreType.DMA((LOADS,)),
            pltpu.SemaphoreType.DMA((PIECES,)),
            pltpu.SemaphoreType.DMA((PIECES,)),
            pltpu.SemaphoreType.DMA((PIECES,)),
        ],
        compiler_params=pltpu.CompilerParams(collective_id=0, has_side_effects=True, vmem_limit_bytes=24 << 20),
        name="blend_slices",
    )(
        stay(receptor_block),
        stay(cell_block),
        stay(slice_index),
        live_counts,
        stay(blend),
        stay(flux),
        stay(footprints),
    )

    smem = pl.BlockSpec(memory_space=pltpu.SMEM)
    part = pl.pallas_call(
        forward_kernel,
        out_shape=jax.ShapeDtypeStruct((window_blocks, BLOCK, ens), BF16),
        in_specs=[smem, vmem(), vmem()],
        out_specs=vmem(),
        scratch_shapes=[pltpu.VMEM((window_blocks + 1, BLOCK, ens), F32)],
        compiler_params=pltpu.CompilerParams(vmem_limit_bytes=16 << 20),
        name="forward_blocks",
    )(index, pairs, panels.reshape(panel_total, BLOCK, ens))

    misfit_all, own, turned = pl.pallas_call(
        functools.partial(exchange_kernel, regions),
        out_shape=(
            jax.ShapeDtypeStruct((regions, rows, ens), BF16),
            jax.ShapeDtypeStruct((rows, ens), BF16),
            jax.ShapeDtypeStruct((slots // 2, BLOCK, 2 * BLOCK), BF16),
        ),
        in_specs=[vmem()] * 4,
        out_specs=(vmem(), vmem(), vmem()),
        scratch_shapes=[
            pltpu.VMEM((regions, rows, ens), BF16),
            pltpu.SemaphoreType.DMA((regions,)),
            pltpu.SemaphoreType.DMA((regions,)),
            pltpu.SemaphoreType.DMA((regions,)),
            pltpu.SemaphoreType.DMA((regions,)),
            pltpu.SemaphoreType.DMA((regions,)),
            pltpu.SemaphoreType.DMA((regions,)),
        ],
        compiler_params=pltpu.CompilerParams(collective_id=1, has_side_effects=True, vmem_limit_bytes=16 << 20),
        name="misfit_exchange",
    )(part.reshape(regions, rows, ens), observed[0], inv_var, pairs)

    collected, misfit = pl.pallas_call(
        adjoint_kernel,
        out_shape=(
            jax.ShapeDtypeStruct((panel_total + 1, BLOCK, ens), F32),
            jax.ShapeDtypeStruct((rows, ens), BF16),
        ),
        in_specs=[smem, vmem(), vmem(), vmem()],
        out_specs=(vmem(), vmem()),
        compiler_params=pltpu.CompilerParams(vmem_limit_bytes=16 << 20),
        name="adjoint_blocks",
    )(index, turned, misfit_all.reshape(window_blocks, BLOCK, ens), own)

    blocks_shape = (cell_blocks, slabs, BLOCK, ens)
    gradient = pl.pallas_call(
        gradient_kernel,
        out_shape=jax.ShapeDtypeStruct((slabs, cells, ens), BF16),
        in_specs=[vmem(), vmem(), vmem()],
        out_specs=vmem(),
        scratch_shapes=[
            pltpu.VMEM(blocks_shape, BF16),
            pltpu.VMEM(blocks_shape, BF16),
            pltpu.VMEM(blocks_shape, BF16),
            pltpu.SemaphoreType.DMA((cell_blocks,)),
            pltpu.SemaphoreType.DMA((cell_blocks,)),
        ],
        compiler_params=pltpu.CompilerParams(collective_id=2, has_side_effects=True, vmem_limit_bytes=16 << 20),
        name="gradient_exchange",
    )(collected, blend, prior_mix)
    return misfit[None], gradient


def table_for(rows):
    row = lax.broadcasted_iota(jnp.int32, (rows, rows), 0)
    col = lax.broadcasted_iota(jnp.int32, (rows, rows), 1)
    inner = row % BLOCK
    return (row // BLOCK) * BLOCK + (inner % HALF) * 2 + inner // HALF == col


def spread_own_first(matrix, width, me, pulling):
    size = matrix.shape[0]
    full = size * width
    row = lax.broadcasted_iota(jnp.int32, (full, size), 0) // width
    col = lax.broadcasted_iota(jnp.int32, (full, size), 1)
    pick = (row == col).astype(BF16)
    pick_own = ((row + me * (size // 2)) % size == col).astype(BF16)
    row_f = lax.broadcasted_iota(jnp.int32, (full, full), 0)
    col_f = lax.broadcasted_iota(jnp.int32, (full, full), 1)
    same = row_f % width == col_f % width
    part = matrix.astype(BF16)
    nt = (((1,), (1,)), ((), ()))
    if pulling:
        tall = lax.dot_general(pick_own, part, nt, preferred_element_type=F32).astype(BF16)
        wide = lax.dot_general(tall, pick, nt, preferred_element_type=F32)
    else:
        tall = jnp.dot(pick, part, preferred_element_type=F32).astype(BF16)
        wide = lax.dot_general(tall, pick_own, nt, preferred_element_type=F32)
    return jnp.where(same, wide, 0.0).astype(BF16)


def slot_rows(raw, base):
    tiles = [raw[pl.ds(base, SUB), i * 2 * BLOCK : (i + 1) * 2 * BLOCK] for i in range(HALF)]
    return jnp.transpose(jnp.stack(tiles, axis=0), (1, 0, 2))


def place_kernel(
    window_blocks,
    cell_blocks,
    recv_hbm,
    cell_hbm,
    slice_hbm,
    live_ref,
    blend_hbm,
    flux_hbm,
    fp_hbm,
    dense_ref,
    spread_ref,
    flux_ref,
    raw,
    recv_ref,
    cell_ref,
    slice_ref,
    blend_ref,
    dest_ref,
    dest_smem,
    sums,
    small_sem,
    fp_sem,
    dest_sem,
):
    slots = raw.shape[0]
    total = dense_ref.shape[0] - 1
    panels = total // window_blocks
    smalls = [
        pltpu.make_async_copy(source, target, small_sem.at[k])
        for k, (source, target) in enumerate(
            (
                (recv_hbm, recv_ref),
                (cell_hbm, cell_ref),
                (slice_hbm, slice_ref),
                (blend_hbm, blend_ref),
            )
        )
    ]
    for copy in smalls:
        copy.start()
    part = slots // LOADS
    loads = []
    for k in range(LOADS):
        span = pl.ds(k * part, part)
        loads.append(pltpu.make_async_copy(fp_hbm.at[0, span, :], raw.at[span, :], fp_sem.at[k]))
        loads[-1].start()

    flux_copy = pltpu.make_async_copy(flux_hbm, flux_ref, dest_sem.at[1])
    flux_copy.start()

    def clear(g, carry):
        dense_ref[pl.ds(g * CLEAR, CLEAR)] = jnp.zeros((CLEAR,) + dense_ref.shape[1:], BF16)
        return carry

    lax.fori_loop(0, total // CLEAR // 2, clear, 0)
    dense_ref[total] = jnp.zeros(dense_ref.shape[1:], BF16)
    for copy in smalls:
        copy.wait()
    live = lax.broadcasted_iota(jnp.int32, recv_ref.shape, 1) < live_ref[0, 0]
    panel = slice_ref[...] * cell_blocks + cell_ref[...]
    dest_ref[...] = jnp.where(live, panel * window_blocks + recv_ref[...], total)
    index = pltpu.make_async_copy(dest_ref, dest_smem, dest_sem.at[0])
    index.start()
    spread_ref[...] = spread_own_first(blend_ref[...], CELLS_AT_ONCE, lax.axis_index("window"), False)
    row = lax.broadcasted_iota(jnp.int32, (panels, slots), 0)
    named = (row == jnp.where(live, panel, -1)).astype(BF16)
    row = lax.broadcasted_iota(jnp.int32, (window_blocks, slots), 0)
    heard = (row == recv_ref[...]).astype(BF16)
    counts = lax.dot_general(named, heard, (((1,), (1,)), ((), ())), preferred_element_type=F32)
    most = jnp.max(counts)
    lax.fori_loop(total // CLEAR // 2, total // CLEAR, clear, 0)
    index.wait()
    flux_copy.wait()

    @pl.when(most <= MOST)
    def _():
        for k in range(LOADS):
            loads[k].wait()

            def body(g, carry):
                for sub in range(DENSE_SUBS):
                    base = pl.multiple_of(k * part + (g * DENSE_SUBS + sub) * SUB, SUB)
                    x = slot_rows(raw, base)
                    for j in range(0, SUB, 2):
                        one, two = dest_smem[0, base + j], dest_smem[0, base + j + 1]
                        first, second = dense_ref[one], dense_ref[two]
                        again = jnp.where(one == two, x[j], jnp.zeros_like(x[j]))
                        dense_ref[one] = first + x[j]
                        dense_ref[two] = second + again + x[j + 1]
                return carry

            lax.fori_loop(0, part // SUB // DENSE_SUBS, body, 0)

    @pl.when(most > MOST)
    def _():
        for k in range(LOADS):
            loads[k].wait()
        chunk = sums.shape[0] - 1

        def span(c, carry):
            sums[...] = jnp.zeros_like(sums)

            def body(g, carry):
                base = pl.multiple_of(g * SUB, SUB)
                x = slot_rows(raw, base)
                for j in range(SUB):
                    to = dest_smem[0, base + j] - c * chunk
                    to = jnp.where((to >= 0) & (to < chunk), to, chunk)
                    sums[to] += x[j].astype(F32)
                return carry

            lax.fori_loop(0, slots // SUB, body, 0)

            def store(g, carry):
                dense_ref[c * chunk + g] = sums[g].astype(BF16)
                return carry

            lax.fori_loop(0, chunk, store, 0)
            return carry

        lax.fori_loop(0, total // chunk, span, 0)


def final_kernel(grad_ref, last_ref, mix_ref, own_ref, grad_hbm, own_hbm, flat, sem):
    slabs, cells, ens = grad_ref.shape
    columns = last_ref.shape[2]
    early = cells - columns
    done = pltpu.make_async_copy(grad_ref.at[:, pl.ds(0, early), :], grad_hbm.at[:, pl.ds(0, early), :], sem.at[0])
    done.start()
    own = pltpu.make_async_copy(own_ref, own_hbm, sem.at[1])
    own.start()
    flat[...] = mixed(last_ref[...], mix_ref[...])
    rest = pltpu.make_async_copy(flat, grad_hbm.at[:, pl.ds(early, columns), :], sem.at[2])
    rest.start()
    done.wait()
    own.wait()
    rest.wait()


def mixed(total, mix):
    slabs, ens, columns = total.shape
    flat = jnp.concatenate([total[s].T for s in range(slabs)], axis=0)
    return jnp.dot(flat, mix, preferred_element_type=F32).astype(BF16).reshape(slabs, columns, ens)


def whole_kernel(
    regions,
    dense_ref,
    flux_ref,
    other_ref,
    spread_ref,
    obs_hbm,
    inv_hbm,
    mix_hbm,
    blend_hbm,
    own_ref,
    grad_ref,
    last_ref,
    mix_ref,
    obs_ref,
    inv_ref,
    blend_ref,
    panels,
    acc,
    part,
    got,
    all_ref,
    tiles,
    sums,
    back,
    mine,
    away,
    pulled,
    send_a,
    recv_a,
    send_b,
    recv_b,
    send_w,
    recv_w,
    small_sem,
):
    me = lax.axis_index("region")
    win = lax.axis_index("window")
    rows, ens = obs_ref.shape
    slabs, cells, _ = flux_ref.shape
    slices = 2 * slabs
    own_blocks = rows // BLOCK
    q_blocks = own_blocks * regions
    cell_blocks = cells // BLOCK
    panel_total = slices * cell_blocks

    barrier = pltpu.get_barrier_semaphore()
    for k in range(1, regions):
        peer = lax.rem(me + k, regions)
        pl.semaphore_signal(barrier, inc=1, device_id={"region": peer}, device_id_type=MESH)
    pl.semaphore_signal(barrier, inc=1, device_id={"window": 1 - win}, device_id_type=MESH)

    smalls = [
        pltpu.make_async_copy(source, target, small_sem.at[k])
        for k, (source, target) in enumerate(((obs_hbm, obs_ref), (inv_hbm, inv_ref), (mix_hbm, mix_ref), (blend_hbm, blend_ref)))
    ]
    for copy in smalls:
        copy.start()
    mixing = spread_ref[...]

    def group(g, carry):
        sides = []
        for half in range(2):
            start = pl.multiple_of((2 * g + half) * CELLS_AT_ONCE, CELLS_AT_ONCE)
            for ref in (flux_ref, other_ref):
                sides.append(ref[:, pl.ds(start, CELLS_AT_ONCE), :].reshape(slabs * CELLS_AT_ONCE, ens))
        rhs = jnp.concatenate(
            [jnp.concatenate(sides[:2], axis=0), jnp.concatenate(sides[2:], axis=0)], axis=1
        )
        out = jnp.dot(mixing, rhs, preferred_element_type=F32).astype(BF16)
        for half in range(2):
            start = pl.multiple_of((2 * g + half) * CELLS_AT_ONCE, CELLS_AT_ONCE)
            panels[:, pl.ds(start, CELLS_AT_ONCE), :] = out[:, half * ens : (half + 1) * ens].reshape(
                slices, CELLS_AT_ONCE, ens
            )
        return carry

    lax.fori_loop(0, cells // (2 * CELLS_AT_ONCE), group, 0, unroll=16)

    group_size = regions // 2
    near = (me // group_size) * group_size
    far = group_size - near
    span = group_size * own_blocks

    tall = own_blocks * HALF

    def forward(targets):
        high_rows = len(targets) * tall
        acc[pl.ds(0, high_rows), :] = jnp.zeros((high_rows, 2 * ens), F32)

        def body(g, carry):
            left, right = [], []
            for u in range(AT_ONCE):
                start = (g * AT_ONCE + u) * q_blocks
                left.append(
                    jnp.concatenate(
                        [
                            dense_ref[pl.ds(start + to * own_blocks, own_blocks)].reshape(tall, 2 * BLOCK)
                            for to in targets
                        ],
                        axis=0,
                    )
                )
                cell = (u % cell_blocks) * BLOCK
                one = panels[g * (AT_ONCE // cell_blocks) + u // cell_blocks, cell : cell + BLOCK, :]
                right.append(both(one, one))
            acc[pl.ds(0, high_rows), :] += jnp.dot(
                jnp.concatenate(left, axis=1), jnp.concatenate(right, axis=0), preferred_element_type=F32
            )
            return carry

        lax.fori_loop(0, panel_total // AT_ONCE, body, 0)
        for k, to in enumerate(targets):
            for q in range(own_blocks):
                for par in range(2):
                    start = q * BLOCK + par * HALF
                    part[to, start : start + HALF, :] = acc[
                        k * tall + q * HALF : k * tall + (q + 1) * HALF, par * ens : (par + 1) * ens
                    ].astype(BF16)

    def reduce_copy(source, to):
        return pltpu.make_async_remote_copy(
            src_ref=part.at[to],
            dst_ref=got.at[source],
            send_sem=send_a.at[to],
            recv_sem=recv_a.at[source],
            device_id={"region": to},
            device_id_type=MESH,
        )

    def gather_copy(source, to):
        return pltpu.make_async_remote_copy(
            src_ref=all_ref.at[source],
            dst_ref=all_ref.at[source],
            send_sem=send_b.at[to],
            recv_sem=recv_b.at[source],
            device_id={"region": to},
            device_id_type=MESH,
        )

    pairs_half = group_size // 2
    height, side = me // 2, lax.rem(me, 2)
    offset = height - near // 2
    near_pairs = [near // 2 + lax.rem(offset + k, pairs_half) for k in range(pairs_half)]
    far_pairs = [far // 2 + lax.rem(2 * pairs_half - 1 - offset + k, pairs_half) for k in range(pairs_half)]
    nears = [2 * height + 1 - side]
    for pair in near_pairs[1:]:
        nears += [2 * pair + side, 2 * pair + 1 - side]
    fars = []
    for pair in far_pairs:
        fars += [2 * pair + side, 2 * pair + 1 - side]

    forward(fars)
    pl.semaphore_wait(barrier, regions)
    for peer in fars:
        reduce_copy(me, peer).start()
    forward([me] + nears)
    for peer in nears:
        reduce_copy(me, peer).start()

    lower = lax.broadcasted_iota(jnp.int32, (HALF, 2 * BLOCK), 1) < BLOCK

    def pair_up(g, carry):
        for k in range(2):
            for q in range(q_blocks):
                one = dense_ref[(4 * g + 2 * k) * q_blocks + q]
                two = dense_ref[(4 * g + 2 * k + 1) * q_blocks + q]
                swapped = halves_swapped(jnp.where(lower, two, one))
                tiles[2 * g + k, pl.ds(q * BLOCK, HALF), :] = jnp.where(lower, one, swapped)
                tiles[2 * g + k, pl.ds(q * BLOCK + HALF, HALF), :] = jnp.where(lower, swapped, two)
        return carry

    for copy in smalls:
        copy.wait()
    table = table_for(rows)
    obs = jnp.dot(table.astype(BF16), obs_ref[...], preferred_element_type=F32)
    inv = jnp.sum(jnp.where(table, inv_ref[...], 0.0), axis=1, keepdims=True)
    rounds = panel_total // 4
    lax.fori_loop(0, rounds // 2, pair_up, 0)

    evolved = part[me].astype(F32)
    for peer in nears + fars:
        reduce_copy(peer, me).wait_recv()
        evolved = evolved + got[peer].astype(F32)
    misfit = (inv * (evolved - obs)).astype(BF16)
    all_ref[me] = misfit.T
    for peer in fars + nears:
        gather_copy(me, peer).start()
    own_ref[...] = lax.dot_general(
        table.astype(BF16), misfit, (((0,), (0,)), ((), ())), preferred_element_type=F32
    ).astype(BF16)
    lax.fori_loop(rounds // 2, rounds, pair_up, 0)
    pulling = spread_own_first(blend_ref[...], CELLS_AT_ONCE, win, True)

    mix = mix_ref[...]
    columns = 2 * BLOCK
    steps = cells // columns

    def send(step):
        return pltpu.make_async_remote_copy(
            src_ref=away.at[step],
            dst_ref=pulled.at[step],
            send_sem=send_w.at[step],
            recv_sem=recv_w.at[step],
            device_id={"window": 1 - win},
            device_id_type=MESH,
        )

    def product(step, half, pair, turned):
        right = [
            tiles[(half * slabs + t) * steps + step, pl.ds(pl.multiple_of(pair * 2 * rows, rows), 2 * rows), :]
            for t in range(slabs)
        ]
        return jnp.dot(turned, jnp.concatenate(right, axis=1), preferred_element_type=F32)

    ordered = near_pairs + far_pairs
    for n, pair in enumerate(ordered):
        for near_side in (1 - side, side) if n else (1 - side,):
            gather_copy(2 * pair + near_side, me).wait_recv()
        turned = jnp.concatenate([all_ref[2 * pair], all_ref[2 * pair + 1]], axis=1)
        if n < len(ordered) - 1:
            for step in range(steps):
                for half in range(2):
                    out = product(step, half, pair, turned)
                    sums[step, half] = sums[step, half] + out if n else out

    def adjoint(step):
        for half in range(2):
            out = (sums[step, half] + product(step, half, ordered[-1], turned)).astype(BF16)
            for t in range(slabs):
                back[half * slabs + t] = out[:, t * columns : (t + 1) * columns]
        for e in range(0, ens, 2 * CELLS_AT_ONCE):
            rhs = jnp.concatenate(
                [
                    back[:, e + h * CELLS_AT_ONCE : e + (h + 1) * CELLS_AT_ONCE, :].reshape(
                        slices * CELLS_AT_ONCE, columns
                    )
                    for h in range(2)
                ],
                axis=1,
            )
            out = jnp.dot(pulling, rhs, preferred_element_type=F32).astype(BF16)
            for h in range(2):
                piece = out[:, h * columns : (h + 1) * columns].reshape(slices, CELLS_AT_ONCE, columns)
                at_e = e + h * CELLS_AT_ONCE
                mine[step, :, at_e : at_e + CELLS_AT_ONCE, :] = piece[:slabs]
                away[step, :, at_e : at_e + CELLS_AT_ONCE, :] = piece[slabs:]

    def finish(step):
        send(step).wait_recv()
        total = (mine[step].astype(F32) + pulled[step].astype(F32)).astype(BF16)
        if step == steps - 1:
            last_ref[...] = total
        else:
            grad_ref[:, step * columns : (step + 1) * columns, :] = mixed(total, mix)

    for step in range(steps):
        adjoint(step)
        send(step).start()
        if step >= DENSE_LAG:
            finish(step - DENSE_LAG)
    for step in range(steps - DENSE_LAG, steps):
        finish(step)
    for step in range(steps):
        send(step).wait_send()
    for peer in nears + fars:
        reduce_copy(me, peer).wait_send()
        gather_copy(me, peer).wait_send()


def dense_shards(
    regions,
    flux,
    blend,
    footprints,
    receptor_block,
    cell_block,
    slice_index,
    live_counts,
    observed,
    inv_var,
    prior_mix,
):
    slabs, cells, ens = flux.shape
    slices = blend.shape[0]
    cell_blocks = cells // BLOCK
    panel_total = slices * cell_blocks
    slots = footprints.shape[1]
    rows = observed.shape[1]
    window_blocks = rows // BLOCK * regions
    total = panel_total * window_blocks
    columns = 2 * BLOCK
    steps = cells // columns

    other = lax.ppermute(flux, "window", [(0, 1), (1, 0)])
    dense, kernels, near_flux = pl.pallas_call(
        functools.partial(place_kernel, window_blocks, cell_blocks),
        out_shape=(
            jax.ShapeDtypeStruct((total + 1, HALF, 2 * BLOCK), BF16),
            jax.ShapeDtypeStruct((slices * CELLS_AT_ONCE, slices * CELLS_AT_ONCE), BF16),
            jax.ShapeDtypeStruct((slabs, cells, ens), BF16),
        ),
        in_specs=[hbm()] * 3 + [pl.BlockSpec(memory_space=pltpu.SMEM)] + [hbm()] * 3,
        out_specs=(vmem(), vmem(), vmem()),
        scratch_shapes=[
            pltpu.VMEM((slots, BLOCK * BLOCK), BF16),
            pltpu.VMEM((1, slots), jnp.int32),
            pltpu.VMEM((1, slots), jnp.int32),
            pltpu.VMEM((1, slots), jnp.int32),
            pltpu.VMEM((slices, slices), F32),
            pltpu.VMEM((1, slots), jnp.int32),
            pltpu.SMEM((1, slots), jnp.int32),
            pltpu.VMEM((total // 8 + 1, HALF, 2 * BLOCK), F32),
            pltpu.SemaphoreType.DMA((4,)),
            pltpu.SemaphoreType.DMA((LOADS,)),
            pltpu.SemaphoreType.DMA((2,)),
        ],
        compiler_params=pltpu.CompilerParams(vmem_limit_bytes=DENSE_VMEM),
        cost_estimate=pl.CostEstimate(flops=0, bytes_accessed=24 << 20, transcendentals=0),
        name="place_blocks",
    )(stay(receptor_block), stay(cell_block), stay(slice_index), live_counts, stay(blend), stay(flux), stay(footprints))

    misfit, gradient, last, mix = pl.pallas_call(
        functools.partial(whole_kernel, regions),
        out_shape=(
            jax.ShapeDtypeStruct((rows, ens), BF16),
            jax.ShapeDtypeStruct((slabs, cells, ens), BF16),
            jax.ShapeDtypeStruct((slabs, ens, columns), BF16),
            jax.ShapeDtypeStruct(prior_mix.shape, BF16),
        ),
        in_specs=[vmem()] * 4 + [hbm()] * 4,
        out_specs=(vmem(), vmem(), vmem(), vmem()),
        scratch_shapes=[
            pltpu.VMEM((rows, ens), BF16),
            pltpu.VMEM((1, rows), F32),
            pltpu.VMEM((slices, slices), F32),
            pltpu.VMEM((slices, cells, ens), BF16),
            pltpu.VMEM((window_blocks // 2 * HALF, 2 * ens), F32),
            pltpu.VMEM((regions, rows, ens), BF16),
            pltpu.VMEM((regions, rows, ens), BF16),
            pltpu.VMEM((regions, ens, rows), BF16),
            pltpu.VMEM((panel_total // 2, window_blocks * BLOCK, columns), BF16),
            pltpu.VMEM((steps, 2, ens, slabs * columns), F32),
            pltpu.VMEM((slices, ens, columns), BF16),
            pltpu.VMEM((steps, slabs, ens, columns), BF16),
            pltpu.VMEM((steps, slabs, ens, columns), BF16),
            pltpu.VMEM((steps, slabs, ens, columns), BF16),
        ]
        + [pltpu.SemaphoreType.DMA((regions,))] * 4
        + [pltpu.SemaphoreType.DMA((steps,))] * 2
        + [pltpu.SemaphoreType.DMA((4,))],
        compiler_params=pltpu.CompilerParams(collective_id=3, has_side_effects=True, vmem_limit_bytes=DENSE_VMEM),
        name="transport",
    )(dense, near_flux, other, kernels, stay(observed[0]), stay(inv_var), stay(prior_mix), stay(blend))

    gradient, misfit = pl.pallas_call(
        final_kernel,
        out_shape=(
            jax.ShapeDtypeStruct((slabs, cells, ens), BF16),
            jax.ShapeDtypeStruct((rows, ens), BF16),
        ),
        in_specs=[vmem()] * 4,
        out_specs=(hbm(), hbm()),
        scratch_shapes=[pltpu.VMEM((slabs, columns, ens), BF16), pltpu.SemaphoreType.DMA((3,))],
        compiler_params=pltpu.CompilerParams(vmem_limit_bytes=4 << 20),
        name="final_mix",
    )(gradient, last, mix, misfit)
    return misfit[None], gradient


def solution(mesh):
    in_specs = (
        P(("group", "window"), "region", None),
        P(),
        P(("group", "window"), "region", None),
        P(("group", "window"), "region"),
        P(("group", "window"), "region"),
        P(("group", "window"), "region"),
        P(("group", "window"), "region"),
        P(("group", "window"), "region", None),
        P(("group", "window"), "region"),
        P(),
    )
    out_specs = (P(("group", "window"), "region", None), P(("group", "window"), "region", None))

    def either(*args):
        regions = mesh.shape["region"]
        blocks = args[7].shape[1] // BLOCK * regions
        return (dense_shards if blocks <= DENSE_BLOCKS and regions % 4 == 0 else shards)(regions, *args)

    return jax.shard_map(
        either,
        mesh=mesh,
        in_specs=in_specs,
        out_specs=out_specs,
        check_vma=False,
    )
```

```python
import functools

import jax
import jax.numpy as jnp
from jax import lax
from jax.experimental import pallas as pl
from jax.experimental.pallas import tpu as pltpu
from jax.sharding import PartitionSpec as P

BLOCK = 64
MESH = pl.DeviceIdType.MESH
F32 = jnp.float32
BF16 = jnp.bfloat16
SUB = 16
SUBS = 4
CELLS_AT_ONCE = 16
PIECES = 4
LOADS = 8
PAIRS = 32
TURNS = 32
LAG = 2
HALF = BLOCK // 2
CLEAR = 64
MOST = 16
DENSE_SUBS = 4
AT_ONCE = 32
DENSE_LAG = 3
DENSE_VMEM = 33 << 20
DENSE_BLOCKS = 16


def spread(matrix, width):
    size = matrix.shape[0]
    full = size * width
    row = lax.broadcasted_iota(jnp.int32, (full, size), 0)
    col = lax.broadcasted_iota(jnp.int32, (full, size), 1)
    pick = (row // width == col).astype(BF16)
    row_f = lax.broadcasted_iota(jnp.int32, (full, full), 0)
    col_f = lax.broadcasted_iota(jnp.int32, (full, full), 1)
    same = row_f % width == col_f % width
    high = matrix.astype(BF16)
    low = (matrix - high.astype(F32)).astype(BF16)
    parts = []
    for part in (high, low):
        tall = jnp.dot(pick, part, preferred_element_type=F32).astype(BF16)
        wide = lax.dot_general(tall, pick, (((1,), (1,)), ((), ())), preferred_element_type=F32)
        parts.append(jnp.where(same, wide, 0.0).astype(BF16))
    return parts


def halves_swapped(x):
    return pltpu.roll(x, BLOCK, 1)


def blend_kernel(
    window_blocks,
    recv_hbm,
    cell_hbm,
    slice_hbm,
    live_ref,
    blend_hbm,
    flux_hbm,
    fp_hbm,
    panels_ref,
    pairs_ref,
    index_ref,
    full,
    raw,
    blend_ref,
    recv_ref,
    cell_ref,
    slice_ref,
    small_sem,
    fp_sem,
    local_sem,
    send_sem,
    recv_sem,
):
    me = lax.axis_index("window")
    other = 1 - me
    slabs, cells, ens = flux_hbm.shape
    slices = panels_ref.shape[0]
    slots = raw.shape[0]
    barrier = pltpu.get_barrier_semaphore()
    pl.semaphore_signal(barrier, inc=1, device_id={"window": other}, device_id_type=MESH)
    smalls = [
        pltpu.make_async_copy(source, target, small_sem.at[k])
        for k, (source, target) in enumerate(
            ((blend_hbm, blend_ref), (recv_hbm, recv_ref), (cell_hbm, cell_ref), (slice_hbm, slice_ref))
        )
    ]
    for copy in smalls:
        copy.start()
    piece = cells // PIECES
    locals_, sends, loads = [], [], []
    for k in range(PIECES):
        span = pl.ds(k * piece, piece)
        locals_.append(
            pltpu.make_async_copy(
                flux_hbm.at[:, span, :], full.at[pl.ds(me * slabs, slabs), span, :], local_sem.at[k]
            )
        )
        locals_[-1].start()
    part = slots // LOADS
    for k in range(LOADS):
        span = pl.ds(k * part, part)
        loads.append(pltpu.make_async_copy(fp_hbm.at[0, span, :], raw.at[span, :], fp_sem.at[k]))
    loads[0].start()
    pl.semaphore_wait(barrier, 1)
    for k in range(PIECES):
        span = pl.ds(k * piece, piece)
        sends.append(
            pltpu.make_async_remote_copy(
                src_ref=flux_hbm.at[:, span, :],
                dst_ref=full.at[pl.ds(me * slabs, slabs), span, :],
                send_sem=send_sem.at[k],
                recv_sem=recv_sem.at[k],
                device_id={"window": other},
                device_id_type=MESH,
            )
        )
        sends[-1].start()
    for k in range(1, LOADS):
        loads[k].start()

    for copy in smalls:
        copy.wait()
    cell_blocks = cells // BLOCK
    live = lax.broadcasted_iota(jnp.int32, recv_ref.shape, 1) < live_ref[...]
    panel = slice_ref[...] * cell_blocks + cell_ref[...]
    index_ref[pl.ds(0, 1), :] = jnp.where(live, recv_ref[...], window_blocks)
    index_ref[pl.ds(1, 1), :] = jnp.where(live, panel, 0)
    index_ref[pl.ds(2, 1), :] = jnp.where(live, panel, slices * cell_blocks)
    index_ref[pl.ds(3, 1), :] = jnp.where(live, recv_ref[...], 0)
    high, low = spread(blend_ref[...], CELLS_AT_ONCE)

    def arrange(k):
        loads[k].wait()

        def body(g, carry):
            lower = lax.broadcasted_iota(jnp.int32, (BLOCK // 2, 2 * BLOCK), 1) < BLOCK
            for sub in range(SUBS):
                base = pl.multiple_of(k * part + g * SUBS * SUB + sub * SUB, SUB)
                x = raw[pl.ds(base, SUB), :].reshape(SUB, BLOCK // 2, 2 * BLOCK)
                for j in range(0, SUB, 2):
                    one, two = x[j], x[j + 1]
                    even = jnp.where(lower, one, halves_swapped(two))
                    odd = jnp.where(lower, halves_swapped(one), two)
                    place = k * (part // 2) + (g * SUBS + sub) * (SUB // 2) + j // 2
                    pairs_ref[place] = jnp.concatenate([even, odd], axis=0)
            return carry

        lax.fori_loop(0, part // SUB // SUBS, body, 0)

    for k in range(LOADS // 2):
        arrange(k)
    for k in range(PIECES):
        locals_[k].wait()
        sends[k].wait_recv()

        def group(g, carry, k=k):
            sides = []
            for half in range(2):
                start = pl.multiple_of(k * piece + g * 2 * CELLS_AT_ONCE + half * CELLS_AT_ONCE, CELLS_AT_ONCE)
                sides.append(full[:, pl.ds(start, CELLS_AT_ONCE), :].reshape(slices * CELLS_AT_ONCE, ens))
            rhs = jnp.concatenate(sides, axis=1)
            out = jnp.dot(high, rhs, preferred_element_type=F32) + jnp.dot(low, rhs, preferred_element_type=F32)
            out = out.astype(BF16)
            for half in range(2):
                start = pl.multiple_of(k * piece + g * 2 * CELLS_AT_ONCE + half * CELLS_AT_ONCE, CELLS_AT_ONCE)
                panels_ref[:, pl.ds(start, CELLS_AT_ONCE), :] = out[:, half * ens : (half + 1) * ens].reshape(
                    slices, CELLS_AT_ONCE, ens
                )
            return carry

        lax.fori_loop(0, piece // (2 * CELLS_AT_ONCE), group, 0, unroll=2)
    for k in range(LOADS // 2, LOADS):
        arrange(k)
    for k in range(PIECES):
        sends[k].wait_send()


def both(one, two):
    zero = jnp.zeros_like(one)
    return jnp.concatenate(
        [jnp.concatenate([one, zero], axis=1), jnp.concatenate([zero, two], axis=1)], axis=0
    )


def products(index_ref, left_ref, right_ref, acc, to, source):
    acc[...] = jnp.zeros_like(acc)
    ens = acc.shape[2]

    def body(g, carry):
        for j in range(PAIRS):
            pair = g * PAIRS + j
            one = right_ref[index_ref[source, 2 * pair]]
            two = right_ref[index_ref[source, 2 * pair + 1]]
            out = jnp.dot(left_ref[pair], both(one, two), preferred_element_type=F32)
            acc[index_ref[to, 2 * pair]] += out[:, :ens]
            acc[index_ref[to, 2 * pair + 1]] += out[:, ens:]
        return carry

    lax.fori_loop(0, left_ref.shape[0] // PAIRS, body, 0)


def forward_kernel(index_ref, pairs_ref, panels_ref, part_ref, acc):
    products(index_ref, pairs_ref, panels_ref, acc, 0, 1)
    part_ref[...] = acc[pl.ds(0, part_ref.shape[0])].astype(BF16)


def turned_pair(x):
    t = x.T
    return jnp.concatenate([t[:BLOCK], t[BLOCK:]], axis=1)


def exchange_kernel(
    regions, part_ref, obs_ref, inv_ref, pairs_ref, all_ref, own_ref, turned_ref, got, send_a, recv_a, send_b, recv_b, send_c, recv_c
):
    me = lax.axis_index("region")
    rows, ens = obs_ref.shape
    barrier = pltpu.get_barrier_semaphore()
    for k in range(1, regions):
        peer = lax.rem(me + k, regions)
        pl.semaphore_signal(barrier, inc=1, device_id={"region": peer}, device_id_type=MESH)
    row = lax.broadcasted_iota(jnp.int32, (rows, rows), 0)
    col = lax.broadcasted_iota(jnp.int32, (rows, rows), 1)
    inner = row % BLOCK
    half = BLOCK // 2
    picked = (row // BLOCK) * BLOCK + (inner % half) * 2 + inner // half == col
    table = picked.astype(BF16)
    obs = jnp.dot(table, obs_ref[...], preferred_element_type=F32)
    inv = jnp.sum(jnp.where(picked, inv_ref[...], 0.0), axis=1, keepdims=True)
    pl.semaphore_wait(barrier, regions - 1)

    def first(k):
        peer = lax.rem(me + k, regions)
        return pltpu.make_async_remote_copy(
            src_ref=part_ref.at[peer],
            dst_ref=got.at[k],
            send_sem=send_a.at[k],
            recv_sem=recv_a.at[k],
            device_id={"region": peer},
            device_id_type=MESH,
        )

    width = 2 if regions % 2 == 0 else 1
    count = regions // width
    high, low = me // width, lax.rem(me, width)

    def at(k, low):
        return lax.rem(high + count - k, count) * width + low

    def along(k, source):
        return pltpu.make_async_remote_copy(
            src_ref=all_ref.at[source],
            dst_ref=all_ref.at[source],
            send_sem=send_b.at[k],
            recv_sem=recv_b.at[k],
            device_id={"region": lax.rem(high + k, count) * width + low},
            device_id_type=MESH,
        )

    def across(k, source):
        return pltpu.make_async_remote_copy(
            src_ref=all_ref.at[source],
            dst_ref=all_ref.at[source],
            send_sem=send_c.at[k],
            recv_sem=recv_c.at[k],
            device_id={"region": high * width + 1 - low},
            device_id_type=MESH,
        )

    firsts = [first(k) for k in range(1, regions)]
    for copy in firsts:
        copy.start()

    pair_count = pairs_ref.shape[0]

    def turn(g, carry):
        for j in range(TURNS):
            turned_ref[g * TURNS + j] = turned_pair(pairs_ref[g * TURNS + j])
        return carry

    rounds = pair_count // TURNS
    lax.fori_loop(0, rounds // 2, turn, 0)
    evolved = part_ref[me].astype(F32)
    for k in range(1, regions):
        firsts[k - 1].wait_recv()
        evolved = evolved + got[k].astype(F32)
    misfit = (inv * (evolved - obs)).astype(BF16)
    all_ref[me] = misfit
    seconds = [along(k, me) for k in range(1, count)]
    for copy in seconds:
        copy.start()
    if width == 2:
        seconds.append(across(0, me))
        seconds[-1].start()
    own_ref[...] = lax.dot_general(
        table, misfit, (((0,), (0,)), ((), ())), preferred_element_type=F32
    ).astype(BF16)
    lax.fori_loop(rounds // 2, rounds * 3 // 4, turn, 0)
    for k in range(1, count):
        along(k, at(k, low)).wait_recv()
        if width == 2:
            seconds.append(across(k, at(k, low)))
            seconds[-1].start()
    lax.fori_loop(rounds * 3 // 4, rounds, turn, 0)
    if width == 2:
        for k in range(count):
            across(k, at(k, 1 - low)).wait_recv()
    for copy in firsts + seconds:
        copy.wait_send()


def adjoint_kernel(index_ref, turned_ref, misfit_ref, own_ref, acc, misfit_out):
    products(index_ref, turned_ref, misfit_ref, acc, 2, 3)
    misfit_out[...] = own_ref[...]


def gradient_kernel(acc_ref, blend_ref, mix_ref, grad_ref, mine, away, got, send_sem, recv_sem):
    me = lax.axis_index("window")
    other = 1 - me
    slabs, cells, ens = grad_ref.shape
    slices = 2 * slabs
    blocks = cells // BLOCK
    barrier = pltpu.get_barrier_semaphore()
    pl.semaphore_signal(barrier, inc=1, device_id={"window": other}, device_id_type=MESH)
    high, low = spread(blend_ref[...], CELLS_AT_ONCE)
    mix = mix_ref[...]
    pl.semaphore_wait(barrier, 1)

    def send(block):
        return pltpu.make_async_remote_copy(
            src_ref=away.at[block],
            dst_ref=got.at[block],
            send_sem=send_sem.at[block],
            recv_sem=recv_sem.at[block],
            device_id={"window": other},
            device_id_type=MESH,
        )

    def pull(block):
        for within in range(BLOCK // (2 * CELLS_AT_ONCE)):
            sides = []
            for half in range(2):
                start = (2 * within + half) * CELLS_AT_ONCE
                rows = [acc_ref[t * blocks + block, pl.ds(start, CELLS_AT_ONCE), :] for t in range(slices)]
                sides.append(jnp.concatenate(rows, axis=0))
            rhs = jnp.concatenate(sides, axis=1)
            rhs_high = rhs.astype(BF16)
            rhs_low = (rhs - rhs_high.astype(F32)).astype(BF16)
            dims = (((0,), (0,)), ((), ()))
            out = lax.dot_general(high, rhs_high, dims, preferred_element_type=F32)
            out = out + lax.dot_general(low, rhs_high, dims, preferred_element_type=F32)
            out = (out + lax.dot_general(high, rhs_low, dims, preferred_element_type=F32)).astype(BF16)
            for half in range(2):
                start = (2 * within + half) * CELLS_AT_ONCE
                piece = out[:, half * ens : (half + 1) * ens].reshape(slices, CELLS_AT_ONCE, ens)
                first, second = piece[:slabs], piece[slabs:]
                mine[block, :, pl.ds(start, CELLS_AT_ONCE), :] = jnp.where(me == 0, first, second)
                away[block, :, pl.ds(start, CELLS_AT_ONCE), :] = jnp.where(me == 0, second, first)

    def finish(block):
        send(block).wait_recv()
        total = (mine[block].astype(F32) + got[block].astype(F32)).astype(BF16).reshape(slabs * BLOCK, ens)
        grad = jnp.dot(total, mix, preferred_element_type=F32).astype(BF16)
        grad_ref[:, pl.ds(block * BLOCK, BLOCK), :] = grad.reshape(slabs, BLOCK, ens)

    for block in range(blocks):
        pull(block)
        send(block).start()
        if block >= LAG:
            finish(block - LAG)
    for block in range(blocks - LAG, blocks):
        finish(block)
    for block in range(blocks):
        send(block).wait_send()


def vmem():
    return pl.BlockSpec(memory_space=pltpu.VMEM)


def hbm():
    return pl.BlockSpec(memory_space=pltpu.HBM)


def stay(x):
    return pltpu.with_memory_space_constraint(x, pltpu.HBM)


def shards(
    regions,
    flux,
    blend,
    footprints,
    receptor_block,
    cell_block,
    slice_index,
    live_counts,
    observed,
    inv_var,
    prior_mix,
):
    slabs, cells, ens = flux.shape
    slices = blend.shape[0]
    cell_blocks = cells // BLOCK
    panel_total = slices * cell_blocks
    slots = footprints.shape[1]
    rows = observed.shape[1]
    own_blocks = rows // BLOCK
    window_blocks = own_blocks * regions

    panels, pairs, index = pl.pallas_call(
        functools.partial(blend_kernel, window_blocks),
        out_shape=(
            jax.ShapeDtypeStruct((slices, cells, ens), BF16),
            jax.ShapeDtypeStruct((slots // 2, BLOCK, 2 * BLOCK), BF16),
            jax.ShapeDtypeStruct((4, slots), jnp.int32),
        ),
        in_specs=[hbm()] * 3 + [vmem()] + [hbm()] * 3,
        out_specs=(vmem(), vmem(), vmem()),
        scratch_shapes=[
            pltpu.VMEM((slices, cells, ens), BF16),
            pltpu.VMEM((slots, BLOCK * BLOCK), BF16),
            pltpu.VMEM((slices, slices), F32),
            pltpu.VMEM((1, slots), jnp.int32),
            pltpu.VMEM((1, slots), jnp.int32),
            pltpu.VMEM((1, slots), jnp.int32),
            pltpu.SemaphoreType.DMA((4,)),
            pltpu.SemaphoreType.DMA((LOADS,)),
            pltpu.SemaphoreType.DMA((PIECES,)),
            pltpu.SemaphoreType.DMA((PIECES,)),
            pltpu.SemaphoreType.DMA((PIECES,)),
        ],
        compiler_params=pltpu.CompilerParams(collective_id=0, has_side_effects=True, vmem_limit_bytes=24 << 20),
        name="blend_slices",
    )(
        stay(receptor_block),
        stay(cell_block),
        stay(slice_index),
        live_counts,
        stay(blend),
        stay(flux),
        stay(footprints),
    )

    smem = pl.BlockSpec(memory_space=pltpu.SMEM)
    part = pl.pallas_call(
        forward_kernel,
        out_shape=jax.ShapeDtypeStruct((window_blocks, BLOCK, ens), BF16),
        in_specs=[smem, vmem(), vmem()],
        out_specs=vmem(),
        scratch_shapes=[pltpu.VMEM((window_blocks + 1, BLOCK, ens), F32)],
        compiler_params=pltpu.CompilerParams(vmem_limit_bytes=16 << 20),
        name="forward_blocks",
    )(index, pairs, panels.reshape(panel_total, BLOCK, ens))

    misfit_all, own, turned = pl.pallas_call(
        functools.partial(exchange_kernel, regions),
        out_shape=(
            jax.ShapeDtypeStruct((regions, rows, ens), BF16),
            jax.ShapeDtypeStruct((rows, ens), BF16),
            jax.ShapeDtypeStruct((slots // 2, BLOCK, 2 * BLOCK), BF16),
        ),
        in_specs=[vmem()] * 4,
        out_specs=(vmem(), vmem(), vmem()),
        scratch_shapes=[
            pltpu.VMEM((regions, rows, ens), BF16),
            pltpu.SemaphoreType.DMA((regions,)),
            pltpu.SemaphoreType.DMA((regions,)),
            pltpu.SemaphoreType.DMA((regions,)),
            pltpu.SemaphoreType.DMA((regions,)),
            pltpu.SemaphoreType.DMA((regions,)),
            pltpu.SemaphoreType.DMA((regions,)),
        ],
        compiler_params=pltpu.CompilerParams(collective_id=1, has_side_effects=True, vmem_limit_bytes=16 << 20),
        name="misfit_exchange",
    )(part.reshape(regions, rows, ens), observed[0], inv_var, pairs)

    collected, misfit = pl.pallas_call(
        adjoint_kernel,
        out_shape=(
            jax.ShapeDtypeStruct((panel_total + 1, BLOCK, ens), F32),
            jax.ShapeDtypeStruct((rows, ens), BF16),
        ),
        in_specs=[smem, vmem(), vmem(), vmem()],
        out_specs=(vmem(), vmem()),
        compiler_params=pltpu.CompilerParams(vmem_limit_bytes=16 << 20),
        name="adjoint_blocks",
    )(index, turned, misfit_all.reshape(window_blocks, BLOCK, ens), own)

    blocks_shape = (cell_blocks, slabs, BLOCK, ens)
    gradient = pl.pallas_call(
        gradient_kernel,
        out_shape=jax.ShapeDtypeStruct((slabs, cells, ens), BF16),
        in_specs=[vmem(), vmem(), vmem()],
        out_specs=vmem(),
        scratch_shapes=[
            pltpu.VMEM(blocks_shape, BF16),
            pltpu.VMEM(blocks_shape, BF16),
            pltpu.VMEM(blocks_shape, BF16),
            pltpu.SemaphoreType.DMA((cell_blocks,)),
            pltpu.SemaphoreType.DMA((cell_blocks,)),
        ],
        compiler_params=pltpu.CompilerParams(collective_id=2, has_side_effects=True, vmem_limit_bytes=16 << 20),
        name="gradient_exchange",
    )(collected, blend, prior_mix)
    return misfit[None], gradient


def table_for(rows):
    row = lax.broadcasted_iota(jnp.int32, (rows, rows), 0)
    col = lax.broadcasted_iota(jnp.int32, (rows, rows), 1)
    inner = row % BLOCK
    return (row // BLOCK) * BLOCK + (inner % HALF) * 2 + inner // HALF == col


def spread_own_first(matrix, width, me, pulling):
    size = matrix.shape[0]
    full = size * width
    row = lax.broadcasted_iota(jnp.int32, (full, size), 0) // width
    col = lax.broadcasted_iota(jnp.int32, (full, size), 1)
    pick = (row == col).astype(BF16)
    pick_own = ((row + me * (size // 2)) % size == col).astype(BF16)
    row_f = lax.broadcasted_iota(jnp.int32, (full, full), 0)
    col_f = lax.broadcasted_iota(jnp.int32, (full, full), 1)
    same = row_f % width == col_f % width
    part = matrix.astype(BF16)
    nt = (((1,), (1,)), ((), ()))
    if pulling:
        tall = lax.dot_general(pick_own, part, nt, preferred_element_type=F32).astype(BF16)
        wide = lax.dot_general(tall, pick, nt, preferred_element_type=F32)
    else:
        tall = jnp.dot(pick, part, preferred_element_type=F32).astype(BF16)
        wide = lax.dot_general(tall, pick_own, nt, preferred_element_type=F32)
    return jnp.where(same, wide, 0.0).astype(BF16)


def slot_rows(raw, base):
    tiles = [raw[pl.ds(base, SUB), i * 2 * BLOCK : (i + 1) * 2 * BLOCK] for i in range(HALF)]
    return jnp.transpose(jnp.stack(tiles, axis=0), (1, 0, 2))


def place_kernel(
    window_blocks,
    cell_blocks,
    recv_hbm,
    cell_hbm,
    slice_hbm,
    live_ref,
    blend_hbm,
    flux_hbm,
    fp_hbm,
    dense_ref,
    spread_ref,
    flux_ref,
    raw,
    recv_ref,
    cell_ref,
    slice_ref,
    blend_ref,
    dest_ref,
    dest_smem,
    sums,
    small_sem,
    fp_sem,
    dest_sem,
):
    slots = raw.shape[0]
    total = dense_ref.shape[0] - 1
    panels = total // window_blocks
    smalls = [
        pltpu.make_async_copy(source, target, small_sem.at[k])
        for k, (source, target) in enumerate(
            (
                (recv_hbm, recv_ref),
                (cell_hbm, cell_ref),
                (slice_hbm, slice_ref),
                (blend_hbm, blend_ref),
            )
        )
    ]
    for copy in smalls:
        copy.start()
    part = slots // LOADS
    loads = []
    for k in range(LOADS):
        span = pl.ds(k * part, part)
        loads.append(pltpu.make_async_copy(fp_hbm.at[0, span, :], raw.at[span, :], fp_sem.at[k]))
        loads[-1].start()

    flux_copy = pltpu.make_async_copy(flux_hbm, flux_ref, dest_sem.at[1])
    flux_copy.start()

    def clear(g, carry):
        dense_ref[pl.ds(g * CLEAR, CLEAR)] = jnp.zeros((CLEAR,) + dense_ref.shape[1:], BF16)
        return carry

    lax.fori_loop(0, total // CLEAR // 2, clear, 0)
    dense_ref[total] = jnp.zeros(dense_ref.shape[1:], BF16)
    for copy in smalls:
        copy.wait()
    live = lax.broadcasted_iota(jnp.int32, recv_ref.shape, 1) < live_ref[0, 0]
    panel = slice_ref[...] * cell_blocks + cell_ref[...]
    dest_ref[...] = jnp.where(live, panel * window_blocks + recv_ref[...], total)
    index = pltpu.make_async_copy(dest_ref, dest_smem, dest_sem.at[0])
    index.start()
    spread_ref[...] = spread_own_first(blend_ref[...], CELLS_AT_ONCE, lax.axis_index("window"), False)
    row = lax.broadcasted_iota(jnp.int32, (panels, slots), 0)
    named = (row == jnp.where(live, panel, -1)).astype(BF16)
    row = lax.broadcasted_iota(jnp.int32, (window_blocks, slots), 0)
    heard = (row == recv_ref[...]).astype(BF16)
    counts = lax.dot_general(named, heard, (((1,), (1,)), ((), ())), preferred_element_type=F32)
    most = jnp.max(counts)
    lax.fori_loop(total // CLEAR // 2, total // CLEAR, clear, 0)
    index.wait()
    flux_copy.wait()

    @pl.when(most <= MOST)
    def _():
        for k in range(LOADS):
            loads[k].wait()

            def body(g, carry):
                for sub in range(DENSE_SUBS):
                    base = pl.multiple_of(k * part + (g * DENSE_SUBS + sub) * SUB, SUB)
                    x = slot_rows(raw, base)
                    for j in range(0, SUB, 2):
                        one, two = dest_smem[0, base + j], dest_smem[0, base + j + 1]
                        first, second = dense_ref[one], dense_ref[two]
                        again = jnp.where(one == two, x[j], jnp.zeros_like(x[j]))
                        dense_ref[one] = first + x[j]
                        dense_ref[two] = second + again + x[j + 1]
                return carry

            lax.fori_loop(0, part // SUB // DENSE_SUBS, body, 0)

    @pl.when(most > MOST)
    def _():
        for k in range(LOADS):
            loads[k].wait()
        chunk = sums.shape[0] - 1

        def span(c, carry):
            sums[...] = jnp.zeros_like(sums)

            def body(g, carry):
                base = pl.multiple_of(g * SUB, SUB)
                x = slot_rows(raw, base)
                for j in range(SUB):
                    to = dest_smem[0, base + j] - c * chunk
                    to = jnp.where((to >= 0) & (to < chunk), to, chunk)
                    sums[to] += x[j].astype(F32)
                return carry

            lax.fori_loop(0, slots // SUB, body, 0)

            def store(g, carry):
                dense_ref[c * chunk + g] = sums[g].astype(BF16)
                return carry

            lax.fori_loop(0, chunk, store, 0)
            return carry

        lax.fori_loop(0, total // chunk, span, 0)


def final_kernel(grad_ref, last_ref, mix_ref, own_ref, grad_hbm, own_hbm, flat, sem):
    slabs, cells, ens = grad_ref.shape
    columns = last_ref.shape[2]
    early = cells - columns
    done = pltpu.make_async_copy(grad_ref.at[:, pl.ds(0, early), :], grad_hbm.at[:, pl.ds(0, early), :], sem.at[0])
    done.start()
    own = pltpu.make_async_copy(own_ref, own_hbm, sem.at[1])
    own.start()
    flat[...] = mixed(last_ref[...], mix_ref[...])
    rest = pltpu.make_async_copy(flat, grad_hbm.at[:, pl.ds(early, columns), :], sem.at[2])
    rest.start()
    done.wait()
    own.wait()
    rest.wait()


def mixed(total, mix):
    slabs, ens, columns = total.shape
    flat = jnp.concatenate([total[s].T for s in range(slabs)], axis=0)
    return jnp.dot(flat, mix, preferred_element_type=F32).astype(BF16).reshape(slabs, columns, ens)


def whole_kernel(
    regions,
    dense_ref,
    flux_ref,
    other_ref,
    spread_ref,
    obs_hbm,
    inv_hbm,
    mix_hbm,
    blend_hbm,
    own_ref,
    grad_ref,
    last_ref,
    mix_ref,
    obs_ref,
    inv_ref,
    blend_ref,
    panels,
    acc,
    part,
    got,
    all_ref,
    tiles,
    sums,
    back,
    mine,
    away,
    pulled,
    send_a,
    recv_a,
    send_b,
    recv_b,
    send_w,
    recv_w,
    small_sem,
):
    me = lax.axis_index("region")
    win = lax.axis_index("window")
    rows, ens = obs_ref.shape
    slabs, cells, _ = flux_ref.shape
    slices = 2 * slabs
    own_blocks = rows // BLOCK
    q_blocks = own_blocks * regions
    cell_blocks = cells // BLOCK
    panel_total = slices * cell_blocks

    barrier = pltpu.get_barrier_semaphore()
    for k in range(1, regions):
        peer = lax.rem(me + k, regions)
        pl.semaphore_signal(barrier, inc=1, device_id={"region": peer}, device_id_type=MESH)
    pl.semaphore_signal(barrier, inc=1, device_id={"window": 1 - win}, device_id_type=MESH)

    smalls = [
        pltpu.make_async_copy(source, target, small_sem.at[k])
        for k, (source, target) in enumerate(((obs_hbm, obs_ref), (inv_hbm, inv_ref), (mix_hbm, mix_ref), (blend_hbm, blend_ref)))
    ]
    for copy in smalls:
        copy.start()
    mixing = spread_ref[...]

    def group(g, carry):
        sides = []
        for half in range(2):
            start = pl.multiple_of((2 * g + half) * CELLS_AT_ONCE, CELLS_AT_ONCE)
            for ref in (flux_ref, other_ref):
                sides.append(ref[:, pl.ds(start, CELLS_AT_ONCE), :].reshape(slabs * CELLS_AT_ONCE, ens))
        rhs = jnp.concatenate(
            [jnp.concatenate(sides[:2], axis=0), jnp.concatenate(sides[2:], axis=0)], axis=1
        )
        out = jnp.dot(mixing, rhs, preferred_element_type=F32).astype(BF16)
        for half in range(2):
            start = pl.multiple_of((2 * g + half) * CELLS_AT_ONCE, CELLS_AT_ONCE)
            panels[:, pl.ds(start, CELLS_AT_ONCE), :] = out[:, half * ens : (half + 1) * ens].reshape(
                slices, CELLS_AT_ONCE, ens
            )
        return carry

    lax.fori_loop(0, cells // (2 * CELLS_AT_ONCE), group, 0, unroll=16)

    group_size = regions // 2
    near = (me // group_size) * group_size
    far = group_size - near
    span = group_size * own_blocks

    tall = own_blocks * HALF

    def forward(targets):
        high_rows = len(targets) * tall
        acc[pl.ds(0, high_rows), :] = jnp.zeros((high_rows, 2 * ens), F32)

        def body(g, carry):
            left, right = [], []
            for u in range(AT_ONCE):
                start = (g * AT_ONCE + u) * q_blocks
                left.append(
                    jnp.concatenate(
                        [
                            dense_ref[pl.ds(start + to * own_blocks, own_blocks)].reshape(tall, 2 * BLOCK)
                            for to in targets
                        ],
                        axis=0,
                    )
                )
                cell = (u % cell_blocks) * BLOCK
                one = panels[g * (AT_ONCE // cell_blocks) + u // cell_blocks, cell : cell + BLOCK, :]
                right.append(both(one, one))
            acc[pl.ds(0, high_rows), :] += jnp.dot(
                jnp.concatenate(left, axis=1), jnp.concatenate(right, axis=0), preferred_element_type=F32
            )
            return carry

        lax.fori_loop(0, panel_total // AT_ONCE, body, 0)
        for k, to in enumerate(targets):
            for q in range(own_blocks):
                for par in range(2):
                    start = q * BLOCK + par * HALF
                    part[to, start : start + HALF, :] = acc[
                        k * tall + q * HALF : k * tall + (q + 1) * HALF, par * ens : (par + 1) * ens
                    ].astype(BF16)

    def reduce_copy(source, to):
        return pltpu.make_async_remote_copy(
            src_ref=part.at[to],
            dst_ref=got.at[source],
            send_sem=send_a.at[to],
            recv_sem=recv_a.at[source],
            device_id={"region": to},
            device_id_type=MESH,
        )

    def gather_copy(source, to):
        return pltpu.make_async_remote_copy(
            src_ref=all_ref.at[source],
            dst_ref=all_ref.at[source],
            send_sem=send_b.at[to],
            recv_sem=recv_b.at[source],
            device_id={"region": to},
            device_id_type=MESH,
        )

    pairs_half = group_size // 2
    height, side = me // 2, lax.rem(me, 2)
    offset = height - near // 2
    near_pairs = [near // 2 + lax.rem(offset + k, pairs_half) for k in range(pairs_half)]
    far_pairs = [far // 2 + lax.rem(2 * pairs_half - 1 - offset + k, pairs_half) for k in range(pairs_half)]
    nears = [2 * height + 1 - side]
    for pair in near_pairs[1:]:
        nears += [2 * pair + side, 2 * pair + 1 - side]
    fars = []
    for pair in far_pairs:
        fars += [2 * pair + side, 2 * pair + 1 - side]

    forward(fars)
    pl.semaphore_wait(barrier, regions)
    for peer in fars:
        reduce_copy(me, peer).start()
    forward([me] + nears)
    for peer in nears:
        reduce_copy(me, peer).start()

    lower = lax.broadcasted_iota(jnp.int32, (HALF, 2 * BLOCK), 1) < BLOCK

    def pair_up(g, carry):
        for k in range(2):
            for q in range(q_blocks):
                one = dense_ref[(4 * g + 2 * k) * q_blocks + q]
                two = dense_ref[(4 * g + 2 * k + 1) * q_blocks + q]
                swapped = halves_swapped(jnp.where(lower, two, one))
                tiles[2 * g + k, pl.ds(q * BLOCK, HALF), :] = jnp.where(lower, one, swapped)
                tiles[2 * g + k, pl.ds(q * BLOCK + HALF, HALF), :] = jnp.where(lower, swapped, two)
        return carry

    for copy in smalls:
        copy.wait()
    table = table_for(rows)
    obs = jnp.dot(table.astype(BF16), obs_ref[...], preferred_element_type=F32)
    inv = jnp.sum(jnp.where(table, inv_ref[...], 0.0), axis=1, keepdims=True)
    rounds = panel_total // 4
    lax.fori_loop(0, rounds // 2, pair_up, 0)

    evolved = part[me].astype(F32)
    for peer in nears + fars:
        reduce_copy(peer, me).wait_recv()
        evolved = evolved + got[peer].astype(F32)
    misfit = (inv * (evolved - obs)).astype(BF16)
    all_ref[me] = misfit.T
    for peer in fars + nears:
        gather_copy(me, peer).start()
    own_ref[...] = lax.dot_general(
        table.astype(BF16), misfit, (((0,), (0,)), ((), ())), preferred_element_type=F32
    ).astype(BF16)
    lax.fori_loop(rounds // 2, rounds, pair_up, 0)
    pulling = spread_own_first(blend_ref[...], CELLS_AT_ONCE, win, True)

    mix = mix_ref[...]
    columns = 2 * BLOCK
    steps = cells // columns

    def send(step):
        return pltpu.make_async_remote_copy(
            src_ref=away.at[step],
            dst_ref=pulled.at[step],
            send_sem=send_w.at[step],
            recv_sem=recv_w.at[step],
            device_id={"window": 1 - win},
            device_id_type=MESH,
        )

    def product(step, half, pair, turned):
        right = [
            tiles[(half * slabs + t) * steps + step, pl.ds(pl.multiple_of(pair * 2 * rows, rows), 2 * rows), :]
            for t in range(slabs)
        ]
        return jnp.dot(turned, jnp.concatenate(right, axis=1), preferred_element_type=F32)

    ordered = near_pairs + far_pairs
    for n, pair in enumerate(ordered):
        for near_side in (1 - side, side) if n else (1 - side,):
            gather_copy(2 * pair + near_side, me).wait_recv()
        turned = jnp.concatenate([all_ref[2 * pair], all_ref[2 * pair + 1]], axis=1)
        if n < len(ordered) - 1:
            for step in range(steps):
                for half in range(2):
                    out = product(step, half, pair, turned)
                    sums[step, half] = sums[step, half] + out if n else out

    def adjoint(step):
        for half in range(2):
            out = (sums[step, half] + product(step, half, ordered[-1], turned)).astype(BF16)
            for t in range(slabs):
                back[half * slabs + t] = out[:, t * columns : (t + 1) * columns]
        for e in range(0, ens, 4 * CELLS_AT_ONCE):
            rhs = jnp.concatenate(
                [
                    back[:, e + h * CELLS_AT_ONCE : e + (h + 1) * CELLS_AT_ONCE, :].reshape(
                        slices * CELLS_AT_ONCE, columns
                    )
                    for h in range(4)
                ],
                axis=1,
            )
            out = jnp.dot(pulling, rhs, preferred_element_type=F32).astype(BF16)
            for h in range(4):
                piece = out[:, h * columns : (h + 1) * columns].reshape(slices, CELLS_AT_ONCE, columns)
                at_e = e + h * CELLS_AT_ONCE
                mine[step, :, at_e : at_e + CELLS_AT_ONCE, :] = piece[:slabs]
                away[step, :, at_e : at_e + CELLS_AT_ONCE, :] = piece[slabs:]

    def finish(step):
        send(step).wait_recv()
        total = (mine[step].astype(F32) + pulled[step].astype(F32)).astype(BF16)
        if step == steps - 1:
            last_ref[...] = total
        else:
            grad_ref[:, step * columns : (step + 1) * columns, :] = mixed(total, mix)

    for step in range(steps):
        adjoint(step)
        send(step).start()
        if step >= DENSE_LAG:
            finish(step - DENSE_LAG)
    for step in range(steps - DENSE_LAG, steps):
        finish(step)
    for step in range(steps):
        send(step).wait_send()
    for peer in nears + fars:
        reduce_copy(me, peer).wait_send()
        gather_copy(me, peer).wait_send()


def dense_shards(
    regions,
    flux,
    blend,
    footprints,
    receptor_block,
    cell_block,
    slice_index,
    live_counts,
    observed,
    inv_var,
    prior_mix,
):
    slabs, cells, ens = flux.shape
    slices = blend.shape[0]
    cell_blocks = cells // BLOCK
    panel_total = slices * cell_blocks
    slots = footprints.shape[1]
    rows = observed.shape[1]
    window_blocks = rows // BLOCK * regions
    total = panel_total * window_blocks
    columns = 2 * BLOCK
    steps = cells // columns

    other = lax.ppermute(flux, "window", [(0, 1), (1, 0)])
    dense, kernels, near_flux = pl.pallas_call(
        functools.partial(place_kernel, window_blocks, cell_blocks),
        out_shape=(
            jax.ShapeDtypeStruct((total + 1, HALF, 2 * BLOCK), BF16),
            jax.ShapeDtypeStruct((slices * CELLS_AT_ONCE, slices * CELLS_AT_ONCE), BF16),
            jax.ShapeDtypeStruct((slabs, cells, ens), BF16),
        ),
        in_specs=[hbm()] * 3 + [pl.BlockSpec(memory_space=pltpu.SMEM)] + [hbm()] * 3,
        out_specs=(vmem(), vmem(), vmem()),
        scratch_shapes=[
            pltpu.VMEM((slots, BLOCK * BLOCK), BF16),
            pltpu.VMEM((1, slots), jnp.int32),
            pltpu.VMEM((1, slots), jnp.int32),
            pltpu.VMEM((1, slots), jnp.int32),
            pltpu.VMEM((slices, slices), F32),
            pltpu.VMEM((1, slots), jnp.int32),
            pltpu.SMEM((1, slots), jnp.int32),
            pltpu.VMEM((total // 8 + 1, HALF, 2 * BLOCK), F32),
            pltpu.SemaphoreType.DMA((4,)),
            pltpu.SemaphoreType.DMA((LOADS,)),
            pltpu.SemaphoreType.DMA((2,)),
        ],
        compiler_params=pltpu.CompilerParams(vmem_limit_bytes=DENSE_VMEM),
        cost_estimate=pl.CostEstimate(flops=0, bytes_accessed=24 << 20, transcendentals=0),
        name="place_blocks",
    )(stay(receptor_block), stay(cell_block), stay(slice_index), live_counts, stay(blend), stay(flux), stay(footprints))

    misfit, gradient, last, mix = pl.pallas_call(
        functools.partial(whole_kernel, regions),
        out_shape=(
            jax.ShapeDtypeStruct((rows, ens), BF16),
            jax.ShapeDtypeStruct((slabs, cells, ens), BF16),
            jax.ShapeDtypeStruct((slabs, ens, columns), BF16),
            jax.ShapeDtypeStruct(prior_mix.shape, BF16),
        ),
        in_specs=[vmem()] * 4 + [hbm()] * 4,
        out_specs=(vmem(), vmem(), vmem(), vmem()),
        scratch_shapes=[
            pltpu.VMEM((rows, ens), BF16),
            pltpu.VMEM((1, rows), F32),
            pltpu.VMEM((slices, slices), F32),
            pltpu.VMEM((slices, cells, ens), BF16),
            pltpu.VMEM((window_blocks // 2 * HALF, 2 * ens), F32),
            pltpu.VMEM((regions, rows, ens), BF16),
            pltpu.VMEM((regions, rows, ens), BF16),
            pltpu.VMEM((regions, ens, rows), BF16),
            pltpu.VMEM((panel_total // 2, window_blocks * BLOCK, columns), BF16),
            pltpu.VMEM((steps, 2, ens, slabs * columns), F32),
            pltpu.VMEM((slices, ens, columns), BF16),
            pltpu.VMEM((steps, slabs, ens, columns), BF16),
            pltpu.VMEM((steps, slabs, ens, columns), BF16),
            pltpu.VMEM((steps, slabs, ens, columns), BF16),
        ]
        + [pltpu.SemaphoreType.DMA((regions,))] * 4
        + [pltpu.SemaphoreType.DMA((steps,))] * 2
        + [pltpu.SemaphoreType.DMA((4,))],
        compiler_params=pltpu.CompilerParams(collective_id=3, has_side_effects=True, vmem_limit_bytes=DENSE_VMEM),
        name="transport",
    )(dense, near_flux, other, kernels, stay(observed[0]), stay(inv_var), stay(prior_mix), stay(blend))

    gradient, misfit = pl.pallas_call(
        final_kernel,
        out_shape=(
            jax.ShapeDtypeStruct((slabs, cells, ens), BF16),
            jax.ShapeDtypeStruct((rows, ens), BF16),
        ),
        in_specs=[vmem()] * 4,
        out_specs=(hbm(), hbm()),
        scratch_shapes=[pltpu.VMEM((slabs, columns, ens), BF16), pltpu.SemaphoreType.DMA((3,))],
        compiler_params=pltpu.CompilerParams(vmem_limit_bytes=4 << 20),
        name="final_mix",
    )(gradient, last, mix, misfit)
    return misfit[None], gradient


def solution(mesh):
    in_specs = (
        P(("group", "window"), "region", None),
        P(),
        P(("group", "window"), "region", None),
        P(("group", "window"), "region"),
        P(("group", "window"), "region"),
        P(("group", "window"), "region"),
        P(("group", "window"), "region"),
        P(("group", "window"), "region", None),
        P(("group", "window"), "region"),
        P(),
    )
    out_specs = (P(("group", "window"), "region", None), P(("group", "window"), "region", None))

    def either(*args):
        regions = mesh.shape["region"]
        blocks = args[7].shape[1] // BLOCK * regions
        return (dense_shards if blocks <= DENSE_BLOCKS and regions % 4 == 0 else shards)(regions, *args)

    return jax.shard_map(
        either,
        mesh=mesh,
        in_specs=in_specs,
        out_specs=out_specs,
        check_vma=False,
    )
```
